128 devices in a mesh: dev: 128 (over z, y, x, core).
Axes of the slice: x: 4, y: 4, z: 4, core: 2. Of those that a mesh axis runs over, the one named last changes fastest.
Arguments:
- start_block: float32 [3, 128, 32, 32, 256], P(None, 'dev'), may hold values from -6 to 6
- modulus: float32 [128, 32, 32], P('dev'), may hold values from 0.05 to 1
- occupancy: int32 [128, 32, 32], P('dev'), may hold values 0 or 1
Outputs:
- basis: float32 [3, 128, 32, 32, 256], P(None, 'dev')
- r_factor: float32 [256, 256], replicated
The draws below stay inside these ranges and needn't reach their ends.
All inputs are finite; a program needn't handle non-finite values. No bound on the sum of `occupancy` on one device may be relied on, other than what follows from the above.
Results may differ from the reference program's by a relative error of at most 0.008.
Values sent between devices are 32-bit elements; how exact they have to be, the bound alone decides.
A program may use at most 192 MiB of HBM per device.

```python
import math
import jax
import jax.numpy as jnp
import numpy as np
from jax import lax

MODES = 256
DEGREE = 3
BX = 32
BY = 32
NZ = 128


def touch_ends(array, stream_key, low, largest):
    dims = array.shape
    index_at = [jax.random.randint(jax.random.fold_in(stream_key, axis), (), 0, dims[axis]) for axis in range(len(dims))]
    array = array.at[tuple(index_at)].set(low)
    longest = dims.index(max(dims))
    index_at[longest] = (index_at[longest] + 1) % dims[longest]
    return array.at[tuple(index_at)].set(largest)


def steps_of(key, dims, cuts, least, high):
    def one(dim, blocks):
        draws = jax.random.uniform(jax.random.fold_in(jax.random.fold_in(key, 6), dim), (blocks,), jnp.float32, least / len(cuts), high / len(cuts))
        return jnp.repeat(jnp.exp(draws), dims[dim] // blocks).reshape((-1,) + (1,) * (len(dims) - dim - 1))

    loudness = one(*cuts[0])
    for cut in cuts[1:]:
        loudness = loudness * one(*cut)
    return loudness


def gaussian(rng, extent, width, limit, shards=(), held_as=jnp.bfloat16):
    array = width * jax.random.normal(rng, extent, jnp.float32)
    if shards:
        array = array * steps_of(rng, extent, shards, -0.22, 0.18)
    return jnp.clip(array, -limit, limit).astype(held_as)


def setup_inputs(seed: int = 0) -> dict:
    arg_keys = jax.random.split(jax.random.key(seed), 4)
    start_block = gaussian(arg_keys[0], (3, NZ, BY, BX, MODES), 1.0, 6.0, ((1, 128),), jnp.float32)
    modulus = jnp.clip(jnp.exp(math.log(1.0) - 2.9957323 * jax.random.uniform(arg_keys[1], (NZ, BY, BX), jnp.float32) ** steps_of(arg_keys[1], (NZ, BY, BX), ((0, 128),), -0.2, 0.2)), 0.05, 1.0)
    occupancy = touch_ends((jax.random.randint(arg_keys[2], (NZ, BY, BX), 0, 4) < 3).astype(jnp.int32), jax.random.fold_in(arg_keys[2], 1), 0, 1)
    return dict(start_block=start_block, modulus=modulus, occupancy=occupancy)


def element_matrix():
    poisson = 0.3
    lame_first = poisson / ((1.0 + poisson) * (1.0 - 2.0 * poisson))
    shear_modulus = 0.5 / (1.0 + poisson)
    elastic = np.zeros((6, 6))
    elastic[:3, :3] = lame_first
    for axis_number in range(3):
        elastic[axis_number, axis_number] += 2.0 * shear_modulus
        elastic[axis_number + 3, axis_number + 3] = shear_modulus
    points = [0.5 - 0.5 / np.sqrt(3.0), 0.5 + 0.5 / np.sqrt(3.0)]
    stiffness = np.zeros((24, 24))
    for point_x in points:
        for point_y in points:
            for point_z in points:
                gradients = np.zeros((3, 8))
                for corner in range(8):
                    offset_x, offset_y, offset_z = (corner % 2, corner // 2 % 2, corner // 4)
                    along_x = point_x if offset_x else 1.0 - point_x
                    along_y = point_y if offset_y else 1.0 - point_y
                    along_z = point_z if offset_z else 1.0 - point_z
                    gradients[0, corner] = (2 * offset_x - 1) * along_y * along_z
                    gradients[1, corner] = (2 * offset_y - 1) * along_x * along_z
                    gradients[2, corner] = (2 * offset_z - 1) * along_x * along_y
                strain_map = np.zeros((6, 24))
                strain_map[0, 0:8] = gradients[0]
                strain_map[1, 8:16] = gradients[1]
                strain_map[2, 16:24] = gradients[2]
                strain_map[3, 0:8] = gradients[1]
                strain_map[3, 8:16] = gradients[0]
                strain_map[4, 8:16] = gradients[2]
                strain_map[4, 16:24] = gradients[1]
                strain_map[5, 0:8] = gradients[2]
                strain_map[5, 16:24] = gradients[0]
                stiffness += strain_map.T @ elastic @ strain_map / 8.0
    return stiffness

def filter_bounds(stiffness):
    upper_end = 8.0 * float(np.max(np.sum(np.abs(stiffness), axis=1)))
    lower_end = 0.15 * upper_end
    return (0.5 * (upper_end + lower_end), 0.5 * (upper_end - lower_end))

def shift_face(face, offset_y, offset_x):
    height, width_x = (face.shape[1], face.shape[2])
    padded = jnp.pad(face, ((0, 0), (offset_y, 0), (offset_x, 0), (0, 0)))
    return padded[:, :height, :width_x]

def element_layer(bottom, top_layer, coeff_layer, stiffness):
    height, width_x, modes = (bottom.shape[1], bottom.shape[2], bottom.shape[3])
    widen = ((0, 0), (0, 1), (0, 1), (0, 0))
    padded_bottom = jnp.pad(bottom, widen)
    padded_top = jnp.pad(top_layer, widen)
    pieces = []
    for corner in range(8):
        offset_x, offset_y, offset_z = (corner % 2, corner // 2 % 2, corner // 4)
        source = padded_top if offset_z else padded_bottom
        pieces.append(source[:, offset_y:offset_y + height, offset_x:offset_x + width_x])
    corners = jnp.stack(pieces, axis=1).reshape(24, height * width_x, modes)
    product = jnp.einsum('ij,jem->iem', stiffness, corners, precision=lax.Precision.HIGHEST)
    product = product * coeff_layer.reshape(1, -1, 1)
    product = product.reshape(3, 8, height, width_x, modes)
    lower_face = None
    upper_face = None
    for corner in range(8):
        offset_x, offset_y, offset_z = (corner % 2, corner // 2 % 2, corner // 4)
        moved = shift_face(product[:, corner], offset_y, offset_x)
        if offset_z:
            upper_face = moved if upper_face is None else upper_face + moved
        else:
            lower_face = moved if lower_face is None else lower_face + moved
    return (lower_face, upper_face)

def reference(start_block, modulus, occupancy):
    stiffness_np = element_matrix()
    stiffness = jnp.asarray(stiffness_np, jnp.float32)
    center, half_width = filter_bounds(stiffness_np)
    coeff = modulus * occupancy.astype(jnp.float32)

    def operate_on(displaced):
        layers = jnp.moveaxis(displaced, 1, 0)
        shifted_up = jnp.concatenate([layers[1:], jnp.zeros_like(layers[:1])], axis=0)

        def advance(carried, inputs):
            bottom, top_layer, coeff_layer = inputs
            lower_face, upper_face = element_layer(bottom, top_layer, coeff_layer, stiffness)
            return (upper_face, lower_face + carried)
        start_face = jnp.zeros(layers.shape[1:], jnp.float32)
        _, forces = lax.scan(advance, start_face, (layers, shifted_up, coeff))
        return jnp.moveaxis(forces, 0, 1)
    previous = start_block
    current = (operate_on(previous) - center * previous) / half_width
    for step_index in range(DEGREE - 1):
        following = 2.0 * (operate_on(current) - center * current) / half_width - previous
        previous, current = (current, following)
    matrix = current.reshape(-1, MODES)
    ortho, upper_tri = jnp.linalg.qr(matrix)
    sign_fix = jnp.where(jnp.diagonal(upper_tri) < 0, -1.0, 1.0).astype(jnp.float32)
    ortho = ortho * sign_fix[None, :]
    upper_tri = upper_tri * sign_fix[:, None]
    row_scale = math.sqrt(matrix.shape[0])
    basis = (ortho * row_scale).reshape(current.shape)
    return (basis, upper_tri / row_scale)
```

```python
import functools
import math

import jax
import jax.numpy as jnp
import numpy as np
from jax import lax
from jax.experimental import pallas as pl
from jax.experimental.pallas import tpu as pltpu
from jax.sharding import PartitionSpec as P

DEGREE = 3
HIGHEST = lax.Precision.HIGHEST


def element_matrix():
    poisson = 0.3
    lame_first = poisson / ((1.0 + poisson) * (1.0 - 2.0 * poisson))
    shear_modulus = 0.5 / (1.0 + poisson)
    elastic = np.zeros((6, 6))
    elastic[:3, :3] = lame_first
    for axis_number in range(3):
        elastic[axis_number, axis_number] += 2.0 * shear_modulus
        elastic[axis_number + 3, axis_number + 3] = shear_modulus
    points = [0.5 - 0.5 / np.sqrt(3.0), 0.5 + 0.5 / np.sqrt(3.0)]
    stiffness = np.zeros((24, 24))
    for point_x in points:
        for point_y in points:
            for point_z in points:
                gradients = np.zeros((3, 8))
                for corner in range(8):
                    offset_x, offset_y, offset_z = (corner % 2, corner // 2 % 2, corner // 4)
                    along_x = point_x if offset_x else 1.0 - point_x
                    along_y = point_y if offset_y else 1.0 - point_y
                    along_z = point_z if offset_z else 1.0 - point_z
                    gradients[0, corner] = (2 * offset_x - 1) * along_y * along_z
                    gradients[1, corner] = (2 * offset_y - 1) * along_x * along_z
                    gradients[2, corner] = (2 * offset_z - 1) * along_x * along_y
                strain_map = np.zeros((6, 24))
                strain_map[0, 0:8] = gradients[0]
                strain_map[1, 8:16] = gradients[1]
                strain_map[2, 16:24] = gradients[2]
                strain_map[3, 0:8] = gradients[1]
                strain_map[3, 8:16] = gradients[0]
                strain_map[4, 8:16] = gradients[2]
                strain_map[4, 16:24] = gradients[1]
                strain_map[5, 0:8] = gradients[2]
                strain_map[5, 16:24] = gradients[0]
                stiffness += strain_map.T @ elastic @ strain_map / 8.0
    return stiffness


def filter_bounds(stiffness):
    upper_end = 8.0 * float(np.max(np.sum(np.abs(stiffness), axis=1)))
    lower_end = 0.15 * upper_end
    return (0.5 * (upper_end + lower_end), 0.5 * (upper_end - lower_end))


LAME = 0.3 / (1.3 * 0.4)
SHEAR = 0.5 / 1.3


def element_forces(h, coeff, factor):
    g = {}

    def coupled(keys, own, shared):
        total = h[keys[0]]
        for key in keys[1:]:
            total = total + h[key]
        total = total * shared
        for key in keys:
            g[key] = total if own is None else own * h[key] + total

    scaled = lambda value: coeff * (value * factor)
    mu16, mu48 = scaled(SHEAR / 16), scaled(SHEAR / 48)
    coupled([(0, "dss"), (1, "sds"), (2, "ssd")], scaled(2 * SHEAR / 16), scaled(LAME / 16))
    own, shared = scaled(3 * SHEAR / 48), scaled(LAME / 48)
    coupled([(0, "dsd"), (1, "sdd")], own, shared)
    coupled([(0, "dds"), (2, "sdd")], own, shared)
    coupled([(1, "dds"), (2, "dsd")], own, shared)
    coupled([(0, "sdd"), (1, "dsd"), (2, "dds")], mu48, mu48)
    coupled([(0, "sds"), (1, "dss")], None, mu16)
    coupled([(0, "ssd"), (2, "dss")], None, mu16)
    coupled([(1, "ssd"), (2, "sds")], None, mu16)
    last = scaled((LAME + 4 * SHEAR) / 144)
    for k in range(3):
        g[(k, "ddd")] = last * h[(k, "ddd")]
    return g


def step_kernel(factor, shift, below, here, above, coeff_below, coeff_here, previous, out, planes, upward):
    height, width = here.shape[1], here.shape[2]
    tiles = width // 8
    rows = lax.broadcasted_iota(jnp.int32, (8, here.shape[3]), 0)
    zero = jnp.zeros((8, here.shape[3]), jnp.float32)

    def row_of(ref, k, y, t):
        a = ref[k, y, pl.ds(8 * t, 8), :]
        if t + 1 < tiles:
            b = ref[k, y, pl.ds(8 * t + 1, 8), :]
        else:
            b = jnp.where(rows == 7, 0.0, pltpu.roll(a, 7, 0))
        return a + b, b - a

    def xz_stage(y, t):
        q = {}
        for k in range(3):
            low, mid, top = (row_of(ref, k, y, t) for ref in (below, here, above))
            for a in (0, 1):
                q[(k, "sd"[a], 0, "s")] = low[a] + mid[a]
                q[(k, "sd"[a], 0, "d")] = mid[a] - low[a]
                q[(k, "sd"[a], 1, "s")] = mid[a] + top[a]
                q[(k, "sd"[a], 1, "d")] = top[a] - mid[a]
        return q

    index = {}
    for k in range(3):
        for a in "sd":
            for e in (0, 1):
                for c in "sd":
                    index[(k, a, e, c)] = len(index)

    def put(slot, t, q):
        for key, value in q.items():
            planes[slot, t, index[key]] = value

    def element_row(y, last):
        slot = y % 2
        carry = [zero] * 3
        for t in range(tiles):
            if last:
                far = None
            else:
                far = xz_stage(y + 1, t)
                put(1 - slot, t, far)
            force = {}
            for e, coeff_ref in ((0, coeff_below), (1, coeff_here)):
                h = {}
                for k in range(3):
                    for a in "sd":
                        for c in "sd":
                            near = planes[slot, t, index[(k, a, e, c)]]
                            if last:
                                h[(k, a + "s" + c)] = near
                                h[(k, a + "d" + c)] = -near
                            else:
                                h[(k, a + "s" + c)] = near + far[(k, a, e, c)]
                                h[(k, a + "d" + c)] = far[(k, a, e, c)] - near
                g = element_forces(h, coeff_ref[y, pl.ds(8 * t, 8), :], factor)
                for k in range(3):
                    for a in "sd":
                        for b in "sd":
                            difference = g[(k, a + b + "d")]
                            if e == 1:
                                difference = -difference
                            if a + b != "ss":
                                difference = g[(k, a + b + "s")] + difference
                            key = (k, a, b)
                            force[key] = difference if e == 0 else force[key] + difference
            for k in range(3):
                part = {}
                for i, a in enumerate("sd"):
                    part[a] = force[(k, a, "s")] - force[(k, a, "d")] + upward[t, 2 * k + i]
                    upward[t, 2 * k + i] = force[(k, a, "s")] + force[(k, a, "d")]
                moved = pltpu.roll(part["s"] + part["d"], 1, 0)
                total = (part["s"] - part["d"]) + jnp.where(rows == 0, carry[k], moved)
                carry[k] = moved
                where = (k, y, pl.ds(8 * t, 8))
                value = total - shift * here[where]
                if previous is not None:
                    value = value - previous[where]
                out[where] = value

    for t in range(tiles):
        put(0, t, xz_stage(0, t))
        for i in range(6):
            upward[t, i] = zero

    @pl.loop(0, height - 1)
    def _(y):
        element_row(y, False)

    element_row(height - 1, True)


def filter_step(below, here, above, coeff_below, coeff_here, previous, factor, shift):
    args = [below, here, above, coeff_below, coeff_here]
    if previous is None:

        def kernel(b, h, a, cb, ch, out, planes, upward):
            step_kernel(factor, shift, b, h, a, cb, ch, None, out, planes, upward)
    else:
        args.append(previous)
        kernel = functools.partial(step_kernel, factor, shift)
    tiles, lanes = here.shape[2] // 8, here.shape[3]
    return pl.pallas_call(
        kernel,
        out_shape=jax.ShapeDtypeStruct(here.shape, jnp.float32),
        in_specs=[pl.BlockSpec(memory_space=pltpu.VMEM)] * len(args),
        out_specs=pl.BlockSpec(memory_space=pltpu.VMEM),
        scratch_shapes=[
            pltpu.VMEM((2, tiles, 24, 8, lanes), jnp.float32),
            pltpu.VMEM((tiles, 6, 8, lanes), jnp.float32),
        ],
        cost_estimate=pl.CostEstimate(flops=40_000_000, bytes_accessed=9_000_000, transcendentals=0),
        name="filter_step",
    )(*args)


def dot(a, b):
    return jnp.dot(a, b, precision=HIGHEST, preferred_element_type=jnp.float32)


def dot_ta(a, b):
    return lax.dot_general(a, b, (((0,), (0,)), ((), ())), precision=HIGHEST, preferred_element_type=jnp.float32)


SWEEPS = 10
TARGET = 1e-6


def factor_kernel(gram, inverse, triangle, misfit):
    g = gram[...]
    n = g.shape[0]
    row = lax.broadcasted_iota(jnp.int32, (n, n), 0)
    col = lax.broadcasted_iota(jnp.int32, (n, n), 1)
    diagonal = jnp.where(row == col, g, 0.0)
    d_col = lax.rsqrt(jnp.sum(diagonal, axis=1, keepdims=True))
    d_row = lax.rsqrt(jnp.sum(diagonal, axis=0, keepdims=True))
    unit = g * d_col * d_row
    one = jnp.where(row == col, 1.0, 0.0)
    weight = jnp.where(row < col, 1.0, jnp.where(row == col, 0.5, 0.0))

    def refined(state):
        s, _, count = state
        excess = dot_ta(s, dot(unit, s)) - one
        s = s - dot(s, excess * weight)
        return (s, jnp.sum(excess * excess), count + 1)

    start = one - (unit - one) * weight
    s, size, _ = lax.while_loop(
        lambda state: jnp.logical_and(state[1] > TARGET, state[2] < SWEEPS), refined, (start, jnp.float32(1.0), 0)
    )
    inverse[...] = d_col * s
    r = dot_ta(s, unit)
    triangle[...] = jnp.where(row <= col, r / d_row, 0.0)
    misfit[0, 0] = size


def factored(gram):
    n = gram.shape[0]
    return pl.pallas_call(
        factor_kernel,
        out_shape=(
            jax.ShapeDtypeStruct((n, n), jnp.float32),
            jax.ShapeDtypeStruct((n, n), jnp.float32),
            jax.ShapeDtypeStruct((1, 1), jnp.float32),
        ),
        in_specs=[pl.BlockSpec(memory_space=pltpu.VMEM)],
        out_specs=(
            pl.BlockSpec(memory_space=pltpu.VMEM),
            pl.BlockSpec(memory_space=pltpu.VMEM),
            pl.BlockSpec(memory_space=pltpu.SMEM),
        ),
        name="factor",
    )(gram)


def elimination_kernel(gram, extra, inverse_t, triangle, a, w):
    n = gram.shape[0]
    row = lax.broadcasted_iota(jnp.int32, (n, n), 0)
    col = lax.broadcasted_iota(jnp.int32, (n, n), 1)
    g = gram[...]
    one = jnp.where(row == col, 1.0, 0.0)
    diagonal = jnp.where(row == col, g, 0.0)
    s_col = jnp.sum(diagonal, axis=1, keepdims=True)
    s_row = jnp.sum(diagonal, axis=0, keepdims=True)
    d_col = lax.rsqrt(jnp.where(s_col > 0, s_col, 1.0))
    d_row = lax.rsqrt(jnp.where(s_row > 0, s_row, 1.0))
    a[...] = g * d_col * d_row + extra[0, 0] * one
    w[...] = one

    @pl.loop(0, n)
    def _(k):
        pivot_row = a[pl.ds(k, 1), :]
        column = jnp.sum(jnp.where(col == k, a[...], 0.0), axis=1, keepdims=True)
        lane = lax.broadcasted_iota(jnp.int32, (1, n), 1)
        pivot = jnp.maximum(jnp.sum(jnp.where(lane == k, pivot_row, 0.0), axis=1, keepdims=True), 1e-12)
        below = lax.broadcasted_iota(jnp.int32, (n, 1), 0) > k
        ratio = jnp.where(below, column / pivot, 0.0)
        w_row = w[pl.ds(k, 1), :]
        a[...] = a[...] - ratio * pivot_row
        w[...] = w[...] - ratio * w_row

    u = a[...]
    pivots = jnp.maximum(jnp.sum(jnp.where(row == col, u, 0.0), axis=1, keepdims=True), 1e-12)
    root = lax.rsqrt(pivots)
    triangle[...] = jnp.where(row < col, u * root, jnp.where(row == col, pivots * root, 0.0)) / d_row
    inverse_t[...] = w[...] * root * d_row


def eliminated(gram, extra):
    n = gram.shape[0]
    return pl.pallas_call(
        elimination_kernel,
        out_shape=(jax.ShapeDtypeStruct((n, n), jnp.float32),) * 2,
        in_specs=[pl.BlockSpec(memory_space=pltpu.VMEM), pl.BlockSpec(memory_space=pltpu.SMEM)],
        out_specs=(pl.BlockSpec(memory_space=pltpu.VMEM),) * 2,
        scratch_shapes=[pltpu.VMEM((n, n), jnp.float32)] * 2,
        name="eliminate",
    )(gram, extra.reshape(1, 1))


def neighbours(x):
    devices = lax.axis_size("dev")
    down = lax.ppermute(x, "dev", [(i, i - 1) for i in range(1, devices)])
    up = lax.ppermute(x, "dev", [(i, i + 1) for i in range(devices - 1)])
    return up, down


def local(start_block, modulus, occupancy):
    center, half_width = filter_bounds(element_matrix())
    coeff = (modulus * occupancy.astype(jnp.float32))[0]
    height, width = coeff.shape
    modes = start_block.shape[4]
    lanes = 128
    blocks = modes // lanes
    devices = lax.axis_size("dev")
    coeff_below = lax.ppermute(coeff, "dev", [(i, i + 1) for i in range(devices - 1)])
    spread = lambda c: jnp.broadcast_to(c[:, :, None], (height, width, lanes))
    coeff_here, coeff_below = spread(coeff), spread(coeff_below)

    flat = start_block.reshape(3, height, width, modes)
    current = [flat[..., i * lanes : (i + 1) * lanes] for i in range(blocks)]
    previous = [None] * blocks
    for step in range(DEGREE):
        scale = (1.0 if step == 0 else 2.0) / half_width
        around = [neighbours(block) for block in current]
        following = [
            filter_step(below, here, above, coeff_below, coeff_here, old, scale, scale * center)
            for (below, above), here, old in zip(around, current, previous)
        ]
        previous, current = current, following

    matrix = jnp.concatenate(current, axis=-1).reshape(-1, modes)
    row_scale = math.sqrt(matrix.shape[0] * devices)
    gram = lax.psum(dot_ta(matrix, matrix), "dev")
    inverse, triangle, misfit = factored(gram)

    def direct(x, gram, inverse, triangle):
        return dot(x, inverse * row_scale), triangle / row_scale

    def general(x, gram, inverse, triangle):
        def one_pass(i, state):
            x, total, gram = state
            extra = jnp.where(i == 0, 3e-5, 0.0).astype(jnp.float32)
            inverse_t, r = eliminated(gram, extra)
            x = dot(x, inverse_t.T)
            return (x, dot(r, total), lax.psum(dot_ta(x, x), "dev"))

        x, total, _ = lax.fori_loop(0, 4, one_pass, (x, jnp.eye(modes, dtype=jnp.float32), gram))
        return x * row_scale, total / row_scale

    basis, triangle = lax.cond(misfit[0, 0] <= 1e-4, direct, general, matrix, gram, inverse, triangle)
    return basis.reshape(start_block.shape), triangle


def solution(mesh):
    return jax.shard_map(
        local,
        mesh=mesh,
        in_specs=(P(None, "dev", None, None, None), P("dev", None, None), P("dev", None, None)),
        out_specs=(P(None, "dev", None, None, None), P()),
        check_vma=False,
    )
```

```python
import functools
import math

import jax
import jax.numpy as jnp
import numpy as np
from jax import lax
from jax.experimental import pallas as pl
from jax.experimental.pallas import tpu as pltpu
from jax.sharding import PartitionSpec as P

DEGREE = 3
HIGHEST = lax.Precision.HIGHEST


def element_matrix():
    poisson = 0.3
    lame_first = poisson / ((1.0 + poisson) * (1.0 - 2.0 * poisson))
    shear_modulus = 0.5 / (1.0 + poisson)
    elastic = np.zeros((6, 6))
    elastic[:3, :3] = lame_first
    for axis_number in range(3):
        elastic[axis_number, axis_number] += 2.0 * shear_modulus
        elastic[axis_number + 3, axis_number + 3] = shear_modulus
    points = [0.5 - 0.5 / np.sqrt(3.0), 0.5 + 0.5 / np.sqrt(3.0)]
    stiffness = np.zeros((24, 24))
    for point_x in points:
        for point_y in points:
            for point_z in points:
                gradients = np.zeros((3, 8))
                for corner in range(8):
                    offset_x, offset_y, offset_z = (corner % 2, corner // 2 % 2, corner // 4)
                    along_x = point_x if offset_x else 1.0 - point_x
                    along_y = point_y if offset_y else 1.0 - point_y
                    along_z = point_z if offset_z else 1.0 - point_z
                    gradients[0, corner] = (2 * offset_x - 1) * along_y * along_z
                    gradients[1, corner] = (2 * offset_y - 1) * along_x * along_z
                    gradients[2, corner] = (2 * offset_z - 1) * along_x * along_y
                strain_map = np.zeros((6, 24))
                strain_map[0, 0:8] = gradients[0]
                strain_map[1, 8:16] = gradients[1]
                strain_map[2, 16:24] = gradients[2]
                strain_map[3, 0:8] = gradients[1]
                strain_map[3, 8:16] = gradients[0]
                strain_map[4, 8:16] = gradients[2]
                strain_map[4, 16:24] = gradients[1]
                strain_map[5, 0:8] = gradients[2]
                strain_map[5, 16:24] = gradients[0]
                stiffness += strain_map.T @ elastic @ strain_map / 8.0
    return stiffness


def filter_bounds(stiffness):
    upper_end = 8.0 * float(np.max(np.sum(np.abs(stiffness), axis=1)))
    lower_end = 0.15 * upper_end
    return (0.5 * (upper_end + lower_end), 0.5 * (upper_end - lower_end))


LAME = 0.3 / (1.3 * 0.4)
SHEAR = 0.5 / 1.3


def element_forces(h, coeff, factor):
    g = {}

    def coupled(keys, own, shared):
        total = h[keys[0]]
        for key in keys[1:]:
            total = total + h[key]
        total = total * shared
        for key in keys:
            g[key] = total if own is None else own * h[key] + total

    scaled = lambda value: coeff * (value * factor)
    mu16, mu48 = scaled(SHEAR / 16), scaled(SHEAR / 48)
    coupled([(0, "dss"), (1, "sds"), (2, "ssd")], scaled(2 * SHEAR / 16), scaled(LAME / 16))
    own, shared = scaled(3 * SHEAR / 48), scaled(LAME / 48)
    coupled([(0, "dsd"), (1, "sdd")], own, shared)
    coupled([(0, "dds"), (2, "sdd")], own, shared)
    coupled([(1, "dds"), (2, "dsd")], own, shared)
    coupled([(0, "sdd"), (1, "dsd"), (2, "dds")], mu48, mu48)
    coupled([(0, "sds"), (1, "dss")], None, mu16)
    coupled([(0, "ssd"), (2, "dss")], None, mu16)
    coupled([(1, "ssd"), (2, "sds")], None, mu16)
    last = scaled((LAME + 4 * SHEAR) / 144)
    for k in range(3):
        g[(k, "ddd")] = last * h[(k, "ddd")]
    return g


def step_kernel(factor, shift, below, here, above, coeff_below, coeff_here, previous, out, planes, upward):
    height, width = here.shape[1], here.shape[2]
    tiles = width // 8
    rows = lax.broadcasted_iota(jnp.int32, (8, here.shape[3]), 0)
    zero = jnp.zeros((8, here.shape[3]), jnp.float32)

    def row_of(ref, k, y, t):
        a = ref[k, y, pl.ds(8 * t, 8), :]
        if t + 1 < tiles:
            b = ref[k, y, pl.ds(8 * t + 1, 8), :]
        else:
            b = jnp.where(rows == 7, 0.0, pltpu.roll(a, 7, 0))
        return a + b, b - a

    def xz_stage(y, t):
        q = {}
        for k in range(3):
            low, mid, top = (row_of(ref, k, y, t) for ref in (below, here, above))
            for a in (0, 1):
                q[(k, "sd"[a], 0, "s")] = low[a] + mid[a]
                q[(k, "sd"[a], 0, "d")] = mid[a] - low[a]
                q[(k, "sd"[a], 1, "s")] = mid[a] + top[a]
                q[(k, "sd"[a], 1, "d")] = top[a] - mid[a]
        return q

    index = {}
    for k in range(3):
        for a in "sd":
            for e in (0, 1):
                for c in "sd":
                    index[(k, a, e, c)] = len(index)

    def put(slot, t, q):
        for key, value in q.items():
            planes[slot, t, index[key]] = value

    def element_row(y, last):
        slot = y % 2
        carry = [zero] * 3
        for t in range(tiles):
            if last:
                far = None
            else:
                far = xz_stage(y + 1, t)
                put(1 - slot, t, far)
            force = {}
            for e, coeff_ref in ((0, coeff_below), (1, coeff_here)):
                h = {}
                for k in range(3):
                    for a in "sd":
                        for c in "sd":
                            near = planes[slot, t, index[(k, a, e, c)]]
                            if last:
                                h[(k, a + "s" + c)] = near
                                h[(k, a + "d" + c)] = -near
                            else:
                                h[(k, a + "s" + c)] = near + far[(k, a, e, c)]
                                h[(k, a + "d" + c)] = far[(k, a, e, c)] - near
                g = element_forces(h, coeff_ref[y, pl.ds(8 * t, 8), :], factor)
                for k in range(3):
                    for a in "sd":
                        for b in "sd":
                            difference = g[(k, a + b + "d")]
                            if e == 1:
                                difference = -difference
                            if a + b != "ss":
                                difference = g[(k, a + b + "s")] + difference
                            key = (k, a, b)
                            force[key] = difference if e == 0 else force[key] + difference
            for k in range(3):
                part = {}
                for i, a in enumerate("sd"):
                    part[a] = force[(k, a, "s")] - force[(k, a, "d")] + upward[t, 2 * k + i]
                    upward[t, 2 * k + i] = force[(k, a, "s")] + force[(k, a, "d")]
                moved = pltpu.roll(part["s"] + part["d"], 1, 0)
                total = (part["s"] - part["d"]) + jnp.where(rows == 0, carry[k], moved)
                carry[k] = moved
                where = (k, y, pl.ds(8 * t, 8))
                value = total - shift * here[where]
                if previous is not None:
                    value = value - previous[where]
                out[where] = value

    for t in range(tiles):
        put(0, t, xz_stage(0, t))
        for i in range(6):
            upward[t, i] = zero

    @pl.loop(0, height - 1)
    def _(y):
        element_row(y, False)

    element_row(height - 1, True)


def filter_step(below, here, above, coeff_below, coeff_here, previous, factor, shift):
    args = [below, here, above, coeff_below, coeff_here]
    if previous is None:

        def kernel(b, h, a, cb, ch, out, planes, upward):
            step_kernel(factor, shift, b, h, a, cb, ch, None, out, planes, upward)
    else:
        args.append(previous)
        kernel = functools.partial(step_kernel, factor, shift)
    tiles, lanes = here.shape[2] // 8, here.shape[3]
    return pl.pallas_call(
        kernel,
        out_shape=jax.ShapeDtypeStruct(here.shape, jnp.float32),
        in_specs=[pl.BlockSpec(memory_space=pltpu.VMEM)] * len(args),
        out_specs=pl.BlockSpec(memory_space=pltpu.VMEM),
        scratch_shapes=[
            pltpu.VMEM((2, tiles, 24, 8, lanes), jnp.float32),
            pltpu.VMEM((tiles, 6, 8, lanes), jnp.float32),
        ],
        cost_estimate=pl.CostEstimate(flops=40_000_000, bytes_accessed=9_000_000, transcendentals=0),
        name="filter_step",
    )(*args)


def dot(a, b):
    return jnp.dot(a, b, precision=HIGHEST, preferred_element_type=jnp.float32)


def dot_ta(a, b):
    return lax.dot_general(a, b, (((0,), (0,)), ((), ())), precision=HIGHEST, preferred_element_type=jnp.float32)


SWEEPS = 10
TARGET = 1e-6


def factor_kernel(gram, inverse, triangle, misfit):
    g = gram[...]
    n = g.shape[0]
    row = lax.broadcasted_iota(jnp.int32, (n, n), 0)
    col = lax.broadcasted_iota(jnp.int32, (n, n), 1)
    diagonal = jnp.where(row == col, g, 0.0)
    d_col = lax.rsqrt(jnp.sum(diagonal, axis=1, keepdims=True))
    d_row = lax.rsqrt(jnp.sum(diagonal, axis=0, keepdims=True))
    unit = g * d_col * d_row
    one = jnp.where(row == col, 1.0, 0.0)
    weight = jnp.where(row < col, 1.0, jnp.where(row == col, 0.5, 0.0))

    def refined(state):
        s, _, count = state
        excess = dot_ta(s, dot(unit, s)) - one
        s = s - dot(s, excess * weight)
        return (s, jnp.sum(excess * excess), count + 1)

    start = one - (unit - one) * weight
    s, size, _ = lax.while_loop(
        lambda state: jnp.logical_and(state[1] > TARGET, state[2] < SWEEPS), refined, (start, jnp.float32(1.0), 0)
    )
    inverse[...] = d_col * s
    r = dot_ta(s, unit)
    triangle[...] = jnp.where(row <= col, r / d_row, 0.0)
    misfit[0, 0] = size


def factored(gram):
    n = gram.shape[0]
    return pl.pallas_call(
        factor_kernel,
        out_shape=(
            jax.ShapeDtypeStruct((n, n), jnp.float32),
            jax.ShapeDtypeStruct((n, n), jnp.float32),
            jax.ShapeDtypeStruct((1, 1), jnp.float32),
        ),
        in_specs=[pl.BlockSpec(memory_space=pltpu.VMEM)],
        out_specs=(
            pl.BlockSpec(memory_space=pltpu.VMEM),
            pl.BlockSpec(memory_space=pltpu.VMEM),
            pl.BlockSpec(memory_space=pltpu.SMEM),
        ),
        name="factor",
    )(gram)


def elimination_kernel(gram, extra, inverse_t, triangle, a, w):
    n = gram.shape[0]
    row = lax.broadcasted_iota(jnp.int32, (n, n), 0)
    col = lax.broadcasted_iota(jnp.int32, (n, n), 1)
    g = gram[...]
    one = jnp.where(row == col, 1.0, 0.0)
    diagonal = jnp.where(row == col, g, 0.0)
    s_col = jnp.sum(diagonal, axis=1, keepdims=True)
    s_row = jnp.sum(diagonal, axis=0, keepdims=True)
    d_col = lax.rsqrt(jnp.where(s_col > 0, s_col, 1.0))
    d_row = lax.rsqrt(jnp.where(s_row > 0, s_row, 1.0))
    a[...] = g * d_col * d_row + extra[0, 0] * one
    w[...] = one

    @pl.loop(0, n)
    def _(k):
        pivot_row = a[pl.ds(k, 1), :]
        column = jnp.sum(jnp.where(col == k, a[...], 0.0), axis=1, keepdims=True)
        lane = lax.broadcasted_iota(jnp.int32, (1, n), 1)
        pivot = jnp.maximum(jnp.sum(jnp.where(lane == k, pivot_row, 0.0), axis=1, keepdims=True), 1e-12)
        below = lax.broadcasted_iota(jnp.int32, (n, 1), 0) > k
        ratio = jnp.where(below, column / pivot, 0.0)
        w_row = w[pl.ds(k, 1), :]
        a[...] = a[...] - ratio * pivot_row
        w[...] = w[...] - ratio * w_row

    u = a[...]
    pivots = jnp.maximum(jnp.sum(jnp.where(row == col, u, 0.0), axis=1, keepdims=True), 1e-12)
    root = lax.rsqrt(pivots)
    triangle[...] = jnp.where(row < col, u * root, jnp.where(row == col, pivots * root, 0.0)) / d_row
    inverse_t[...] = w[...] * root * d_row


def eliminated(gram, extra):
    n = gram.shape[0]
    return pl.pallas_call(
        elimination_kernel,
        out_shape=(jax.ShapeDtypeStruct((n, n), jnp.float32),) * 2,
        in_specs=[pl.BlockSpec(memory_space=pltpu.VMEM), pl.BlockSpec(memory_space=pltpu.SMEM)],
        out_specs=(pl.BlockSpec(memory_space=pltpu.VMEM),) * 2,
        scratch_shapes=[pltpu.VMEM((n, n), jnp.float32)] * 2,
        name="eliminate",
    )(gram, extra.reshape(1, 1))

MESH = pl.DeviceIdType.MESH


def all_reduce_kernel(sizes, x, out, half, part, summed, full, core_in, x_in, y_in, z_in, send, core_sem, x_sem, y_sem, z_sem, back_sem, pair_sem):
    nz, ny, nx = sizes
    me = lax.axis_index("dev")
    core, at_x = me % 2, me // 2 % nx
    at_y, at_z = me // (2 * nx) % ny, me // (2 * nx * ny)
    partner = me + 1 - 2 * core
    along = lambda at, j, size, stride: ((at + j) % size, me + ((at + j) % size - at) * stride)
    x_peers = [along(at_x, j, nx, 2) for j in range(1, nx)]
    y_peers = [along(at_y, j, ny, 2 * nx) for j in range(1, ny)]
    z_peers = [along(at_z, j, nz, 2 * nx * ny) for j in range(1, nz)]

    barrier = pltpu.get_barrier_semaphore()
    others = [partner] + [peer for _, peer in x_peers + y_peers + z_peers]
    for peer in others:
        pl.semaphore_signal(barrier, inc=1, device_id=(peer,), device_id_type=MESH)
    pl.semaphore_wait(barrier, len(others))

    started = []

    def copy(src, dst, recv_sem, peer):
        transfer = pltpu.make_async_remote_copy(
            src_ref=src, dst_ref=dst, send_sem=send.at[len(started)], recv_sem=recv_sem, device_id=(peer,), device_id_type=MESH
        )
        transfer.start()
        started.append(transfer)

    def arrived(dst, recv_sem):
        pltpu.make_async_remote_copy(
            src_ref=dst, dst_ref=dst, send_sem=send.at[0], recv_sem=recv_sem, device_id=(partner,), device_id_type=MESH
        ).wait_recv()

    rows = x.shape[0] // 2
    piece = rows // nx
    copy(x.at[pl.ds((1 - core) * rows, rows)], core_in, core_sem, partner)
    arrived(core_in, core_sem)
    half[...] = x[pl.ds(core * rows, rows)] + core_in[...]

    for other, peer in x_peers:
        copy(half.at[pl.ds(other * piece, piece)], x_in.at[at_x], x_sem.at[at_x], peer)
    x_in[at_x] = half[pl.ds(at_x * piece, piece)]
    for other, peer in x_peers:
        arrived(x_in.at[other], x_sem.at[other])
    total = x_in[0]
    for i in range(1, nx):
        total = total + x_in[i]

    for stage, (peers, at, size, slots, sem) in enumerate(((y_peers, at_y, ny, y_in, y_sem), (z_peers, at_z, nz, z_in, z_sem))):
        part[stage] = total
        for other, peer in peers:
            copy(part.at[stage], slots.at[at], sem.at[at], peer)
        slots[at] = total
        for other, peer in peers:
            arrived(slots.at[other], sem.at[other])
        total = slots[0]
        for i in range(1, size):
            total = total + slots[i]

    summed[...] = total
    mine = core * rows + at_x * piece
    for other, peer in x_peers:
        copy(summed, full.at[pl.ds(mine, piece)], back_sem.at[at_x], peer)
    copy(summed, full.at[pl.ds(mine, piece)], pair_sem.at[at_x], partner)
    full[pl.ds(mine, piece)] = total
    for other, peer in x_peers:
        there = full.at[pl.ds(core * rows + other * piece, piece)]
        arrived(there, back_sem.at[other])
        copy(there, there, pair_sem.at[other], partner)
    for i in range(nx):
        arrived(full.at[pl.ds((1 - core) * rows + i * piece, piece)], pair_sem.at[i])
    out[...] = full[...]
    for transfer in started:
        transfer.wait_send()


def all_reduce(x, sizes=(4, 4, 4)):
    nz, ny, nx = sizes
    n, m = x.shape
    rows = n // 2
    piece = rows // nx
    copies = 1 + (nx - 1) + (ny - 1) + (nz - 1) + nx + (nx - 1)
    block = lambda *lead: pltpu.VMEM((*lead, m), jnp.float32)
    return pl.pallas_call(
        functools.partial(all_reduce_kernel, sizes),
        out_shape=jax.ShapeDtypeStruct(x.shape, jnp.float32),
        in_specs=[pl.BlockSpec(memory_space=pltpu.VMEM)],
        out_specs=pl.BlockSpec(memory_space=pltpu.VMEM),
        scratch_shapes=[
            block(rows), block(2, piece), block(piece), block(n), block(rows), block(nx, piece), block(ny, piece), block(nz, piece),
            pltpu.SemaphoreType.DMA((copies,)), pltpu.SemaphoreType.DMA, pltpu.SemaphoreType.DMA((nx,)), pltpu.SemaphoreType.DMA((ny,)),
            pltpu.SemaphoreType.DMA((nz,)), pltpu.SemaphoreType.DMA((nx,)), pltpu.SemaphoreType.DMA((nx,)),
        ],
        compiler_params=pltpu.CompilerParams(collective_id=0, has_side_effects=True),
        name="all_reduce",
    )(x)


def neighbours(x):
    devices = lax.axis_size("dev")
    down = lax.ppermute(x, "dev", [(i, i - 1) for i in range(1, devices)])
    up = lax.ppermute(x, "dev", [(i, i + 1) for i in range(devices - 1)])
    return up, down


def local(start_block, modulus, occupancy):
    center, half_width = filter_bounds(element_matrix())
    coeff = (modulus * occupancy.astype(jnp.float32))[0]
    height, width = coeff.shape
    modes = start_block.shape[4]
    lanes = 128
    blocks = modes // lanes
    devices = lax.axis_size("dev")
    coeff_below = lax.ppermute(coeff, "dev", [(i, i + 1) for i in range(devices - 1)])
    spread = lambda c: jnp.broadcast_to(c[:, :, None], (height, width, lanes))
    coeff_here, coeff_below = spread(coeff), spread(coeff_below)

    flat = start_block.reshape(3, height, width, modes)
    current = [flat[..., i * lanes : (i + 1) * lanes] for i in range(blocks)]
    previous = [None] * blocks
    for step in range(DEGREE):
        scale = (1.0 if step == 0 else 2.0) / half_width
        around = [neighbours(block) for block in current]
        following = [
            filter_step(below, here, above, coeff_below, coeff_here, old, scale, scale * center)
            for (below, above), here, old in zip(around, current, previous)
        ]
        previous, current = current, following

    matrix = jnp.concatenate(current, axis=-1).reshape(-1, modes)
    row_scale = math.sqrt(matrix.shape[0] * devices)
    gram = all_reduce(dot_ta(matrix, matrix))
    inverse, triangle, misfit = factored(gram)

    def direct(x, gram, inverse, triangle):
        return dot(x, inverse * row_scale), triangle / row_scale

    def general(x, gram, inverse, triangle):
        def one_pass(i, state):
            x, total, gram = state
            extra = jnp.where(i == 0, 3e-5, 0.0).astype(jnp.float32)
            inverse_t, r = eliminated(gram, extra)
            x = dot(x, inverse_t.T)
            return (x, dot(r, total), all_reduce(dot_ta(x, x)))

        x, total, _ = lax.fori_loop(0, 4, one_pass, (x, jnp.eye(modes, dtype=jnp.float32), gram))
        return x * row_scale, total / row_scale

    basis, triangle = lax.cond(misfit[0, 0] <= 1e-4, direct, general, matrix, gram, inverse, triangle)
    return basis.reshape(start_block.shape), triangle


def solution(mesh):
    return jax.shard_map(
        local,
        mesh=mesh,
        in_specs=(P(None, "dev", None, None, None), P("dev", None, None), P("dev", None, None)),
        out_specs=(P(None, "dev", None, None, None), P()),
        check_vma=False,
    )
```

```python
import functools
import math

import jax
import jax.numpy as jnp
import numpy as np
from jax import lax
from jax.experimental import pallas as pl
from jax.experimental.pallas import tpu as pltpu
from jax.sharding import PartitionSpec as P

DEGREE = 3
HIGHEST = lax.Precision.HIGHEST


def element_matrix():
    poisson = 0.3
    lame_first = poisson / ((1.0 + poisson) * (1.0 - 2.0 * poisson))
    shear_modulus = 0.5 / (1.0 + poisson)
    elastic = np.zeros((6, 6))
    elastic[:3, :3] = lame_first
    for axis_number in range(3):
        elastic[axis_number, axis_number] += 2.0 * shear_modulus
        elastic[axis_number + 3, axis_number + 3] = shear_modulus
    points = [0.5 - 0.5 / np.sqrt(3.0), 0.5 + 0.5 / np.sqrt(3.0)]
    stiffness = np.zeros((24, 24))
    for point_x in points:
        for point_y in points:
            for point_z in points:
                gradients = np.zeros((3, 8))
                for corner in range(8):
                    offset_x, offset_y, offset_z = (corner % 2, corner // 2 % 2, corner // 4)
                    along_x = point_x if offset_x else 1.0 - point_x
                    along_y = point_y if offset_y else 1.0 - point_y
                    along_z = point_z if offset_z else 1.0 - point_z
                    gradients[0, corner] = (2 * offset_x - 1) * along_y * along_z
                    gradients[1, corner] = (2 * offset_y - 1) * along_x * along_z
                    gradients[2, corner] = (2 * offset_z - 1) * along_x * along_y
                strain_map = np.zeros((6, 24))
                strain_map[0, 0:8] = gradients[0]
                strain_map[1, 8:16] = gradients[1]
                strain_map[2, 16:24] = gradients[2]
                strain_map[3, 0:8] = gradients[1]
                strain_map[3, 8:16] = gradients[0]
                strain_map[4, 8:16] = gradients[2]
                strain_map[4, 16:24] = gradients[1]
                strain_map[5, 0:8] = gradients[2]
                strain_map[5, 16:24] = gradients[0]
                stiffness += strain_map.T @ elastic @ strain_map / 8.0
    return stiffness


def filter_bounds(stiffness):
    upper_end = 8.0 * float(np.max(np.sum(np.abs(stiffness), axis=1)))
    lower_end = 0.15 * upper_end
    return (0.5 * (upper_end + lower_end), 0.5 * (upper_end - lower_end))


LAME = 0.3 / (1.3 * 0.4)
SHEAR = 0.5 / 1.3


def element_forces(h, coeff, factor):
    g = {}

    def coupled(keys, own, shared):
        total = h[keys[0]]
        for key in keys[1:]:
            total = total + h[key]
        total = total * shared
        for key in keys:
            g[key] = total if own is None else own * h[key] + total

    scaled = lambda value: coeff * (value * factor)
    mu16, mu48 = scaled(SHEAR / 16), scaled(SHEAR / 48)
    coupled([(0, "dss"), (1, "sds"), (2, "ssd")], scaled(2 * SHEAR / 16), scaled(LAME / 16))
    own, shared = scaled(3 * SHEAR / 48), scaled(LAME / 48)
    coupled([(0, "dsd"), (1, "sdd")], own, shared)
    coupled([(0, "dds"), (2, "sdd")], own, shared)
    coupled([(1, "dds"), (2, "dsd")], own, shared)
    coupled([(0, "sdd"), (1, "dsd"), (2, "dds")], mu48, mu48)
    coupled([(0, "sds"), (1, "dss")], None, mu16)
    coupled([(0, "ssd"), (2, "dss")], None, mu16)
    coupled([(1, "ssd"), (2, "sds")], None, mu16)
    last = scaled((LAME + 4 * SHEAR) / 144)
    for k in range(3):
        g[(k, "ddd")] = last * h[(k, "ddd")]
    return g


def step_kernel(factor, shift, below, here, above, coeff_below, coeff_here, previous, out, planes, upward):
    height, width = here.shape[1], here.shape[2]
    tiles = width // 8
    rows = lax.broadcasted_iota(jnp.int32, (8, here.shape[3]), 0)
    zero = jnp.zeros((8, here.shape[3]), jnp.float32)

    def row_of(ref, k, y, t):
        a = ref[k, y, pl.ds(8 * t, 8), :]
        if t + 1 < tiles:
            b = ref[k, y, pl.ds(8 * t + 1, 8), :]
        else:
            b = jnp.where(rows == 7, 0.0, pltpu.roll(a, 7, 0))
        return a + b, b - a

    def xz_stage(y, t):
        q = {}
        for k in range(3):
            low, mid, top = (row_of(ref, k, y, t) for ref in (below, here, above))
            for a in (0, 1):
                q[(k, "sd"[a], 0, "s")] = low[a] + mid[a]
                q[(k, "sd"[a], 0, "d")] = mid[a] - low[a]
                q[(k, "sd"[a], 1, "s")] = mid[a] + top[a]
                q[(k, "sd"[a], 1, "d")] = top[a] - mid[a]
        return q

    index = {}
    for k in range(3):
        for a in "sd":
            for e in (0, 1):
                for c in "sd":
                    index[(k, a, e, c)] = len(index)

    def put(slot, t, q):
        for key, value in q.items():
            planes[slot, t, index[key]] = value

    def element_row(y, last):
        slot = y % 2
        carry = [zero] * 3
        for t in range(tiles):
            if last:
                far = None
            else:
                far = xz_stage(y + 1, t)
                put(1 - slot, t, far)
            force = {}
            for e, coeff_ref in ((0, coeff_below), (1, coeff_here)):
                h = {}
                for k in range(3):
                    for a in "sd":
                        for c in "sd":
                            near = planes[slot, t, index[(k, a, e, c)]]
                            if last:
                                h[(k, a + "s" + c)] = near
                                h[(k, a + "d" + c)] = -near
                            else:
                                h[(k, a + "s" + c)] = near + far[(k, a, e, c)]
                                h[(k, a + "d" + c)] = far[(k, a, e, c)] - near
                g = element_forces(h, coeff_ref[y, pl.ds(8 * t, 8), :], factor)
                for k in range(3):
                    for a in "sd":
                        for b in "sd":
                            difference = g[(k, a + b + "d")]
                            if e == 1:
                                difference = -difference
                            if a + b != "ss":
                                difference = g[(k, a + b + "s")] + difference
                            key = (k, a, b)
                            force[key] = difference if e == 0 else force[key] + difference
            for k in range(3):
                part = {}
                for i, a in enumerate("sd"):
                    part[a] = force[(k, a, "s")] - force[(k, a, "d")] + upward[t, 2 * k + i]
                    upward[t, 2 * k + i] = force[(k, a, "s")] + force[(k, a, "d")]
                moved = pltpu.roll(part["s"] + part["d"], 1, 0)
                total = (part["s"] - part["d"]) + jnp.where(rows == 0, carry[k], moved)
                carry[k] = moved
                where = (k, y, pl.ds(8 * t, 8))
                value = total - shift * here[where]
                if previous is not None:
                    value = value - previous[where]
                out[where] = value

    for t in range(tiles):
        put(0, t, xz_stage(0, t))
        for i in range(6):
            upward[t, i] = zero

    @pl.loop(0, height - 1)
    def _(y):
        element_row(y, False)

    element_row(height - 1, True)


def filter_step(below, here, above, coeff_below, coeff_here, previous, factor, shift):
    args = [below, here, above, coeff_below, coeff_here]
    if previous is None:

        def kernel(b, h, a, cb, ch, out, planes, upward):
            step_kernel(factor, shift, b, h, a, cb, ch, None, out, planes, upward)
    else:
        args.append(previous)
        kernel = functools.partial(step_kernel, factor, shift)
    tiles, lanes = here.shape[2] // 8, here.shape[3]
    return pl.pallas_call(
        kernel,
        out_shape=jax.ShapeDtypeStruct(here.shape, jnp.float32),
        in_specs=[pl.BlockSpec(memory_space=pltpu.VMEM)] * len(args),
        out_specs=pl.BlockSpec(memory_space=pltpu.VMEM),
        scratch_shapes=[
            pltpu.VMEM((2, tiles, 24, 8, lanes), jnp.float32),
            pltpu.VMEM((tiles, 6, 8, lanes), jnp.float32),
        ],
        cost_estimate=pl.CostEstimate(flops=40_000_000, bytes_accessed=9_000_000, transcendentals=0),
        name="filter_step",
    )(*args)


def dot(a, b):
    return jnp.dot(a, b, precision=HIGHEST, preferred_element_type=jnp.float32)


def dot_ta(a, b):
    return lax.dot_general(a, b, (((0,), (0,)), ((), ())), precision=HIGHEST, preferred_element_type=jnp.float32)


SWEEPS = 10
TARGET = 1e-6


def factor_kernel(gram, inverse, triangle, misfit):
    g = gram[...]
    n = g.shape[0]
    row = lax.broadcasted_iota(jnp.int32, (n, n), 0)
    col = lax.broadcasted_iota(jnp.int32, (n, n), 1)
    diagonal = jnp.where(row == col, g, 0.0)
    d_col = lax.rsqrt(jnp.sum(diagonal, axis=1, keepdims=True))
    d_row = lax.rsqrt(jnp.sum(diagonal, axis=0, keepdims=True))
    unit = g * d_col * d_row
    one = jnp.where(row == col, 1.0, 0.0)
    weight = jnp.where(row < col, 1.0, jnp.where(row == col, 0.5, 0.0))

    def refined(state):
        s, _, count = state
        excess = dot_ta(s, dot(unit, s)) - one
        s = s - dot(s, excess * weight)
        return (s, jnp.sum(excess * excess), count + 1)

    start = one - (unit - one) * weight
    s, size, _ = lax.while_loop(
        lambda state: jnp.logical_and(state[1] > TARGET, state[2] < SWEEPS), refined, (start, jnp.float32(1.0), 0)
    )
    inverse[...] = d_col * s
    r = dot_ta(s, unit)
    triangle[...] = jnp.where(row <= col, r / d_row, 0.0)
    norm = jnp.sum(s * s)
    misfit[0, 0] = jnp.where(norm <= n + 50.0, size, 1.0)


def factored(gram):
    n = gram.shape[0]
    return pl.pallas_call(
        factor_kernel,
        out_shape=(
            jax.ShapeDtypeStruct((n, n), jnp.float32),
            jax.ShapeDtypeStruct((n, n), jnp.float32),
            jax.ShapeDtypeStruct((1, 1), jnp.float32),
        ),
        in_specs=[pl.BlockSpec(memory_space=pltpu.VMEM)],
        out_specs=(
            pl.BlockSpec(memory_space=pltpu.VMEM),
            pl.BlockSpec(memory_space=pltpu.VMEM),
            pl.BlockSpec(memory_space=pltpu.SMEM),
        ),
        name="factor",
    )(gram)


def elimination_kernel(gram, extra, inverse_t, triangle, a, w):
    n = gram.shape[0]
    row = lax.broadcasted_iota(jnp.int32, (n, n), 0)
    col = lax.broadcasted_iota(jnp.int32, (n, n), 1)
    g = gram[...]
    one = jnp.where(row == col, 1.0, 0.0)
    diagonal = jnp.where(row == col, g, 0.0)
    s_col = jnp.sum(diagonal, axis=1, keepdims=True)
    s_row = jnp.sum(diagonal, axis=0, keepdims=True)
    d_col = lax.rsqrt(jnp.where(s_col > 0, s_col, 1.0))
    d_row = lax.rsqrt(jnp.where(s_row > 0, s_row, 1.0))
    a[...] = g * d_col * d_row + extra[0, 0] * one
    w[...] = one

    @pl.loop(0, n)
    def _(k):
        pivot_row = a[pl.ds(k, 1), :]
        column = jnp.sum(jnp.where(col == k, a[...], 0.0), axis=1, keepdims=True)
        lane = lax.broadcasted_iota(jnp.int32, (1, n), 1)
        pivot = jnp.maximum(jnp.sum(jnp.where(lane == k, pivot_row, 0.0), axis=1, keepdims=True), 1e-12)
        below = lax.broadcasted_iota(jnp.int32, (n, 1), 0) > k
        ratio = jnp.where(below, column / pivot, 0.0)
        w_row = w[pl.ds(k, 1), :]
        a[...] = a[...] - ratio * pivot_row
        w[...] = w[...] - ratio * w_row

    u = a[...]
    pivots = jnp.maximum(jnp.sum(jnp.where(row == col, u, 0.0), axis=1, keepdims=True), 1e-12)
    root = lax.rsqrt(pivots)
    triangle[...] = jnp.where(row < col, u * root, jnp.where(row == col, pivots * root, 0.0)) / d_row
    inverse_t[...] = w[...] * root * d_row


def eliminated(gram, extra):
    n = gram.shape[0]
    return pl.pallas_call(
        elimination_kernel,
        out_shape=(jax.ShapeDtypeStruct((n, n), jnp.float32),) * 2,
        in_specs=[pl.BlockSpec(memory_space=pltpu.VMEM), pl.BlockSpec(memory_space=pltpu.SMEM)],
        out_specs=(pl.BlockSpec(memory_space=pltpu.VMEM),) * 2,
        scratch_shapes=[pltpu.VMEM((n, n), jnp.float32)] * 2,
        name="eliminate",
    )(gram, extra.reshape(1, 1))

MESH = pl.DeviceIdType.MESH


def all_reduce_kernel(sizes, x, out, half, part, summed, full, core_in, x_in, y_in, z_in, send, core_sem, x_sem, y_sem, z_sem, back_sem, pair_sem):
    nz, ny, nx = sizes
    me = lax.axis_index("dev")
    core, at_x = me % 2, me // 2 % nx
    at_y, at_z = me // (2 * nx) % ny, me // (2 * nx * ny)
    partner = me + 1 - 2 * core
    along = lambda at, j, size, stride: ((at + j) % size, me + ((at + j) % size - at) * stride)
    x_peers = [along(at_x, j, nx, 2) for j in range(1, nx)]
    y_peers = [along(at_y, j, ny, 2 * nx) for j in range(1, ny)]
    z_peers = [along(at_z, j, nz, 2 * nx * ny) for j in range(1, nz)]

    barrier = pltpu.get_barrier_semaphore()
    others = [partner] + [peer for _, peer in x_peers + y_peers + z_peers]
    for peer in others:
        pl.semaphore_signal(barrier, inc=1, device_id=(peer,), device_id_type=MESH)
    pl.semaphore_wait(barrier, len(others))

    started = []

    def copy(src, dst, recv_sem, peer):
        transfer = pltpu.make_async_remote_copy(
            src_ref=src, dst_ref=dst, send_sem=send.at[len(started)], recv_sem=recv_sem, device_id=(peer,), device_id_type=MESH
        )
        transfer.start()
        started.append(transfer)

    def arrived(dst, recv_sem):
        pltpu.make_async_remote_copy(
            src_ref=dst, dst_ref=dst, send_sem=send.at[0], recv_sem=recv_sem, device_id=(partner,), device_id_type=MESH
        ).wait_recv()

    rows = x.shape[0] // 2
    piece = rows // nx
    copy(x.at[pl.ds((1 - core) * rows, rows)], core_in, core_sem, partner)
    arrived(core_in, core_sem)
    half[...] = x[pl.ds(core * rows, rows)] + core_in[...]

    for other, peer in x_peers:
        copy(half.at[pl.ds(other * piece, piece)], x_in.at[at_x], x_sem.at[at_x], peer)
    x_in[at_x] = half[pl.ds(at_x * piece, piece)]
    for other, peer in x_peers:
        arrived(x_in.at[other], x_sem.at[other])
    total = x_in[0]
    for i in range(1, nx):
        total = total + x_in[i]

    for stage, (peers, at, size, slots, sem) in enumerate(((y_peers, at_y, ny, y_in, y_sem), (z_peers, at_z, nz, z_in, z_sem))):
        part[stage] = total
        for other, peer in peers:
            copy(part.at[stage], slots.at[at], sem.at[at], peer)
        slots[at] = total
        for other, peer in peers:
            arrived(slots.at[other], sem.at[other])
        total = slots[0]
        for i in range(1, size):
            total = total + slots[i]

    summed[...] = total
    mine = core * rows + at_x * piece
    for other, peer in x_peers:
        copy(summed, full.at[pl.ds(mine, piece)], back_sem.at[at_x], peer)
    copy(summed, full.at[pl.ds(mine, piece)], pair_sem.at[at_x], partner)
    full[pl.ds(mine, piece)] = total
    for other, peer in x_peers:
        there = full.at[pl.ds(core * rows + other * piece, piece)]
        arrived(there, back_sem.at[other])
        copy(there, there, pair_sem.at[other], partner)
    for i in range(nx):
        arrived(full.at[pl.ds((1 - core) * rows + i * piece, piece)], pair_sem.at[i])
    out[...] = full[...]
    for transfer in started:
        transfer.wait_send()


def all_reduce(x, sizes=(4, 4, 4)):
    nz, ny, nx = sizes
    n, m = x.shape
    rows = n // 2
    piece = rows // nx
    copies = 1 + (nx - 1) + (ny - 1) + (nz - 1) + nx + (nx - 1)
    block = lambda *lead: pltpu.VMEM((*lead, m), jnp.float32)
    return pl.pallas_call(
        functools.partial(all_reduce_kernel, sizes),
        out_shape=jax.ShapeDtypeStruct(x.shape, jnp.float32),
        in_specs=[pl.BlockSpec(memory_space=pltpu.VMEM)],
        out_specs=pl.BlockSpec(memory_space=pltpu.VMEM),
        scratch_shapes=[
            block(rows), block(2, piece), block(piece), block(n), block(rows), block(nx, piece), block(ny, piece), block(nz, piece),
            pltpu.SemaphoreType.DMA((copies,)), pltpu.SemaphoreType.DMA, pltpu.SemaphoreType.DMA((nx,)), pltpu.SemaphoreType.DMA((ny,)),
            pltpu.SemaphoreType.DMA((nz,)), pltpu.SemaphoreType.DMA((nx,)), pltpu.SemaphoreType.DMA((nx,)),
        ],
        compiler_params=pltpu.CompilerParams(collective_id=0, has_side_effects=True),
        name="all_reduce",
    )(x)


def split(x):
    high = x.astype(jnp.bfloat16)
    return high, (x - high.astype(jnp.float32)).astype(jnp.bfloat16)


def gram_kernel(a, b, out, cross):
    k, y = pl.program_id(0), pl.program_id(1)

    @pl.when(jnp.logical_and(k == 0, y == 0))
    def _():
        out[...] = jnp.zeros_like(out)
        cross[...] = jnp.zeros_like(cross)

    x = jnp.concatenate([r[...].reshape(-1, r.shape[-1]) for r in (a, b)], axis=1)
    high, low = split(x)
    product = lambda p, q: lax.dot_general(p, q, (((0,), (0,)), ((), ())), preferred_element_type=jnp.float32)
    out[...] += product(high, high)
    cross[...] += product(high, low)

    @pl.when(jnp.logical_and(k == pl.num_programs(0) - 1, y == pl.num_programs(1) - 1))
    def _():
        out[...] += cross[...] + cross[...].T


ROWS = 16


def gram_of(a, b):
    n = a.shape[3] + b.shape[3]
    spec = pl.BlockSpec((1, ROWS, a.shape[2], a.shape[3]), lambda k, y: (k, y, 0, 0))
    return pl.pallas_call(
        gram_kernel,
        out_shape=jax.ShapeDtypeStruct((n, n), jnp.float32),
        grid=(3, a.shape[1] // ROWS),
        in_specs=[spec, spec],
        out_specs=pl.BlockSpec((n, n), lambda k, y: (0, 0)),
        scratch_shapes=[pltpu.VMEM((n, n), jnp.float32)],
        name="gram",
    )(a, b)


def product_kernel(row_scale, a, b, inverse, out, high_s, low_s):
    @pl.when(jnp.logical_and(pl.program_id(0) == 0, pl.program_id(1) == 0))
    def _():
        high_s[...], low_s[...] = split(inverse[...] * row_scale)

    x = jnp.concatenate([r[...].reshape(-1, r.shape[-1]) for r in (a, b)], axis=1)
    high, low = split(x)
    product = lambda p, q: jnp.dot(p, q, preferred_element_type=jnp.float32)
    total = product(low, high_s[...]) + product(high, low_s[...]) + product(high, high_s[...])
    out[...] = total.reshape(out.shape)


def product_of(a, b, inverse, row_scale):
    n = a.shape[3] + b.shape[3]
    spec = pl.BlockSpec((1, ROWS, a.shape[2], a.shape[3]), lambda k, y: (k, y, 0, 0))
    return pl.pallas_call(
        functools.partial(product_kernel, row_scale),
        out_shape=jax.ShapeDtypeStruct((*a.shape[:3], n), jnp.float32),
        grid=(3, a.shape[1] // ROWS),
        in_specs=[spec, spec, pl.BlockSpec((n, n), lambda k, y: (0, 0))],
        out_specs=pl.BlockSpec((1, ROWS, a.shape[2], n), lambda k, y: (k, y, 0, 0)),
        scratch_shapes=[pltpu.VMEM((n, n), jnp.bfloat16)] * 2,
        name="product",
    )(a, b, inverse)


def neighbours(x):
    devices = lax.axis_size("dev")
    down = lax.ppermute(x, "dev", [(i, i - 1) for i in range(1, devices)])
    up = lax.ppermute(x, "dev", [(i, i + 1) for i in range(devices - 1)])
    return up, down


def local(start_block, modulus, occupancy):
    center, half_width = filter_bounds(element_matrix())
    coeff = (modulus * occupancy.astype(jnp.float32))[0]
    height, width = coeff.shape
    modes = start_block.shape[4]
    lanes = 128
    devices = lax.axis_size("dev")
    coeff_below = lax.ppermute(coeff, "dev", [(i, i + 1) for i in range(devices - 1)])
    spread = lambda c: jnp.broadcast_to(c[:, :, None], (height, width, lanes))

    flat = start_block.reshape(3, height, width, modes)
    current = [flat[..., i * lanes : (i + 1) * lanes] for i in range(modes // lanes)]
    *current, coeff_below = lax.optimization_barrier((*current, coeff_below))
    coeff_here, coeff_below = spread(coeff), spread(coeff_below)
    previous = [None] * len(current)
    for step in range(DEGREE):
        scale = (1.0 if step == 0 else 2.0) / half_width
        around = [neighbours(block) for block in current]
        following = [
            filter_step(below, here, above, coeff_below, coeff_here, old, scale, scale * center)
            for (below, above), here, old in zip(around, current, previous)
        ]
        previous, current = current, following

    first, second = current
    row_scale = math.sqrt(3 * height * width * devices)
    gram = all_reduce(gram_of(first, second))
    inverse, triangle, misfit = factored(gram)

    def direct(first, second, gram, inverse, triangle):
        return product_of(first, second, inverse, row_scale), triangle / row_scale

    def general(first, second, gram, inverse, triangle):
        x = jnp.concatenate([first, second], axis=-1).reshape(-1, modes)

        def one_pass(i, state):
            x, total = state
            extra = jnp.where(i == 0, 3e-5, 0.0).astype(jnp.float32)
            inverse_t, r = eliminated(all_reduce(dot_ta(x, x)), extra)
            return (dot(x, inverse_t.T), dot(r, total))

        x, total = lax.fori_loop(0, 4, one_pass, (x, jnp.eye(modes, dtype=jnp.float32)))
        return (x * row_scale).reshape(3, height, width, modes), total / row_scale

    basis, triangle = lax.cond(misfit[0, 0] <= 1e-4, direct, general, first, second, gram, inverse, triangle)
    return basis.reshape(start_block.shape), triangle


def solution(mesh):
    return jax.shard_map(
        local,
        mesh=mesh,
        in_specs=(P(None, "dev", None, None, None), P("dev", None, None), P("dev", None, None)),
        out_specs=(P(None, "dev", None, None, None), P()),
        check_vma=False,
    )
```

```python
import functools
import math

import jax
import jax.numpy as jnp
import numpy as np
from jax import lax
from jax.experimental import pallas as pl
from jax.experimental.pallas import tpu as pltpu
from jax.sharding import PartitionSpec as P

DEGREE = 3
HIGHEST = lax.Precision.HIGHEST
MESH = pl.DeviceIdType.MESH


def element_matrix():
    poisson = 0.3
    lame_first = poisson / ((1.0 + poisson) * (1.0 - 2.0 * poisson))
    shear_modulus = 0.5 / (1.0 + poisson)
    elastic = np.zeros((6, 6))
    elastic[:3, :3] = lame_first
    for axis_number in range(3):
        elastic[axis_number, axis_number] += 2.0 * shear_modulus
        elastic[axis_number + 3, axis_number + 3] = shear_modulus
    points = [0.5 - 0.5 / np.sqrt(3.0), 0.5 + 0.5 / np.sqrt(3.0)]
    stiffness = np.zeros((24, 24))
    for point_x in points:
        for point_y in points:
            for point_z in points:
                gradients = np.zeros((3, 8))
                for corner in range(8):
                    offset_x, offset_y, offset_z = (corner % 2, corner // 2 % 2, corner // 4)
                    along_x = point_x if offset_x else 1.0 - point_x
                    along_y = point_y if offset_y else 1.0 - point_y
                    along_z = point_z if offset_z else 1.0 - point_z
                    gradients[0, corner] = (2 * offset_x - 1) * along_y * along_z
                    gradients[1, corner] = (2 * offset_y - 1) * along_x * along_z
                    gradients[2, corner] = (2 * offset_z - 1) * along_x * along_y
                strain_map = np.zeros((6, 24))
                strain_map[0, 0:8] = gradients[0]
                strain_map[1, 8:16] = gradients[1]
                strain_map[2, 16:24] = gradients[2]
                strain_map[3, 0:8] = gradients[1]
                strain_map[3, 8:16] = gradients[0]
                strain_map[4, 8:16] = gradients[2]
                strain_map[4, 16:24] = gradients[1]
                strain_map[5, 0:8] = gradients[2]
                strain_map[5, 16:24] = gradients[0]
                stiffness += strain_map.T @ elastic @ strain_map / 8.0
    return stiffness


def filter_bounds(stiffness):
    upper_end = 8.0 * float(np.max(np.sum(np.abs(stiffness), axis=1)))
    lower_end = 0.15 * upper_end
    return (0.5 * (upper_end + lower_end), 0.5 * (upper_end - lower_end))


LAME = 0.3 / (1.3 * 0.4)
SHEAR = 0.5 / 1.3


def element_forces(h, coeff, factor):
    g = {}

    def coupled(keys, own, shared):
        total = h[keys[0]]
        for key in keys[1:]:
            total = total + h[key]
        total = total * shared
        for key in keys:
            g[key] = total if own is None else own * h[key] + total

    scaled = lambda value: coeff * (value * factor)
    mu16, mu48 = scaled(SHEAR / 16), scaled(SHEAR / 48)
    coupled([(0, "dss"), (1, "sds"), (2, "ssd")], scaled(2 * SHEAR / 16), scaled(LAME / 16))
    own, shared = scaled(3 * SHEAR / 48), scaled(LAME / 48)
    coupled([(0, "dsd"), (1, "sdd")], own, shared)
    coupled([(0, "dds"), (2, "sdd")], own, shared)
    coupled([(1, "dds"), (2, "dsd")], own, shared)
    coupled([(0, "sdd"), (1, "dsd"), (2, "dds")], mu48, mu48)
    coupled([(0, "sds"), (1, "dss")], None, mu16)
    coupled([(0, "ssd"), (2, "dss")], None, mu16)
    coupled([(1, "ssd"), (2, "sds")], None, mu16)
    last = scaled((LAME + 4 * SHEAR) / 144)
    for k in range(3):
        g[(k, "ddd")] = last * h[(k, "ddd")]
    return g


PLANES = {}
for _k in range(3):
    for _a in "sd":
        for _e in (0, 1):
            for _c in "sd":
                PLANES[(_k, _a, _e, _c)] = len(PLANES)

LANES = 128
CHUNK = 4


def element_rows(factor, shift, below, here, above, coeff, previous, out, planes, upward):
    tiles = here.shape[2] // 8
    rows = lax.broadcasted_iota(jnp.int32, (8, LANES), 0)

    def along_x(ref, k, y, t, lanes):
        a = ref[k, y, pl.ds(8 * t, 8), lanes]
        if t + 1 < tiles:
            b = ref[k, y, pl.ds(8 * t + 1, 8), lanes]
        else:
            b = jnp.where(rows == 7, 0.0, pltpu.roll(a, 7, 0))
        return a + b, b - a

    def along_xz(y, t, lanes):
        q = {}
        for k in range(3):
            low, mid, top = (along_x(ref, k, y, t, lanes) for ref in (below, here, above))
            for i, a in enumerate("sd"):
                q[(k, a, 0, "s")] = low[i] + mid[i]
                q[(k, a, 0, "d")] = mid[i] - low[i]
                q[(k, a, 1, "s")] = mid[i] + top[i]
                q[(k, a, 1, "d")] = top[i] - mid[i]
        return q

    def put(block, slot, t, q):
        for key, value in q.items():
            planes[block, slot, t, PLANES[key]] = value

    def lanes_of(block):
        return pl.ds(pl.multiple_of(block * LANES, LANES), LANES)

    def start(block):
        for t in range(tiles):
            put(block, 0, t, along_xz(0, t, lanes_of(block)))
            for i in range(6):
                upward[block, t, i] = jnp.zeros((8, LANES), jnp.float32)

    def work(y, block, last):
        slot = y % 2
        lanes = lanes_of(block)
        carry = [jnp.zeros((8, LANES), jnp.float32)] * 3
        for t in range(tiles):
            if not last:
                far = along_xz(y + 1, t, lanes)
                put(block, 1 - slot, t, far)
            force = {}
            for e in (0, 1):
                h = {}
                for k in range(3):
                    for a in "sd":
                        for c in "sd":
                            near = planes[block, slot, t, PLANES[(k, a, e, c)]]
                            if last:
                                h[(k, a + "s" + c)] = near
                                h[(k, a + "d" + c)] = -near
                            else:
                                h[(k, a + "s" + c)] = near + far[(k, a, e, c)]
                                h[(k, a + "d" + c)] = far[(k, a, e, c)] - near
                g = element_forces(h, coeff[e, y, pl.ds(8 * t, 8), :], factor)
                for k in range(3):
                    for a in "sd":
                        for b in "sd":
                            difference = g[(k, a + b + "d")]
                            if e == 1:
                                difference = -difference
                            if a + b != "ss":
                                difference = g[(k, a + b + "s")] + difference
                            key = (k, a, b)
                            force[key] = difference if e == 0 else force[key] + difference
            for k in range(3):
                part = {}
                for i, a in enumerate("sd"):
                    part[a] = force[(k, a, "s")] - force[(k, a, "d")] + upward[block, t, 2 * k + i]
                    upward[block, t, 2 * k + i] = force[(k, a, "s")] + force[(k, a, "d")]
                moved = pltpu.roll(part["s"] + part["d"], 1, 0)
                total = (part["s"] - part["d"]) + jnp.where(rows == 0, carry[k], moved)
                carry[k] = moved
                where = (k, y, pl.ds(8 * t, 8), lanes)
                value = total - shift * here[where]
                if previous is not None:
                    value = value - previous[where]
                out[where] = value

    return start, work


def filter_kernel(
    devices, center, half_width, first, coeff_t, out, second, third, below, above, coeff_in, coeff, planes, upward,
    send, recv, coeff_send, coeff_recv,
):
    height = first.shape[1]
    chunks = height // CHUNK
    blocks = first.shape[3] // LANES
    me = lax.axis_index("dev")
    has_below, has_above = me > 0, me < devices - 1
    stages = [first, second, third, out]
    sides = ((has_below, me - 1, above, 0), (has_above, me + 1, below, 1))
    barrier = pltpu.get_barrier_semaphore()
    for present, peer, _, _ in sides:

        @pl.when(present)
        def _():
            pl.semaphore_signal(barrier, inc=1, device_id=(peer,), device_id_type=MESH)

    pl.semaphore_wait(barrier, has_below.astype(jnp.int32) + has_above.astype(jnp.int32))

    def chunk_copy(r, side, j):
        present, peer, landing, way = sides[side]
        rows = pl.ds(pl.multiple_of(j * CHUNK, CHUNK), CHUNK)
        return pltpu.make_async_remote_copy(
            src_ref=stages[r].at[:, rows], dst_ref=landing.at[r, :, rows], send_sem=send.at[r, way, j],
            recv_sem=recv.at[r, way, j], device_id=(peer,), device_id_type=MESH,
        )

    def coeff_copy():
        return pltpu.make_async_remote_copy(
            src_ref=coeff_t, dst_ref=coeff_in, send_sem=coeff_send, recv_sem=coeff_recv, device_id=(me + 1,), device_id_type=MESH
        )

    def send_chunk(r, j):
        for side in (0, 1):

            @pl.when(sides[side][0])
            def _():
                chunk_copy(r, side, j).start()

    @pl.when(has_above)
    def _():
        coeff_copy().start()

    @pl.loop(0, chunks)
    def _(j):
        send_chunk(0, j)

    def clear(ref):
        @pl.loop(0, height)
        def _(y):
            for r in range(3):
                for k in range(3):
                    ref[r, k, y] = jnp.zeros(ref.shape[3:], jnp.float32)

    @pl.when(jnp.logical_not(has_below))
    def _():
        clear(below)
        coeff_in[...] = jnp.zeros_like(coeff_in)

    @pl.when(jnp.logical_not(has_above))
    def _():
        clear(above)

    @pl.when(has_below)
    def _():
        coeff_copy().wait_recv()

    for e, ref in enumerate((coeff_in, coeff_t)):
        columns = ref[...]
        for y in range(height):
            coeff[e, y] = jnp.broadcast_to(columns[:, y : y + 1], (columns.shape[0], LANES))

    for r in range(3):
        factor = (1.0 if r == 0 else 2.0) / half_width
        start, work = element_rows(
            factor, factor * center, below.at[r], stages[r], above.at[r], coeff, stages[r - 1] if r else None, stages[r + 1], planes, upward
        )

        @pl.loop(0, chunks)
        def _(j):
            @pl.when(has_below)
            def _():
                chunk_copy(r, 1, j).wait_recv()

            @pl.when(has_above)
            def _():
                chunk_copy(r, 0, j).wait_recv()

            @pl.when(j == 0)
            def _():
                @pl.loop(0, blocks)
                def _(block):
                    start(block)

            @pl.loop(jnp.maximum(j * CHUNK - 1, 0), j * CHUNK + CHUNK - 1)
            def _(y):
                @pl.loop(0, blocks)
                def _(block):
                    work(y, block, False)

            if r < 2:

                @pl.when(j > 0)
                def _():
                    send_chunk(r + 1, j - 1)

        @pl.loop(0, blocks)
        def _(block):
            work(height - 1, block, True)

        if r < 2:
            send_chunk(r + 1, chunks - 1)

    @pl.when(has_above)
    def _():
        coeff_copy().wait_send()

    for r in range(3):

        @pl.loop(0, chunks)
        def _(j):
            for side in (0, 1):

                @pl.when(sides[side][0])
                def _():
                    chunk_copy(r, side, j).wait_send()


def filtered(block, coeff_t, center, half_width):
    _, height, width, modes = block.shape
    chunks, blocks = height // CHUNK, modes // LANES
    vmem = lambda *shape: pltpu.VMEM(shape, jnp.float32)
    return pl.pallas_call(
        functools.partial(filter_kernel, lax.axis_size("dev"), center, half_width),
        out_shape=jax.ShapeDtypeStruct(block.shape, jnp.float32),
        in_specs=[pl.BlockSpec(memory_space=pltpu.VMEM)] * 2,
        out_specs=pl.BlockSpec(memory_space=pltpu.VMEM),
        scratch_shapes=[
            vmem(*block.shape), vmem(*block.shape), vmem(3, *block.shape), vmem(3, *block.shape), vmem(*coeff_t.shape),
            vmem(2, height, width, LANES), vmem(blocks, 2, width // 8, 24, 8, LANES), vmem(blocks, width // 8, 6, 8, LANES),
            pltpu.SemaphoreType.DMA((3, 2, chunks)), pltpu.SemaphoreType.DMA((3, 2, chunks)),
            pltpu.SemaphoreType.DMA, pltpu.SemaphoreType.DMA,
        ],
        compiler_params=pltpu.CompilerParams(collective_id=1, has_side_effects=True),
        name="filter",
    )(block, coeff_t)


def dot(a, b):
    return jnp.dot(a, b, precision=HIGHEST, preferred_element_type=jnp.float32)


def dot_ta(a, b):
    return lax.dot_general(a, b, (((0,), (0,)), ((), ())), precision=HIGHEST, preferred_element_type=jnp.float32)


SWEEPS = 10
TARGET = 1e-6


def factor_kernel(scale, gram, inverse, triangle, misfit):
    g = gram[...]
    n = g.shape[0]
    row = lax.broadcasted_iota(jnp.int32, (n, n), 0)
    col = lax.broadcasted_iota(jnp.int32, (n, n), 1)
    diagonal = jnp.where(row == col, g, 0.0)
    d_col = lax.rsqrt(jnp.sum(diagonal, axis=1, keepdims=True))
    d_row = lax.rsqrt(jnp.sum(diagonal, axis=0, keepdims=True))
    unit = g * d_col * d_row
    one = jnp.where(row == col, 1.0, 0.0)
    weight = jnp.where(row < col, 1.0, jnp.where(row == col, 0.5, 0.0))

    def refined(state):
        s, _, count = state
        excess = dot_ta(s, dot(unit, s)) - one
        s = s - dot(s, excess * weight)
        return (s, jnp.sum(excess * excess), count + 1)

    start = one - (unit - one) * weight
    s, size, _ = lax.while_loop(
        lambda state: jnp.logical_and(state[1] > TARGET, state[2] < SWEEPS), refined, (start, jnp.float32(1.0), 0)
    )
    inverse[...] = d_col * s
    r = dot_ta(s, unit)
    triangle[...] = jnp.where(row <= col, r * (scale / d_row), 0.0)
    norm = jnp.sum(s * s)
    misfit[0, 0] = jnp.where(norm <= n + 50.0, size, 1.0)


def factored(gram, scale):
    n = gram.shape[0]
    return pl.pallas_call(
        functools.partial(factor_kernel, scale),
        out_shape=(
            jax.ShapeDtypeStruct((n, n), jnp.float32),
            jax.ShapeDtypeStruct((n, n), jnp.float32),
            jax.ShapeDtypeStruct((1, 1), jnp.float32),
        ),
        in_specs=[pl.BlockSpec(memory_space=pltpu.VMEM)],
        out_specs=(
            pl.BlockSpec(memory_space=pltpu.VMEM),
            pl.BlockSpec(memory_space=pltpu.VMEM),
            pl.BlockSpec(memory_space=pltpu.SMEM),
        ),
        name="factor",
    )(gram)


def elimination_kernel(gram, extra, inverse_t, triangle, a, w):
    n = gram.shape[0]
    row = lax.broadcasted_iota(jnp.int32, (n, n), 0)
    col = lax.broadcasted_iota(jnp.int32, (n, n), 1)
    g = gram[...]
    one = jnp.where(row == col, 1.0, 0.0)
    diagonal = jnp.where(row == col, g, 0.0)
    s_col = jnp.sum(diagonal, axis=1, keepdims=True)
    s_row = jnp.sum(diagonal, axis=0, keepdims=True)
    d_col = lax.rsqrt(jnp.where(s_col > 0, s_col, 1.0))
    d_row = lax.rsqrt(jnp.where(s_row > 0, s_row, 1.0))
    a[...] = g * d_col * d_row + extra[0, 0] * one
    w[...] = one

    @pl.loop(0, n)
    def _(k):
        pivot_row = a[pl.ds(k, 1), :]
        column = jnp.sum(jnp.where(col == k, a[...], 0.0), axis=1, keepdims=True)
        lane = lax.broadcasted_iota(jnp.int32, (1, n), 1)
        pivot = jnp.maximum(jnp.sum(jnp.where(lane == k, pivot_row, 0.0), axis=1, keepdims=True), 1e-12)
        below = lax.broadcasted_iota(jnp.int32, (n, 1), 0) > k
        ratio = jnp.where(below, column / pivot, 0.0)
        w_row = w[pl.ds(k, 1), :]
        a[...] = a[...] - ratio * pivot_row
        w[...] = w[...] - ratio * w_row

    u = a[...]
    pivots = jnp.maximum(jnp.sum(jnp.where(row == col, u, 0.0), axis=1, keepdims=True), 1e-12)
    root = lax.rsqrt(pivots)
    triangle[...] = jnp.where(row < col, u * root, jnp.where(row == col, pivots * root, 0.0)) / d_row
    inverse_t[...] = w[...] * root * d_row


def eliminated(gram, extra):
    n = gram.shape[0]
    return pl.pallas_call(
        elimination_kernel,
        out_shape=(jax.ShapeDtypeStruct((n, n), jnp.float32),) * 2,
        in_specs=[pl.BlockSpec(memory_space=pltpu.VMEM), pl.BlockSpec(memory_space=pltpu.SMEM)],
        out_specs=(pl.BlockSpec(memory_space=pltpu.VMEM),) * 2,
        scratch_shapes=[pltpu.VMEM((n, n), jnp.float32)] * 2,
        name="eliminate",
    )(gram, extra.reshape(1, 1))


def all_reduce_kernel(sizes, x, out, half, part, summed, full, core_in, x_in, y_in, z_in, send, core_sem, x_sem, y_sem, z_sem, back_sem, pair_sem):
    nz, ny, nx = sizes
    me = lax.axis_index("dev")
    core, at_x = me % 2, me // 2 % nx
    at_y, at_z = me // (2 * nx) % ny, me // (2 * nx * ny)
    partner = me + 1 - 2 * core
    along = lambda at, j, size, stride: ((at + j) % size, me + ((at + j) % size - at) * stride)
    x_peers = [along(at_x, j, nx, 2) for j in range(1, nx)]
    y_peers = [along(at_y, j, ny, 2 * nx) for j in range(1, ny)]
    z_peers = [along(at_z, j, nz, 2 * nx * ny) for j in range(1, nz)]

    barrier = pltpu.get_barrier_semaphore()
    others = [partner] + [peer for _, peer in x_peers + y_peers + z_peers]
    for peer in others:
        pl.semaphore_signal(barrier, inc=1, device_id=(peer,), device_id_type=MESH)
    pl.semaphore_wait(barrier, len(others))

    started = []

    def copy(src, dst, recv_sem, peer):
        transfer = pltpu.make_async_remote_copy(
            src_ref=src, dst_ref=dst, send_sem=send.at[len(started)], recv_sem=recv_sem, device_id=(peer,), device_id_type=MESH
        )
        transfer.start()
        started.append(transfer)

    def arrived(dst, recv_sem):
        pltpu.make_async_remote_copy(
            src_ref=dst, dst_ref=dst, send_sem=send.at[0], recv_sem=recv_sem, device_id=(partner,), device_id_type=MESH
        ).wait_recv()

    rows = x.shape[0] // 2
    piece = rows // nx
    copy(x.at[pl.ds((1 - core) * rows, rows)], core_in, core_sem, partner)
    arrived(core_in, core_sem)
    half[...] = x[pl.ds(core * rows, rows)] + core_in[...]

    for other, peer in x_peers:
        copy(half.at[pl.ds(other * piece, piece)], x_in.at[at_x], x_sem.at[at_x], peer)
    x_in[at_x] = half[pl.ds(at_x * piece, piece)]
    for other, peer in x_peers:
        arrived(x_in.at[other], x_sem.at[other])
    total = x_in[0]
    for i in range(1, nx):
        total = total + x_in[i]

    for stage, (peers, at, size, slots, sem) in enumerate(((y_peers, at_y, ny, y_in, y_sem), (z_peers, at_z, nz, z_in, z_sem))):
        part[stage] = total
        for other, peer in peers:
            copy(part.at[stage], slots.at[at], sem.at[at], peer)
        slots[at] = total
        for other, peer in peers:
            arrived(slots.at[other], sem.at[other])
        total = slots[0]
        for i in range(1, size):
            total = total + slots[i]

    summed[...] = total
    mine = core * rows + at_x * piece
    for other, peer in x_peers:
        copy(summed, full.at[pl.ds(mine, piece)], back_sem.at[at_x], peer)
    copy(summed, full.at[pl.ds(mine, piece)], pair_sem.at[at_x], partner)
    full[pl.ds(mine, piece)] = total
    for other, peer in x_peers:
        there = full.at[pl.ds(core * rows + other * piece, piece)]
        arrived(there, back_sem.at[other])
        copy(there, there, pair_sem.at[other], partner)
    for i in range(nx):
        arrived(full.at[pl.ds((1 - core) * rows + i * piece, piece)], pair_sem.at[i])
    out[...] = full[...]
    for transfer in started:
        transfer.wait_send()


def all_reduce(x, sizes=(4, 4, 4)):
    nz, ny, nx = sizes
    n, m = x.shape
    rows = n // 2
    piece = rows // nx
    copies = 1 + (nx - 1) + (ny - 1) + (nz - 1) + nx + (nx - 1)
    block = lambda *lead: pltpu.VMEM((*lead, m), jnp.float32)
    return pl.pallas_call(
        functools.partial(all_reduce_kernel, sizes),
        out_shape=jax.ShapeDtypeStruct(x.shape, jnp.float32),
        in_specs=[pl.BlockSpec(memory_space=pltpu.VMEM)],
        out_specs=pl.BlockSpec(memory_space=pltpu.VMEM),
        scratch_shapes=[
            block(rows), block(2, piece), block(piece), block(n), block(rows), block(nx, piece), block(ny, piece), block(nz, piece),
            pltpu.SemaphoreType.DMA((copies,)), pltpu.SemaphoreType.DMA, pltpu.SemaphoreType.DMA((nx,)), pltpu.SemaphoreType.DMA((ny,)),
            pltpu.SemaphoreType.DMA((nz,)), pltpu.SemaphoreType.DMA((nx,)), pltpu.SemaphoreType.DMA((nx,)),
        ],
        compiler_params=pltpu.CompilerParams(collective_id=0, has_side_effects=True),
        name="all_reduce",
    )(x)


def split(x):
    high = x.astype(jnp.bfloat16)
    return high, (x - high.astype(jnp.float32)).astype(jnp.bfloat16)


def gram_kernel(x_ref, out, cross):
    k, y = pl.program_id(0), pl.program_id(1)

    @pl.when(jnp.logical_and(k == 0, y == 0))
    def _():
        out[...] = jnp.zeros_like(out)
        cross[...] = jnp.zeros_like(cross)

    high, low = split(x_ref[...].reshape(-1, x_ref.shape[-1]))
    product = lambda p, q: lax.dot_general(p, q, (((0,), (0,)), ((), ())), preferred_element_type=jnp.float32)
    out[...] += product(high, high)
    cross[...] += product(high, low)

    @pl.when(jnp.logical_and(k == pl.num_programs(0) - 1, y == pl.num_programs(1) - 1))
    def _():
        out[...] += cross[...] + cross[...].T


ROWS = 16


def gram_of(x):
    n = x.shape[3]
    return pl.pallas_call(
        gram_kernel,
        out_shape=jax.ShapeDtypeStruct((n, n), jnp.float32),
        grid=(3, x.shape[1] // ROWS),
        in_specs=[pl.BlockSpec((1, ROWS, x.shape[2], n), lambda k, y: (k, y, 0, 0))],
        out_specs=pl.BlockSpec((n, n), lambda k, y: (0, 0)),
        scratch_shapes=[pltpu.VMEM((n, n), jnp.float32)],
        name="gram",
    )(x)


def product_kernel(row_scale, x_ref, inverse, out, high_s, low_s):
    @pl.when(jnp.logical_and(pl.program_id(0) == 0, pl.program_id(1) == 0))
    def _():
        high_s[...], low_s[...] = split(inverse[...] * row_scale)

    high, low = split(x_ref[...].reshape(-1, x_ref.shape[-1]))
    product = lambda p, q: jnp.dot(p, q, preferred_element_type=jnp.float32)
    total = product(low, high_s[...]) + product(high, low_s[...]) + product(high, high_s[...])
    out[...] = total.reshape(out.shape)


def product_of(x, inverse, row_scale):
    n = x.shape[3]
    spec = pl.BlockSpec((1, ROWS, x.shape[2], n), lambda k, y: (k, y, 0, 0))
    return pl.pallas_call(
        functools.partial(product_kernel, row_scale),
        out_shape=jax.ShapeDtypeStruct(x.shape, jnp.float32),
        grid=(3, x.shape[1] // ROWS),
        in_specs=[spec, pl.BlockSpec((n, n), lambda k, y: (0, 0))],
        out_specs=spec,
        scratch_shapes=[pltpu.VMEM((n, n), jnp.bfloat16)] * 2,
        name="product",
    )(x, inverse)


def local(start_block, modulus, occupancy):
    center, half_width = filter_bounds(element_matrix())
    coeff_t = (modulus * occupancy.astype(jnp.float32))[0].T
    modes = start_block.shape[4]
    flat = start_block.reshape(3, *start_block.shape[2:])
    row_scale = math.sqrt(math.prod(flat.shape[:3]) * lax.axis_size("dev"))
    current = filtered(flat, coeff_t, center, half_width)
    gram = all_reduce(gram_of(current))
    inverse, triangle, misfit = factored(gram, 1.0 / row_scale)

    def direct(x, gram, inverse, triangle):
        return product_of(x, inverse, row_scale), triangle

    def general(x, gram, inverse, triangle):
        def one_pass(i, state):
            x, total = state
            extra = jnp.where(i == 0, 3e-5, 0.0).astype(jnp.float32)
            inverse_t, r = eliminated(all_reduce(dot_ta(x, x)), extra)
            return (dot(x, inverse_t.T), dot(r, total))

        x, total = lax.fori_loop(0, 4, one_pass, (x.reshape(-1, modes), jnp.eye(modes, dtype=jnp.float32)))
        return (x * row_scale).reshape(flat.shape), total / row_scale

    basis, triangle = lax.cond(misfit[0, 0] <= 1e-4, direct, general, current, gram, inverse, triangle)
    return basis.reshape(start_block.shape), triangle


def solution(mesh):
    return jax.shard_map(
        local,
        mesh=mesh,
        in_specs=(P(None, "dev", None, None, None), P("dev", None, None), P("dev", None, None)),
        out_specs=(P(None, "dev", None, None, None), P()),
        check_vma=False,
    )
```

```python
import functools
import math

import jax
import jax.numpy as jnp
import numpy as np
from jax import lax
from jax.experimental import pallas as pl
from jax.experimental.pallas import tpu as pltpu
from jax.sharding import PartitionSpec as P

DEGREE = 3
HIGHEST = lax.Precision.HIGHEST
MESH = pl.DeviceIdType.MESH


def element_matrix():
    poisson = 0.3
    lame_first = poisson / ((1.0 + poisson) * (1.0 - 2.0 * poisson))
    shear_modulus = 0.5 / (1.0 + poisson)
    elastic = np.zeros((6, 6))
    elastic[:3, :3] = lame_first
    for axis_number in range(3):
        elastic[axis_number, axis_number] += 2.0 * shear_modulus
        elastic[axis_number + 3, axis_number + 3] = shear_modulus
    points = [0.5 - 0.5 / np.sqrt(3.0), 0.5 + 0.5 / np.sqrt(3.0)]
    stiffness = np.zeros((24, 24))
    for point_x in points:
        for point_y in points:
            for point_z in points:
                gradients = np.zeros((3, 8))
                for corner in range(8):
                    offset_x, offset_y, offset_z = (corner % 2, corner // 2 % 2, corner // 4)
                    along_x = point_x if offset_x else 1.0 - point_x
                    along_y = point_y if offset_y else 1.0 - point_y
                    along_z = point_z if offset_z else 1.0 - point_z
                    gradients[0, corner] = (2 * offset_x - 1) * along_y * along_z
                    gradients[1, corner] = (2 * offset_y - 1) * along_x * along_z
                    gradients[2, corner] = (2 * offset_z - 1) * along_x * along_y
                strain_map = np.zeros((6, 24))
                strain_map[0, 0:8] = gradients[0]
                strain_map[1, 8:16] = gradients[1]
                strain_map[2, 16:24] = gradients[2]
                strain_map[3, 0:8] = gradients[1]
                strain_map[3, 8:16] = gradients[0]
                strain_map[4, 8:16] = gradients[2]
                strain_map[4, 16:24] = gradients[1]
                strain_map[5, 0:8] = gradients[2]
                strain_map[5, 16:24] = gradients[0]
                stiffness += strain_map.T @ elastic @ strain_map / 8.0
    return stiffness


def filter_bounds(stiffness):
    upper_end = 8.0 * float(np.max(np.sum(np.abs(stiffness), axis=1)))
    lower_end = 0.15 * upper_end
    return (0.5 * (upper_end + lower_end), 0.5 * (upper_end - lower_end))


LAME = 0.3 / (1.3 * 0.4)
SHEAR = 0.5 / 1.3


def element_forces(h, coeff, factor):
    g = {}

    def coupled(keys, own, shared):
        total = h[keys[0]]
        for key in keys[1:]:
            total = total + h[key]
        total = total * shared
        for key in keys:
            g[key] = total if own is None else own * h[key] + total

    scaled = lambda value: coeff * (value * factor)
    mu16, mu48 = scaled(SHEAR / 16), scaled(SHEAR / 48)
    coupled([(0, "dss"), (1, "sds"), (2, "ssd")], scaled(2 * SHEAR / 16), scaled(LAME / 16))
    own, shared = scaled(3 * SHEAR / 48), scaled(LAME / 48)
    coupled([(0, "dsd"), (1, "sdd")], own, shared)
    coupled([(0, "dds"), (2, "sdd")], own, shared)
    coupled([(1, "dds"), (2, "dsd")], own, shared)
    coupled([(0, "sdd"), (1, "dsd"), (2, "dds")], mu48, mu48)
    coupled([(0, "sds"), (1, "dss")], None, mu16)
    coupled([(0, "ssd"), (2, "dss")], None, mu16)
    coupled([(1, "ssd"), (2, "sds")], None, mu16)
    last = scaled((LAME + 4 * SHEAR) / 144)
    for k in range(3):
        g[(k, "ddd")] = last * h[(k, "ddd")]
    return g


PLANES = {}
for _k in range(3):
    for _a in "sd":
        for _b in "sd":
            PLANES[(_k, _a, _b)] = len(PLANES)

TILE = 128
GROUP = 8
ROW = 8
SPARE = ROW + 2


def filter_round(factor, shift, width, here, previous, out, coeff, planes, upward):
    tiles = here.shape[3] // TILE
    lane = lax.broadcasted_iota(jnp.int32, (GROUP, TILE), 1)
    first_x, last_x = lane % width == 0, lane % width == width - 1
    low_rows, high_rows = lane < TILE - width, lane >= width
    tile = lambda t: pl.ds(t * TILE, TILE)

    def along_x(layer, t):
        q = {}
        for k in range(3):
            a = here[layer, k, :, tile(t)]
            b = jnp.where(last_x, 0.0, pltpu.roll(a, TILE - 1, 1))
            for name, value in (("s", a + b), ("d", b - a)):
                q[(k, name)] = (value, pltpu.roll(value, TILE - width, 1))
        return q

    def along_xy(layer):
        ahead = along_x(layer, 0)
        for t in range(tiles):
            now = ahead
            ahead = along_x(layer, t + 1) if t + 1 < tiles else None
            q = {}
            for key, (value, rolled) in now.items():
                after = jnp.where(low_rows, rolled, ahead[key][1] if ahead else 0.0)
                q[(*key, "s")] = value + after
                q[(*key, "d")] = after - value
            yield t, q

    def put(slot, t, q):
        for key, value in q.items():
            planes[slot, t, PLANES[key]] = value

    for t, q in along_xy(0):
        put(0, t, q)

    @pl.loop(0, ROW + 1)
    def _(e):
        slot = e % 2
        target = jnp.where(e == 0, SPARE, e)
        behind = {}
        for t, far in along_xy(e + 1):
            h = {}
            for key, value in far.items():
                near = planes[slot, t, PLANES[key]]
                name = key[1] + key[2]
                h[(key[0], name + "s")] = near + value
                h[(key[0], name + "d")] = value - near
            put(1 - slot, t, far)
            g = element_forces(h, jnp.broadcast_to(coeff[e, pl.ds(t, 1), :], (GROUP, TILE)), factor)
            force = {}
            for key, place in PLANES.items():
                name = key[1] + key[2]
                even, odd = g.get((key[0], name + "s")), g[(key[0], name + "d")]
                force[key] = upward[t, place] + (-odd if even is None else even - odd)
                upward[t, place] = odd if even is None else even + odd
            for k in range(3):
                part = {}
                for a in "sd":
                    up, down = force[(k, a, "s")], force[(k, a, "d")]
                    rolled = pltpu.roll(up + down, width, 1)
                    part[a] = (up - down) + jnp.where(high_rows, rolled, behind.get((k, a), 0.0))
                    behind[(k, a)] = rolled
                moved = jnp.where(first_x, 0.0, pltpu.roll(part["s"] + part["d"], 1, 1))
                where = (k, slice(None), tile(t))
                value = (part["s"] - part["d"]) + moved - shift * here[(e, *where)]
                if previous is not None:
                    value = value - previous[(e, *where)]
                out[(target, *where)] = value


ORDER = (
    ("in", 0), (0, 0), ("in", 1), (1, 0), (0, 1), ("in", 2), (2, 0), (1, 1),
    (0, 2), ("in", 3), (2, 1), (1, 2), (0, 3), (2, 2), (1, 3), (2, 3),
)


def filter_kernel(
    devices, center, half_width, width, x, coeff_mine, home, turned, state, coeff, planes, upward,
    in_send, in_recv, halo_send, halo_recv, out_send, out_recv, coeff_send, coeff_recv, edge_send, edge_recv,
):
    me = lax.axis_index("dev")
    place, row = me % ROW, me // ROW
    base = me - place
    has_below, has_above = row > 0, row < devices // ROW - 1
    groups = turned.shape[0] // ROW
    nodes = x.shape[1]
    mates = []
    for side in (0, 1):
        for step in (1, 3, 2) if side == 0 else (1, 3, 2, 0):
            chip, core = (place // 2 + step) % (ROW // 2), (place % 2 + side) % 2
            mates.append(2 * chip + core)
    barrier = pltpu.get_barrier_semaphore()
    for mate in mates:
        pl.semaphore_signal(barrier, inc=1, device_id=(base + mate,), device_id_type=MESH)
    for present, peer in ((has_below, me - ROW), (has_above, me + ROW)):

        @pl.when(present)
        def _():
            pl.semaphore_signal(barrier, inc=1, device_id=(peer,), device_id_type=MESH)

    @pl.loop(0, 3 * (nodes // TILE))
    def _(i):
        k, t = i // (nodes // TILE), i % (nodes // TILE)
        lanes = pl.ds(pl.multiple_of(t * TILE, TILE), TILE)
        for c in range(x.shape[2] // TILE):
            block = x[k, lanes, pl.ds(c * TILE, TILE)].T
            for g in range(TILE // GROUP):
                turned[c * (TILE // GROUP) + g, k, :, lanes] = block[g * GROUP : (g + 1) * GROUP]

    coeff[1 + place] = coeff_mine[...]

    def remote(src, dst, send_sem, recv_sem, peer):
        return pltpu.make_async_remote_copy(
            src_ref=src, dst_ref=dst, send_sem=send_sem, recv_sem=recv_sem, device_id=(peer,), device_id_type=MESH
        )

    def coeff_copy(mate):
        return remote(coeff_mine, coeff.at[1 + place], coeff_send.at[mate], coeff_recv.at[place], base + mate)

    def in_copy(q, mate):
        return remote(
            turned.at[groups * mate + q], state.at[0, q, 1 + place], in_send.at[q, mate], in_recv.at[q, place], base + mate
        )

    def out_copy(q, mate):
        return remote(state.at[3, q, 1 + mate], home.at[groups * place + q], out_send.at[q, mate], out_recv.at[q, place], base + mate)

    def halo_copy(s, q, way):
        source, target, peer = ((ROW, 0, me + ROW), (1, ROW + 1, me - ROW))[way]
        return remote(state.at[s, q, source], state.at[s, q, target], halo_send.at[s, q, way], halo_recv.at[s, q, way], peer)

    def edge_copy():
        return remote(coeff.at[ROW], coeff.at[0], edge_send, edge_recv, me + ROW)

    def arrived(dst, recv_sem):
        remote(dst, dst, edge_send, recv_sem, base + mates[0]).wait_recv()

    pl.semaphore_wait(barrier, len(mates) + has_below.astype(jnp.int32) + has_above.astype(jnp.int32))
    for mate in mates:
        coeff_copy(mate).start()

    @pl.loop(0, groups)
    def _(q):
        for mate in mates:
            in_copy(q, mate).start()

    @pl.loop(0, groups)
    def _(q):
        state[0, q, 1 + place] = turned[groups * place + q]

    upward[...] = jnp.zeros_like(upward)

    @pl.when(jnp.logical_not(has_below))
    def _():
        coeff[0] = jnp.zeros(coeff.shape[1:], jnp.float32)

    for present, layer in ((has_below, 0), (has_above, ROW + 1)):

        @pl.when(jnp.logical_not(present))
        def _():
            @pl.loop(0, groups)
            def _(q):
                for s in range(3):
                    state[s, q, layer] = jnp.zeros(state.shape[3:], jnp.float32)

    for mate in mates:
        arrived(coeff.at[1 + mate], coeff_recv.at[mate])

    @pl.when(has_above)
    def _():
        edge_copy().start()

    @pl.when(has_below)
    def _():
        arrived(coeff.at[0], edge_recv)

    def send_halo(s, q):
        for present, way in ((has_above, 0), (has_below, 1)):

            @pl.when(present)
            def _():
                halo_copy(s, q, way).start()

    for s, q in ORDER:
        if s == "in":
            for mate in mates:
                arrived(state.at[0, q, 1 + mate], in_recv.at[q, mate])
            send_halo(0, q)
            continue
        for present, way, layer in ((has_below, 0, 0), (has_above, 1, ROW + 1)):

            @pl.when(present)
            def _():
                arrived(state.at[s, q, layer], halo_recv.at[s, q, way])

        factor = (1.0 if s == 0 else 2.0) / half_width
        previous = state.at[s - 1, q] if s else None
        filter_round(factor, factor * center, width, state.at[s, q], previous, state.at[s + 1, q], coeff, planes, upward)
        if s < 2:
            send_halo(s + 1, q)
        else:
            for mate in mates:
                out_copy(q, mate).start()
            home[groups * place + q] = state[3, q, 1 + place]

    @pl.loop(0, groups)
    def _(q):
        for mate in mates:
            arrived(home.at[groups * mate + q], out_recv.at[q, mate])
            in_copy(q, mate).wait_send()
            out_copy(q, mate).wait_send()
        for s in range(3):
            for present, way in ((has_above, 0), (has_below, 1)):

                @pl.when(present)
                def _():
                    halo_copy(s, q, way).wait_send()

    for mate in mates:
        coeff_copy(mate).wait_send()

    @pl.when(has_above)
    def _():
        edge_copy().wait_send()


def filtered(block, coeff, center, half_width, width):
    _, nodes, modes = block.shape
    groups, tiles = modes // GROUP // ROW, nodes // TILE
    vmem = lambda *shape: pltpu.VMEM(shape, jnp.float32)
    dma = pltpu.SemaphoreType.DMA
    return pl.pallas_call(
        functools.partial(filter_kernel, lax.axis_size("dev"), center, half_width, width),
        out_shape=jax.ShapeDtypeStruct((modes // GROUP, 3, GROUP, nodes), jnp.float32),
        in_specs=[pl.BlockSpec(memory_space=pltpu.VMEM)] * 2,
        out_specs=pl.BlockSpec(memory_space=pltpu.VMEM),
        scratch_shapes=[
            vmem(modes // GROUP, 3, GROUP, nodes), vmem(4, groups, SPARE + 1, 3, GROUP, nodes), vmem(ROW + 1, tiles, TILE),
            vmem(2, tiles, 12, GROUP, TILE), vmem(tiles, 12, GROUP, TILE),
            dma((groups, ROW)), dma((groups, ROW)), dma((3, groups, 2)), dma((3, groups, 2)), dma((groups, ROW)), dma((groups, ROW)),
            dma((ROW,)), dma((ROW,)), dma, dma,
        ],
        compiler_params=pltpu.CompilerParams(collective_id=1, has_side_effects=True),
        name="filter",
    )(block, coeff)


def dot(a, b):
    return jnp.dot(a, b, precision=HIGHEST, preferred_element_type=jnp.float32)


def dot_ta(a, b):
    return lax.dot_general(a, b, (((0,), (0,)), ((), ())), precision=HIGHEST, preferred_element_type=jnp.float32)


SWEEPS = 10
TARGET = 1e-6


def factor_kernel(scale, gram, inverse, triangle, misfit):
    g = gram[...]
    n = g.shape[0]
    row = lax.broadcasted_iota(jnp.int32, (n, n), 0)
    col = lax.broadcasted_iota(jnp.int32, (n, n), 1)
    diagonal = jnp.where(row == col, g, 0.0)
    d_col = lax.rsqrt(jnp.sum(diagonal, axis=1, keepdims=True))
    d_row = lax.rsqrt(jnp.sum(diagonal, axis=0, keepdims=True))
    unit = g * d_col * d_row
    one = jnp.where(row == col, 1.0, 0.0)
    weight = jnp.where(row < col, 1.0, jnp.where(row == col, 0.5, 0.0))

    def refined(state):
        s, _, count = state
        excess = dot_ta(s, dot(unit, s)) - one
        s = s - dot(s, excess * weight)
        return (s, jnp.sum(excess * excess), count + 1)

    start = one - (unit - one) * weight
    s, size, _ = lax.while_loop(
        lambda state: jnp.logical_and(state[1] > TARGET, state[2] < SWEEPS), refined, (start, jnp.float32(1.0), 0)
    )
    inverse[...] = d_col * s
    r = dot_ta(s, unit)
    triangle[...] = jnp.where(row <= col, r * (scale / d_row), 0.0)
    norm = jnp.sum(s * s)
    misfit[0, 0] = jnp.where(norm <= n + 50.0, size, 1.0)


def factored(gram, scale):
    n = gram.shape[0]
    return pl.pallas_call(
        functools.partial(factor_kernel, scale),
        out_shape=(
            jax.ShapeDtypeStruct((n, n), jnp.float32),
            jax.ShapeDtypeStruct((n, n), jnp.float32),
            jax.ShapeDtypeStruct((1, 1), jnp.float32),
        ),
        in_specs=[pl.BlockSpec(memory_space=pltpu.VMEM)],
        out_specs=(
            pl.BlockSpec(memory_space=pltpu.VMEM),
            pl.BlockSpec(memory_space=pltpu.VMEM),
            pl.BlockSpec(memory_space=pltpu.SMEM),
        ),
        name="factor",
    )(gram)


def elimination_kernel(gram, extra, inverse_t, triangle, a, w):
    n = gram.shape[0]
    row = lax.broadcasted_iota(jnp.int32, (n, n), 0)
    col = lax.broadcasted_iota(jnp.int32, (n, n), 1)
    g = gram[...]
    one = jnp.where(row == col, 1.0, 0.0)
    diagonal = jnp.where(row == col, g, 0.0)
    s_col = jnp.sum(diagonal, axis=1, keepdims=True)
    s_row = jnp.sum(diagonal, axis=0, keepdims=True)
    d_col = lax.rsqrt(jnp.where(s_col > 0, s_col, 1.0))
    d_row = lax.rsqrt(jnp.where(s_row > 0, s_row, 1.0))
    a[...] = g * d_col * d_row + extra[0, 0] * one
    w[...] = one

    @pl.loop(0, n)
    def _(k):
        pivot_row = a[pl.ds(k, 1), :]
        column = jnp.sum(jnp.where(col == k, a[...], 0.0), axis=1, keepdims=True)
        lane = lax.broadcasted_iota(jnp.int32, (1, n), 1)
        pivot = jnp.maximum(jnp.sum(jnp.where(lane == k, pivot_row, 0.0), axis=1, keepdims=True), 1e-12)
        below = lax.broadcasted_iota(jnp.int32, (n, 1), 0) > k
        ratio = jnp.where(below, column / pivot, 0.0)
        w_row = w[pl.ds(k, 1), :]
        a[...] = a[...] - ratio * pivot_row
        w[...] = w[...] - ratio * w_row

    u = a[...]
    pivots = jnp.maximum(jnp.sum(jnp.where(row == col, u, 0.0), axis=1, keepdims=True), 1e-12)
    root = lax.rsqrt(pivots)
    triangle[...] = jnp.where(row < col, u * root, jnp.where(row == col, pivots * root, 0.0)) / d_row
    inverse_t[...] = w[...] * root * d_row


def eliminated(gram, extra):
    n = gram.shape[0]
    return pl.pallas_call(
        elimination_kernel,
        out_shape=(jax.ShapeDtypeStruct((n, n), jnp.float32),) * 2,
        in_specs=[pl.BlockSpec(memory_space=pltpu.VMEM), pl.BlockSpec(memory_space=pltpu.SMEM)],
        out_specs=(pl.BlockSpec(memory_space=pltpu.VMEM),) * 2,
        scratch_shapes=[pltpu.VMEM((n, n), jnp.float32)] * 2,
        name="eliminate",
    )(gram, extra.reshape(1, 1))


def all_reduce_kernel(sizes, x, out, half, part, summed, full, core_in, x_in, y_in, z_in, send, core_sem, x_sem, y_sem, z_sem, back_sem, pair_sem):
    nz, ny, nx = sizes
    me = lax.axis_index("dev")
    core, at_x = me % 2, me // 2 % nx
    at_y, at_z = me // (2 * nx) % ny, me // (2 * nx * ny)
    partner = me + 1 - 2 * core
    along = lambda at, j, size, stride: ((at + j) % size, me + ((at + j) % size - at) * stride)
    x_peers = [along(at_x, j, nx, 2) for j in range(1, nx)]
    y_peers = [along(at_y, j, ny, 2 * nx) for j in range(1, ny)]
    z_peers = [along(at_z, j, nz, 2 * nx * ny) for j in range(1, nz)]

    barrier = pltpu.get_barrier_semaphore()
    others = [partner] + [peer for _, peer in x_peers + y_peers + z_peers]
    for peer in others:
        pl.semaphore_signal(barrier, inc=1, device_id=(peer,), device_id_type=MESH)
    pl.semaphore_wait(barrier, len(others))

    started = []

    def copy(src, dst, recv_sem, peer):
        transfer = pltpu.make_async_remote_copy(
            src_ref=src, dst_ref=dst, send_sem=send.at[len(started)], recv_sem=recv_sem, device_id=(peer,), device_id_type=MESH
        )
        transfer.start()
        started.append(transfer)

    def arrived(dst, recv_sem):
        pltpu.make_async_remote_copy(
            src_ref=dst, dst_ref=dst, send_sem=send.at[0], recv_sem=recv_sem, device_id=(partner,), device_id_type=MESH
        ).wait_recv()

    rows = x.shape[0] // 2
    piece = rows // nx
    copy(x.at[pl.ds((1 - core) * rows, rows)], core_in, core_sem, partner)
    arrived(core_in, core_sem)
    half[...] = x[pl.ds(core * rows, rows)] + core_in[...]

    for other, peer in x_peers:
        copy(half.at[pl.ds(other * piece, piece)], x_in.at[at_x], x_sem.at[at_x], peer)
    x_in[at_x] = half[pl.ds(at_x * piece, piece)]
    for other, peer in x_peers:
        arrived(x_in.at[other], x_sem.at[other])
    total = x_in[0]
    for i in range(1, nx):
        total = total + x_in[i]

    for stage, (peers, at, size, slots, sem) in enumerate(((y_peers, at_y, ny, y_in, y_sem), (z_peers, at_z, nz, z_in, z_sem))):
        part[stage] = total
        for other, peer in peers:
            copy(part.at[stage], slots.at[at], sem.at[at], peer)
        slots[at] = total
        for other, peer in peers:
            arrived(slots.at[other], sem.at[other])
        total = slots[0]
        for i in range(1, size):
            total = total + slots[i]

    summed[...] = total
    mine = core * rows + at_x * piece
    for other, peer in x_peers:
        copy(summed, full.at[pl.ds(mine, piece)], back_sem.at[at_x], peer)
    copy(summed, full.at[pl.ds(mine, piece)], pair_sem.at[at_x], partner)
    full[pl.ds(mine, piece)] = total
    for other, peer in x_peers:
        there = full.at[pl.ds(core * rows + other * piece, piece)]
        arrived(there, back_sem.at[other])
        copy(there, there, pair_sem.at[other], partner)
    for i in range(nx):
        arrived(full.at[pl.ds((1 - core) * rows + i * piece, piece)], pair_sem.at[i])
    out[...] = full[...]
    for transfer in started:
        transfer.wait_send()


def all_reduce(x, sizes=(4, 4, 4)):
    nz, ny, nx = sizes
    n, m = x.shape
    rows = n // 2
    piece = rows // nx
    copies = 1 + (nx - 1) + (ny - 1) + (nz - 1) + nx + (nx - 1)
    block = lambda *lead: pltpu.VMEM((*lead, m), jnp.float32)
    return pl.pallas_call(
        functools.partial(all_reduce_kernel, sizes),
        out_shape=jax.ShapeDtypeStruct(x.shape, jnp.float32),
        in_specs=[pl.BlockSpec(memory_space=pltpu.VMEM)],
        out_specs=pl.BlockSpec(memory_space=pltpu.VMEM),
        scratch_shapes=[
            block(rows), block(2, piece), block(piece), block(n), block(rows), block(nx, piece), block(ny, piece), block(nz, piece),
            pltpu.SemaphoreType.DMA((copies,)), pltpu.SemaphoreType.DMA, pltpu.SemaphoreType.DMA((nx,)), pltpu.SemaphoreType.DMA((ny,)),
            pltpu.SemaphoreType.DMA((nz,)), pltpu.SemaphoreType.DMA((nx,)), pltpu.SemaphoreType.DMA((nx,)),
        ],
        compiler_params=pltpu.CompilerParams(collective_id=0, has_side_effects=True),
        name="all_reduce",
    )(x)


def split(x):
    high = x.astype(jnp.bfloat16)
    return high, (x - high.astype(jnp.float32)).astype(jnp.bfloat16)


def gram_kernel(x_ref, out, cross):
    k = pl.program_id(0)

    @pl.when(k == 0)
    def _():
        out[...] = jnp.zeros_like(out)
        cross[...] = jnp.zeros_like(cross)

    high, low = split(x_ref[...].reshape(-1, x_ref.shape[-1]))
    product = lambda p, q: lax.dot_general(p, q, (((1,), (1,)), ((), ())), preferred_element_type=jnp.float32)
    out[...] += product(high, high)
    cross[...] += product(high, low)

    @pl.when(k == pl.num_programs(0) - 1)
    def _():
        out[...] += cross[...] + cross[...].T


def component_spec(x):
    return pl.BlockSpec((x.shape[0], 1, *x.shape[2:]), lambda k: (0, k, 0, 0))


def gram_of(x):
    n = x.shape[0] * x.shape[2]
    return pl.pallas_call(
        gram_kernel,
        out_shape=jax.ShapeDtypeStruct((n, n), jnp.float32),
        grid=(3,),
        in_specs=[component_spec(x)],
        out_specs=pl.BlockSpec((n, n), lambda k: (0, 0)),
        scratch_shapes=[pltpu.VMEM((n, n), jnp.float32)],
        name="gram",
    )(x)


def product_kernel(row_scale, x_ref, inverse, out, high_s, low_s):
    @pl.when(pl.program_id(0) == 0)
    def _():
        high_s[...], low_s[...] = split(inverse[...] * row_scale)

    high, low = split(x_ref[...].reshape(-1, x_ref.shape[-1]))
    product = lambda p, q: lax.dot_general(p, q, (((0,), (0,)), ((), ())), preferred_element_type=jnp.float32)
    out[0] = product(low, high_s[...]) + product(high, low_s[...]) + product(high, high_s[...])


def product_of(x, inverse, row_scale):
    n, nodes = x.shape[0] * x.shape[2], x.shape[3]
    return pl.pallas_call(
        functools.partial(product_kernel, row_scale),
        out_shape=jax.ShapeDtypeStruct((3, nodes, n), jnp.float32),
        grid=(3,),
        in_specs=[component_spec(x), pl.BlockSpec((n, n), lambda k: (0, 0))],
        out_specs=pl.BlockSpec((1, nodes, n), lambda k: (k, 0, 0)),
        scratch_shapes=[pltpu.VMEM((n, n), jnp.bfloat16)] * 2,
        name="product",
    )(x, inverse)


def local(start_block, modulus, occupancy):
    center, half_width = filter_bounds(element_matrix())
    coeff = (modulus * occupancy.astype(jnp.float32)).reshape(-1, TILE)
    modes = start_block.shape[4]
    flat = start_block.reshape(3, -1, modes)
    row_scale = math.sqrt(math.prod(flat.shape[:2]) * lax.axis_size("dev"))
    current = filtered(flat, coeff, center, half_width, start_block.shape[3])
    gram = all_reduce(gram_of(current))
    inverse, triangle, misfit = factored(gram, 1.0 / row_scale)

    def direct(x, gram, inverse, triangle):
        return product_of(x, inverse, row_scale), triangle

    def general(x, gram, inverse, triangle):
        def one_pass(i, state):
            x, total = state
            extra = jnp.where(i == 0, 3e-5, 0.0).astype(jnp.float32)
            inverse_t, r = eliminated(all_reduce(dot_ta(x, x)), extra)
            return (dot(x, inverse_t.T), dot(r, total))

        x, total = lax.fori_loop(0, 4, one_pass, (x.transpose(1, 3, 0, 2).reshape(-1, modes), jnp.eye(modes, dtype=jnp.float32)))
        return (x * row_scale).reshape(flat.shape), total / row_scale

    basis, triangle = lax.cond(misfit[0, 0] <= 1e-4, direct, general, current, gram, inverse, triangle)
    return basis.reshape(start_block.shape), triangle


def solution(mesh):
    return jax.shard_map(
        local,
        mesh=mesh,
        in_specs=(P(None, "dev", None, None, None), P("dev", None, None), P("dev", None, None)),
        out_specs=(P(None, "dev", None, None, None), P()),
        check_vma=False,
    )
```

```python
import functools
import math

import jax
import jax.numpy as jnp
import numpy as np
from jax import lax
from jax.experimental import pallas as pl
from jax.experimental.pallas import tpu as pltpu
from jax.sharding import PartitionSpec as P

DEGREE = 3
HIGHEST = lax.Precision.HIGHEST
MESH = pl.DeviceIdType.MESH


def element_matrix():
    poisson = 0.3
    lame_first = poisson / ((1.0 + poisson) * (1.0 - 2.0 * poisson))
    shear_modulus = 0.5 / (1.0 + poisson)
    elastic = np.zeros((6, 6))
    elastic[:3, :3] = lame_first
    for axis_number in range(3):
        elastic[axis_number, axis_number] += 2.0 * shear_modulus
        elastic[axis_number + 3, axis_number + 3] = shear_modulus
    points = [0.5 - 0.5 / np.sqrt(3.0), 0.5 + 0.5 / np.sqrt(3.0)]
    stiffness = np.zeros((24, 24))
    for point_x in points:
        for point_y in points:
            for point_z in points:
                gradients = np.zeros((3, 8))
                for corner in range(8):
                    offset_x, offset_y, offset_z = (corner % 2, corner // 2 % 2, corner // 4)
                    along_x = point_x if offset_x else 1.0 - point_x
                    along_y = point_y if offset_y else 1.0 - point_y
                    along_z = point_z if offset_z else 1.0 - point_z
                    gradients[0, corner] = (2 * offset_x - 1) * along_y * along_z
                    gradients[1, corner] = (2 * offset_y - 1) * along_x * along_z
                    gradients[2, corner] = (2 * offset_z - 1) * along_x * along_y
                strain_map = np.zeros((6, 24))
                strain_map[0, 0:8] = gradients[0]
                strain_map[1, 8:16] = gradients[1]
                strain_map[2, 16:24] = gradients[2]
                strain_map[3, 0:8] = gradients[1]
                strain_map[3, 8:16] = gradients[0]
                strain_map[4, 8:16] = gradients[2]
                strain_map[4, 16:24] = gradients[1]
                strain_map[5, 0:8] = gradients[2]
                strain_map[5, 16:24] = gradients[0]
                stiffness += strain_map.T @ elastic @ strain_map / 8.0
    return stiffness


def filter_bounds(stiffness):
    upper_end = 8.0 * float(np.max(np.sum(np.abs(stiffness), axis=1)))
    lower_end = 0.15 * upper_end
    return (0.5 * (upper_end + lower_end), 0.5 * (upper_end - lower_end))


LAME = 0.3 / (1.3 * 0.4)
SHEAR = 0.5 / 1.3


def element_forces(h, coeff, factor):
    g = {}

    def coupled(keys, own, shared):
        total = h[keys[0]]
        for key in keys[1:]:
            total = total + h[key]
        total = total * shared
        for key in keys:
            g[key] = total if own is None else own * h[key] + total

    scaled = lambda value: coeff * (value * factor)
    mu16, mu48 = scaled(SHEAR / 16), scaled(SHEAR / 48)
    coupled([(0, "dss"), (1, "sds"), (2, "ssd")], scaled(2 * SHEAR / 16), scaled(LAME / 16))
    own, shared = scaled(3 * SHEAR / 48), scaled(LAME / 48)
    coupled([(0, "dsd"), (1, "sdd")], own, shared)
    coupled([(0, "dds"), (2, "sdd")], own, shared)
    coupled([(1, "dds"), (2, "dsd")], own, shared)
    coupled([(0, "sdd"), (1, "dsd"), (2, "dds")], mu48, mu48)
    coupled([(0, "sds"), (1, "dss")], None, mu16)
    coupled([(0, "ssd"), (2, "dss")], None, mu16)
    coupled([(1, "ssd"), (2, "sds")], None, mu16)
    last = scaled((LAME + 4 * SHEAR) / 144)
    for k in range(3):
        g[(k, "ddd")] = last * h[(k, "ddd")]
    return g


PLANES = {}
for _k in range(3):
    for _a in "sd":
        for _b in "sd":
            PLANES[(_k, _a, _b)] = len(PLANES)

TILE = 128
GROUP = 8
ROW = 8
SPARE = ROW + 2
PAIR = 4


def filter_round(factor, shift, width, here, previous, out, coeff, planes, ahead, forces, upward):
    tiles = here.shape[3] // TILE
    lane = lax.broadcasted_iota(jnp.int32, (GROUP, TILE), 1)
    first_x, last_x = lane % width == 0, lane % width == width - 1
    low_rows, high_rows = lane < TILE - width, lane >= width
    tile = lambda t: pl.ds(t * TILE, TILE)

    def along_x(layer, t):
        q = {}
        for k in range(3):
            a = here[layer, k, :, tile(t)]
            b = jnp.where(last_x, 0.0, pltpu.roll(a, TILE - 1, 1))
            for name, value in (("s", a + b), ("d", b - a)):
                q[(k, name)] = (value, pltpu.roll(value, TILE - width, 1))
        return q

    def along_xy(layer):
        later = along_x(layer, 0)
        for t in range(tiles):
            now = later
            later = along_x(layer, t + 1) if t + 1 < tiles else None
            q = {}
            for key, (value, rolled) in now.items():
                after = jnp.where(low_rows, rolled, later[key][1] if later else 0.0)
                q[(*key, "s")] = value + after
                q[(*key, "d")] = after - value
            yield t, q

    def fill(into, layer):
        for t, q in along_xy(layer):
            for key, value in q.items():
                into[t, PLANES[key]] = value

    fill(planes, 0)
    fill(ahead, 1)

    @pl.loop(0, ROW + 1)
    def _(e):
        target = jnp.where(e == 0, SPARE, e)

        @pl.loop(0, tiles, step=PAIR)
        def _(first):
            for t in [first + i for i in range(PAIR)]:
                h = {}
                for key, place in PLANES.items():
                    near, far = planes[t, place], ahead[t, place]
                    name = key[1] + key[2]
                    h[(key[0], name + "s")] = near + far
                    h[(key[0], name + "d")] = far - near
                    planes[t, place] = far
                g = element_forces(h, jnp.broadcast_to(coeff[e, pl.ds(t, 1), :], (GROUP, TILE)), factor)
                for key, place in PLANES.items():
                    name = key[1] + key[2]
                    even, odd = g.get((key[0], name + "s")), g[(key[0], name + "d")]
                    forces[t, place] = upward[t, place] + (-odd if even is None else even - odd)
                    upward[t, place] = odd if even is None else even + odd

        fill(ahead, jnp.minimum(e + 2, ROW + 1))
        behind = {}
        for t in range(tiles):
            for k in range(3):
                part = {}
                for a in "sd":
                    up, down = forces[t, PLANES[(k, a, "s")]], forces[t, PLANES[(k, a, "d")]]
                    rolled = pltpu.roll(up + down, width, 1)
                    part[a] = (up - down) + jnp.where(high_rows, rolled, behind.get((k, a), 0.0))
                    behind[(k, a)] = rolled
                moved = jnp.where(first_x, 0.0, pltpu.roll(part["s"] + part["d"], 1, 1))
                where = (k, slice(None), tile(t))
                value = (part["s"] - part["d"]) + moved - shift * here[(e, *where)]
                if previous is not None:
                    value = value - previous[(e, *where)]
                out[(target, *where)] = value


ORDER = (
    ("in", 0), (0, 0), ("in", 1), (1, 0), (0, 1), ("in", 2), (2, 0), (1, 1),
    (0, 2), ("in", 3), (2, 1), (1, 2), (0, 3), (2, 2), (1, 3), (2, 3),
)


def filter_kernel(
    devices, center, half_width, width, x, coeff_mine, home, turned, state_0, state_1, state_2, state_3, coeff, planes, ahead, forces, upward,
    in_send, in_recv, halo_send, halo_recv, out_send, out_recv, coeff_send, coeff_recv, edge_send, edge_recv,
):
    me = lax.axis_index("dev")
    place, row = me % ROW, me // ROW
    base = me - place
    has_below, has_above = row > 0, row < devices // ROW - 1
    groups = turned.shape[0] // ROW
    state = [state_0, state_1, state_2, state_3]
    nodes = x.shape[1]
    mates = []
    for side in (0, 1):
        for step in (1, 3, 2) if side == 0 else (1, 3, 2, 0):
            chip, core = (place // 2 + step) % (ROW // 2), (place % 2 + side) % 2
            mates.append(2 * chip + core)
    barrier = pltpu.get_barrier_semaphore()
    for mate in mates:
        pl.semaphore_signal(barrier, inc=1, device_id=(base + mate,), device_id_type=MESH)
    for present, peer in ((has_below, me - ROW), (has_above, me + ROW)):

        @pl.when(present)
        def _():
            pl.semaphore_signal(barrier, inc=1, device_id=(peer,), device_id_type=MESH)

    @pl.loop(0, 3 * (nodes // TILE))
    def _(i):
        k, t = i // (nodes // TILE), i % (nodes // TILE)
        lanes = pl.ds(pl.multiple_of(t * TILE, TILE), TILE)
        for c in range(x.shape[2] // TILE):
            block = x[k, lanes, pl.ds(c * TILE, TILE)].T
            for g in range(TILE // GROUP):
                turned[c * (TILE // GROUP) + g, k, :, lanes] = block[g * GROUP : (g + 1) * GROUP]

    coeff[1 + place] = coeff_mine[...]

    def remote(src, dst, send_sem, recv_sem, peer):
        return pltpu.make_async_remote_copy(
            src_ref=src, dst_ref=dst, send_sem=send_sem, recv_sem=recv_sem, device_id=(peer,), device_id_type=MESH
        )

    def coeff_copy(mate):
        return remote(coeff_mine, coeff.at[1 + place], coeff_send.at[mate], coeff_recv.at[place], base + mate)

    def in_copy(q, mate):
        return remote(
            turned.at[groups * mate + q], state[0].at[q, 1 + place], in_send.at[q, mate], in_recv.at[q, place], base + mate
        )

    def out_copy(q, mate):
        return remote(state[3].at[q, 1 + mate], home.at[groups * place + q], out_send.at[q, mate], out_recv.at[q, place], base + mate)

    def halo_copy(s, q, way):
        source, target, peer = ((ROW, 0, me + ROW), (1, ROW + 1, me - ROW))[way]
        return remote(state[s].at[q, source], state[s].at[q, target], halo_send.at[s, q, way], halo_recv.at[s, q, way], peer)

    def edge_copy():
        return remote(coeff.at[ROW], coeff.at[0], edge_send, edge_recv, me + ROW)

    def arrived(dst, recv_sem):
        remote(dst, dst, edge_send, recv_sem, base + mates[0]).wait_recv()

    pl.semaphore_wait(barrier, len(mates) + has_below.astype(jnp.int32) + has_above.astype(jnp.int32))
    for mate in mates:
        coeff_copy(mate).start()

    @pl.loop(0, groups)
    def _(q):
        for mate in mates:
            in_copy(q, mate).start()

    @pl.loop(0, groups)
    def _(q):
        state[0][q, 1 + place] = turned[groups * place + q]

    upward[...] = jnp.zeros_like(upward)

    @pl.when(jnp.logical_not(has_below))
    def _():
        coeff[0] = jnp.zeros(coeff.shape[1:], jnp.float32)

    for present, layer in ((has_below, 0), (has_above, ROW + 1)):

        @pl.when(jnp.logical_not(present))
        def _():
            @pl.loop(0, groups)
            def _(q):
                for s in range(3):
                    state[s][q, layer] = jnp.zeros(state[s].shape[2:], jnp.float32)

    for mate in mates:
        arrived(coeff.at[1 + mate], coeff_recv.at[mate])

    @pl.when(has_above)
    def _():
        edge_copy().start()

    @pl.when(has_below)
    def _():
        arrived(coeff.at[0], edge_recv)

    def send_halo(s, q):
        for present, way in ((has_above, 0), (has_below, 1)):

            @pl.when(present)
            def _():
                halo_copy(s, q, way).start()

    for s, q in ORDER:
        if s == "in":
            for mate in mates:
                arrived(state[0].at[q, 1 + mate], in_recv.at[q, mate])
            send_halo(0, q)
            continue
        for present, way, layer in ((has_below, 0, 0), (has_above, 1, ROW + 1)):

            @pl.when(present)
            def _():
                arrived(state[s].at[q, layer], halo_recv.at[s, q, way])

        factor = (1.0 if s == 0 else 2.0) / half_width
        previous = state[s - 1].at[q] if s else None
        filter_round(factor, factor * center, width, state[s].at[q], previous, state[s + 1].at[q], coeff, planes, ahead, forces, upward)
        if s < 2:
            send_halo(s + 1, q)
        else:
            for mate in mates:
                out_copy(q, mate).start()
            home[groups * place + q] = state[3][q, 1 + place]

    @pl.loop(0, groups)
    def _(q):
        for mate in mates:
            arrived(home.at[groups * mate + q], out_recv.at[q, mate])
            in_copy(q, mate).wait_send()
            out_copy(q, mate).wait_send()
        for s in range(3):
            for present, way in ((has_above, 0), (has_below, 1)):

                @pl.when(present)
                def _():
                    halo_copy(s, q, way).wait_send()

    for mate in mates:
        coeff_copy(mate).wait_send()

    @pl.when(has_above)
    def _():
        edge_copy().wait_send()


def filtered(block, coeff, center, half_width, width):
    _, nodes, modes = block.shape
    groups, tiles = modes // GROUP // ROW, nodes // TILE
    vmem = lambda *shape: pltpu.VMEM(shape, jnp.float32)
    dma = pltpu.SemaphoreType.DMA
    return pl.pallas_call(
        functools.partial(filter_kernel, lax.axis_size("dev"), center, half_width, width),
        out_shape=jax.ShapeDtypeStruct((modes // GROUP, 3, GROUP, nodes), jnp.float32),
        in_specs=[pl.BlockSpec(memory_space=pltpu.VMEM)] * 2,
        out_specs=pl.BlockSpec(memory_space=pltpu.VMEM),
        scratch_shapes=[
            vmem(modes // GROUP, 3, GROUP, nodes), *[vmem(groups, SPARE + 1, 3, GROUP, nodes)] * 4, vmem(ROW + 1, tiles, TILE),
            *[vmem(tiles, 12, GROUP, TILE)] * 4,
            dma((groups, ROW)), dma((groups, ROW)), dma((3, groups, 2)), dma((3, groups, 2)), dma((groups, ROW)), dma((groups, ROW)),
            dma((ROW,)), dma((ROW,)), dma, dma,
        ],
        compiler_params=pltpu.CompilerParams(collective_id=1, has_side_effects=True),
        name="filter",
    )(block, coeff)


def dot(a, b):
    return jnp.dot(a, b, precision=HIGHEST, preferred_element_type=jnp.float32)


def dot_ta(a, b):
    return lax.dot_general(a, b, (((0,), (0,)), ((), ())), precision=HIGHEST, preferred_element_type=jnp.float32)


SWEEPS = 10
TARGET = 1e-6


def factor_kernel(scale, gram, inverse, triangle, misfit):
    g = gram[...]
    n = g.shape[0]
    row = lax.broadcasted_iota(jnp.int32, (n, n), 0)
    col = lax.broadcasted_iota(jnp.int32, (n, n), 1)
    diagonal = jnp.where(row == col, g, 0.0)
    d_col = lax.rsqrt(jnp.sum(diagonal, axis=1, keepdims=True))
    d_row = lax.rsqrt(jnp.sum(diagonal, axis=0, keepdims=True))
    unit = g * d_col * d_row
    one = jnp.where(row == col, 1.0, 0.0)
    weight = jnp.where(row < col, 1.0, jnp.where(row == col, 0.5, 0.0))

    def refined(state):
        s, _, count = state
        excess = dot_ta(s, dot(unit, s)) - one
        s = s - dot(s, excess * weight)
        return (s, jnp.sum(excess * excess), count + 1)

    start = one - (unit - one) * weight
    s, size, _ = lax.while_loop(
        lambda state: jnp.logical_and(state[1] > TARGET, state[2] < SWEEPS), refined, (start, jnp.float32(1.0), 0)
    )
    inverse[...] = d_col * s
    r = dot_ta(s, unit)
    triangle[...] = jnp.where(row <= col, r * (scale / d_row), 0.0)
    norm = jnp.sum(s * s)
    misfit[0, 0] = jnp.where(norm <= n + 50.0, size, 1.0)


def factored(gram, scale):
    n = gram.shape[0]
    return pl.pallas_call(
        functools.partial(factor_kernel, scale),
        out_shape=(
            jax.ShapeDtypeStruct((n, n), jnp.float32),
            jax.ShapeDtypeStruct((n, n), jnp.float32),
            jax.ShapeDtypeStruct((1, 1), jnp.float32),
        ),
        in_specs=[pl.BlockSpec(memory_space=pltpu.VMEM)],
        out_specs=(
            pl.BlockSpec(memory_space=pltpu.VMEM),
            pl.BlockSpec(memory_space=pltpu.VMEM),
            pl.BlockSpec(memory_space=pltpu.SMEM),
        ),
        name="factor",
    )(gram)


def elimination_kernel(gram, extra, inverse_t, triangle, a, w):
    n = gram.shape[0]
    row = lax.broadcasted_iota(jnp.int32, (n, n), 0)
    col = lax.broadcasted_iota(jnp.int32, (n, n), 1)
    g = gram[...]
    one = jnp.where(row == col, 1.0, 0.0)
    diagonal = jnp.where(row == col, g, 0.0)
    s_col = jnp.sum(diagonal, axis=1, keepdims=True)
    s_row = jnp.sum(diagonal, axis=0, keepdims=True)
    d_col = lax.rsqrt(jnp.where(s_col > 0, s_col, 1.0))
    d_row = lax.rsqrt(jnp.where(s_row > 0, s_row, 1.0))
    a[...] = g * d_col * d_row + extra[0, 0] * one
    w[...] = one

    @pl.loop(0, n)
    def _(k):
        pivot_row = a[pl.ds(k, 1), :]
        column = jnp.sum(jnp.where(col == k, a[...], 0.0), axis=1, keepdims=True)
        lane = lax.broadcasted_iota(jnp.int32, (1, n), 1)
        pivot = jnp.maximum(jnp.sum(jnp.where(lane == k, pivot_row, 0.0), axis=1, keepdims=True), 1e-12)
        below = lax.broadcasted_iota(jnp.int32, (n, 1), 0) > k
        ratio = jnp.where(below, column / pivot, 0.0)
        w_row = w[pl.ds(k, 1), :]
        a[...] = a[...] - ratio * pivot_row
        w[...] = w[...] - ratio * w_row

    u = a[...]
    pivots = jnp.maximum(jnp.sum(jnp.where(row == col, u, 0.0), axis=1, keepdims=True), 1e-12)
    root = lax.rsqrt(pivots)
    triangle[...] = jnp.where(row < col, u * root, jnp.where(row == col, pivots * root, 0.0)) / d_row
    inverse_t[...] = w[...] * root * d_row


def eliminated(gram, extra):
    n = gram.shape[0]
    return pl.pallas_call(
        elimination_kernel,
        out_shape=(jax.ShapeDtypeStruct((n, n), jnp.float32),) * 2,
        in_specs=[pl.BlockSpec(memory_space=pltpu.VMEM), pl.BlockSpec(memory_space=pltpu.SMEM)],
        out_specs=(pl.BlockSpec(memory_space=pltpu.VMEM),) * 2,
        scratch_shapes=[pltpu.VMEM((n, n), jnp.float32)] * 2,
        name="eliminate",
    )(gram, extra.reshape(1, 1))


def all_reduce_kernel(sizes, x, out, half, part, summed, full, core_in, x_in, y_in, z_in, send, core_sem, x_sem, y_sem, z_sem, back_sem, pair_sem):
    nz, ny, nx = sizes
    me = lax.axis_index("dev")
    core, at_x = me % 2, me // 2 % nx
    at_y, at_z = me // (2 * nx) % ny, me // (2 * nx * ny)
    partner = me + 1 - 2 * core
    along = lambda at, j, size, stride: ((at + j) % size, me + ((at + j) % size - at) * stride)
    x_peers = [along(at_x, j, nx, 2) for j in range(1, nx)]
    y_peers = [along(at_y, j, ny, 2 * nx) for j in range(1, ny)]
    z_peers = [along(at_z, j, nz, 2 * nx * ny) for j in range(1, nz)]

    barrier = pltpu.get_barrier_semaphore()
    others = [partner] + [peer for _, peer in x_peers + y_peers + z_peers]
    for peer in others:
        pl.semaphore_signal(barrier, inc=1, device_id=(peer,), device_id_type=MESH)
    pl.semaphore_wait(barrier, len(others))

    started = []

    def copy(src, dst, recv_sem, peer):
        transfer = pltpu.make_async_remote_copy(
            src_ref=src, dst_ref=dst, send_sem=send.at[len(started)], recv_sem=recv_sem, device_id=(peer,), device_id_type=MESH
        )
        transfer.start()
        started.append(transfer)

    def arrived(dst, recv_sem):
        pltpu.make_async_remote_copy(
            src_ref=dst, dst_ref=dst, send_sem=send.at[0], recv_sem=recv_sem, device_id=(partner,), device_id_type=MESH
        ).wait_recv()

    rows = x.shape[0] // 2
    piece = rows // nx
    copy(x.at[pl.ds((1 - core) * rows, rows)], core_in, core_sem, partner)
    arrived(core_in, core_sem)
    half[...] = x[pl.ds(core * rows, rows)] + core_in[...]

    for other, peer in x_peers:
        copy(half.at[pl.ds(other * piece, piece)], x_in.at[at_x], x_sem.at[at_x], peer)
    x_in[at_x] = half[pl.ds(at_x * piece, piece)]
    for other, peer in x_peers:
        arrived(x_in.at[other], x_sem.at[other])
    total = x_in[0]
    for i in range(1, nx):
        total = total + x_in[i]

    for stage, (peers, at, size, slots, sem) in enumerate(((y_peers, at_y, ny, y_in, y_sem), (z_peers, at_z, nz, z_in, z_sem))):
        part[stage] = total
        for other, peer in peers:
            copy(part.at[stage], slots.at[at], sem.at[at], peer)
        slots[at] = total
        for other, peer in peers:
            arrived(slots.at[other], sem.at[other])
        total = slots[0]
        for i in range(1, size):
            total = total + slots[i]

    summed[...] = total
    mine = core * rows + at_x * piece
    for other, peer in x_peers:
        copy(summed, full.at[pl.ds(mine, piece)], back_sem.at[at_x], peer)
    copy(summed, full.at[pl.ds(mine, piece)], pair_sem.at[at_x], partner)
    full[pl.ds(mine, piece)] = total
    for other, peer in x_peers:
        there = full.at[pl.ds(core * rows + other * piece, piece)]
        arrived(there, back_sem.at[other])
        copy(there, there, pair_sem.at[other], partner)
    for i in range(nx):
        arrived(full.at[pl.ds((1 - core) * rows + i * piece, piece)], pair_sem.at[i])
    out[...] = full[...]
    for transfer in started:
        transfer.wait_send()


def all_reduce(x, sizes=(4, 4, 4)):
    nz, ny, nx = sizes
    n, m = x.shape
    rows = n // 2
    piece = rows // nx
    copies = 1 + (nx - 1) + (ny - 1) + (nz - 1) + nx + (nx - 1)
    block = lambda *lead: pltpu.VMEM((*lead, m), jnp.float32)
    return pl.pallas_call(
        functools.partial(all_reduce_kernel, sizes),
        out_shape=jax.ShapeDtypeStruct(x.shape, jnp.float32),
        in_specs=[pl.BlockSpec(memory_space=pltpu.VMEM)],
        out_specs=pl.BlockSpec(memory_space=pltpu.VMEM),
        scratch_shapes=[
            block(rows), block(2, piece), block(piece), block(n), block(rows), block(nx, piece), block(ny, piece), block(nz, piece),
            pltpu.SemaphoreType.DMA((copies,)), pltpu.SemaphoreType.DMA, pltpu.SemaphoreType.DMA((nx,)), pltpu.SemaphoreType.DMA((ny,)),
            pltpu.SemaphoreType.DMA((nz,)), pltpu.SemaphoreType.DMA((nx,)), pltpu.SemaphoreType.DMA((nx,)),
        ],
        compiler_params=pltpu.CompilerParams(collective_id=0, has_side_effects=True),
        name="all_reduce",
    )(x)


def split(x):
    high = x.astype(jnp.bfloat16)
    return high, (x - high.astype(jnp.float32)).astype(jnp.bfloat16)


def gram_kernel(x_ref, out, cross):
    k = pl.program_id(0)

    @pl.when(k == 0)
    def _():
        out[...] = jnp.zeros_like(out)
        cross[...] = jnp.zeros_like(cross)

    high, low = split(x_ref[...].reshape(-1, x_ref.shape[-1]))
    product = lambda p, q: lax.dot_general(p, q, (((1,), (1,)), ((), ())), preferred_element_type=jnp.float32)
    out[...] += product(high, high)
    cross[...] += product(high, low)

    @pl.when(k == pl.num_programs(0) - 1)
    def _():
        out[...] += cross[...] + cross[...].T


def component_spec(x):
    return pl.BlockSpec((x.shape[0], 1, *x.shape[2:]), lambda k: (0, k, 0, 0))


def gram_of(x):
    n = x.shape[0] * x.shape[2]
    return pl.pallas_call(
        gram_kernel,
        out_shape=jax.ShapeDtypeStruct((n, n), jnp.float32),
        grid=(3,),
        in_specs=[component_spec(x)],
        out_specs=pl.BlockSpec((n, n), lambda k: (0, 0)),
        scratch_shapes=[pltpu.VMEM((n, n), jnp.float32)],
        name="gram",
    )(x)


def product_kernel(row_scale, x_ref, inverse, out, high_s, low_s):
    @pl.when(pl.program_id(0) == 0)
    def _():
        high_s[...], low_s[...] = split(inverse[...] * row_scale)

    high, low = split(x_ref[...].reshape(-1, x_ref.shape[-1]))
    product = lambda p, q: lax.dot_general(p, q, (((0,), (0,)), ((), ())), preferred_element_type=jnp.float32)
    out[0] = product(low, high_s[...]) + product(high, low_s[...]) + product(high, high_s[...])


def product_of(x, inverse, row_scale):
    n, nodes = x.shape[0] * x.shape[2], x.shape[3]
    return pl.pallas_call(
        functools.partial(product_kernel, row_scale),
        out_shape=jax.ShapeDtypeStruct((3, nodes, n), jnp.float32),
        grid=(3,),
        in_specs=[component_spec(x), pl.BlockSpec((n, n), lambda k: (0, 0))],
        out_specs=pl.BlockSpec((1, nodes, n), lambda k: (k, 0, 0)),
        scratch_shapes=[pltpu.VMEM((n, n), jnp.bfloat16)] * 2,
        name="product",
    )(x, inverse)


def local(start_block, modulus, occupancy):
    center, half_width = filter_bounds(element_matrix())
    coeff = (modulus * occupancy.astype(jnp.float32)).reshape(-1, TILE)
    modes = start_block.shape[4]
    flat = start_block.reshape(3, -1, modes)
    row_scale = math.sqrt(math.prod(flat.shape[:2]) * lax.axis_size("dev"))
    current = filtered(flat, coeff, center, half_width, start_block.shape[3])
    gram = all_reduce(gram_of(current))
    inverse, triangle, misfit = factored(gram, 1.0 / row_scale)

    def direct(x, gram, inverse, triangle):
        return product_of(x, inverse, row_scale), triangle

    def general(x, gram, inverse, triangle):
        def one_pass(i, state):
            x, total = state
            extra = jnp.where(i == 0, 3e-5, 0.0).astype(jnp.float32)
            inverse_t, r = eliminated(all_reduce(dot_ta(x, x)), extra)
            return (dot(x, inverse_t.T), dot(r, total))

        x, total = lax.fori_loop(0, 4, one_pass, (x.transpose(1, 3, 0, 2).reshape(-1, modes), jnp.eye(modes, dtype=jnp.float32)))
        return (x * row_scale).reshape(flat.shape), total / row_scale

    basis, triangle = lax.cond(misfit[0, 0] <= 1e-4, direct, general, current, gram, inverse, triangle)
    return basis.reshape(start_block.shape), triangle


def solution(mesh):
    return jax.shard_map(
        local,
        mesh=mesh,
        in_specs=(P(None, "dev", None, None, None), P("dev", None, None), P("dev", None, None)),
        out_specs=(P(None, "dev", None, None, None), P()),
        check_vma=False,
    )
```

```python
import functools
import math

import jax
import jax.numpy as jnp
import numpy as np
from jax import lax
from jax.experimental import pallas as pl
from jax.experimental.pallas import tpu as pltpu
from jax.sharding import PartitionSpec as P

DEGREE = 3
HIGHEST = lax.Precision.HIGHEST
MESH = pl.DeviceIdType.MESH


def element_matrix():
    poisson = 0.3
    lame_first = poisson / ((1.0 + poisson) * (1.0 - 2.0 * poisson))
    shear_modulus = 0.5 / (1.0 + poisson)
    elastic = np.zeros((6, 6))
    elastic[:3, :3] = lame_first
    for axis_number in range(3):
        elastic[axis_number, axis_number] += 2.0 * shear_modulus
        elastic[axis_number + 3, axis_number + 3] = shear_modulus
    points = [0.5 - 0.5 / np.sqrt(3.0), 0.5 + 0.5 / np.sqrt(3.0)]
    stiffness = np.zeros((24, 24))
    for point_x in points:
        for point_y in points:
            for point_z in points:
                gradients = np.zeros((3, 8))
                for corner in range(8):
                    offset_x, offset_y, offset_z = (corner % 2, corner // 2 % 2, corner // 4)
                    along_x = point_x if offset_x else 1.0 - point_x
                    along_y = point_y if offset_y else 1.0 - point_y
                    along_z = point_z if offset_z else 1.0 - point_z
                    gradients[0, corner] = (2 * offset_x - 1) * along_y * along_z
                    gradients[1, corner] = (2 * offset_y - 1) * along_x * along_z
                    gradients[2, corner] = (2 * offset_z - 1) * along_x * along_y
                strain_map = np.zeros((6, 24))
                strain_map[0, 0:8] = gradients[0]
                strain_map[1, 8:16] = gradients[1]
                strain_map[2, 16:24] = gradients[2]
                strain_map[3, 0:8] = gradients[1]
                strain_map[3, 8:16] = gradients[0]
                strain_map[4, 8:16] = gradients[2]
                strain_map[4, 16:24] = gradients[1]
                strain_map[5, 0:8] = gradients[2]
                strain_map[5, 16:24] = gradients[0]
                stiffness += strain_map.T @ elastic @ strain_map / 8.0
    return stiffness


def filter_bounds(stiffness):
    upper_end = 8.0 * float(np.max(np.sum(np.abs(stiffness), axis=1)))
    lower_end = 0.15 * upper_end
    return (0.5 * (upper_end + lower_end), 0.5 * (upper_end - lower_end))


LAME = 0.3 / (1.3 * 0.4)
SHEAR = 0.5 / 1.3


def element_forces(h, coeff, factor):
    g = {}

    def coupled(keys, own, shared):
        total = h[keys[0]]
        for key in keys[1:]:
            total = total + h[key]
        total = total * shared
        for key in keys:
            g[key] = total if own is None else own * h[key] + total

    scaled = lambda value: coeff * (value * factor)
    mu16, mu48 = scaled(SHEAR / 16), scaled(SHEAR / 48)
    coupled([(0, "dss"), (1, "sds"), (2, "ssd")], scaled(2 * SHEAR / 16), scaled(LAME / 16))
    own, shared = scaled(3 * SHEAR / 48), scaled(LAME / 48)
    coupled([(0, "dsd"), (1, "sdd")], own, shared)
    coupled([(0, "dds"), (2, "sdd")], own, shared)
    coupled([(1, "dds"), (2, "dsd")], own, shared)
    coupled([(0, "sdd"), (1, "dsd"), (2, "dds")], mu48, mu48)
    coupled([(0, "sds"), (1, "dss")], None, mu16)
    coupled([(0, "ssd"), (2, "dss")], None, mu16)
    coupled([(1, "ssd"), (2, "sds")], None, mu16)
    last = scaled((LAME + 4 * SHEAR) / 144)
    for k in range(3):
        g[(k, "ddd")] = last * h[(k, "ddd")]
    return g


PLANES = {}
for _k in range(3):
    for _a in "sd":
        for _b in "sd":
            PLANES[(_k, _a, _b)] = len(PLANES)

TILE = 128
GROUP = 8
ROW = 8
SPARE = ROW + 2
PAIR = 4


def filter_round(factor, shift, width, here, previous, out, coeff, planes, ahead, forces, upward):
    tiles = here.shape[3] // TILE
    lane = lax.broadcasted_iota(jnp.int32, (GROUP, TILE), 1)
    first_x, last_x = lane % width == 0, lane % width == width - 1
    low_rows, high_rows = lane < TILE - width, lane >= width
    tile = lambda t: pl.ds(t * TILE, TILE)

    def along_x(layer, t):
        q = {}
        for k in range(3):
            a = here[layer, k, :, tile(t)]
            b = jnp.where(last_x, 0.0, pltpu.roll(a, TILE - 1, 1))
            for name, value in (("s", a + b), ("d", b - a)):
                q[(k, name)] = (value, pltpu.roll(value, TILE - width, 1))
        return q

    def along_xy(layer):
        later = along_x(layer, 0)
        for t in range(tiles):
            now = later
            later = along_x(layer, t + 1) if t + 1 < tiles else None
            q = {}
            for key, (value, rolled) in now.items():
                after = jnp.where(low_rows, rolled, later[key][1] if later else 0.0)
                q[(*key, "s")] = value + after
                q[(*key, "d")] = after - value
            yield t, q

    def fill(into, layer):
        for t, q in along_xy(layer):
            for key, value in q.items():
                into[t, PLANES[key]] = value

    fill(planes, 0)
    fill(ahead, 1)

    @pl.loop(0, ROW + 1)
    def _(e):
        target = jnp.where(e == 0, SPARE, e)

        @pl.loop(0, tiles, step=PAIR)
        def _(first):
            for t in [first + i for i in range(PAIR)]:
                h = {}
                for key, place in PLANES.items():
                    near, far = planes[t, place], ahead[t, place]
                    name = key[1] + key[2]
                    h[(key[0], name + "s")] = near + far
                    h[(key[0], name + "d")] = far - near
                    planes[t, place] = far
                g = element_forces(h, jnp.broadcast_to(coeff[e, pl.ds(t, 1), :], (GROUP, TILE)), factor)
                for key, place in PLANES.items():
                    name = key[1] + key[2]
                    even, odd = g.get((key[0], name + "s")), g[(key[0], name + "d")]
                    forces[t, place] = upward[t, place] + (-odd if even is None else even - odd)
                    upward[t, place] = odd if even is None else even + odd

        fill(ahead, jnp.minimum(e + 2, ROW + 1))
        behind = {}
        for t in range(tiles):
            for k in range(3):
                part = {}
                for a in "sd":
                    up, down = forces[t, PLANES[(k, a, "s")]], forces[t, PLANES[(k, a, "d")]]
                    rolled = pltpu.roll(up + down, width, 1)
                    part[a] = (up - down) + jnp.where(high_rows, rolled, behind.get((k, a), 0.0))
                    behind[(k, a)] = rolled
                moved = jnp.where(first_x, 0.0, pltpu.roll(part["s"] + part["d"], 1, 1))
                where = (k, slice(None), tile(t))
                value = (part["s"] - part["d"]) + moved - shift * here[(e, *where)]
                if previous is not None:
                    value = value - previous[(e, *where)]
                out[(target, *where)] = value


ORDER = (
    ("in", 0), (0, 0), ("in", 1), (1, 0), (0, 1), ("in", 2), (2, 0), (1, 1),
    (0, 2), ("in", 3), (2, 1), (1, 2), (0, 3), (2, 2), (1, 3), (2, 3),
)


def filter_kernel(
    devices, center, half_width, width, x, coeff_mine, home, turned, state_0, state_1, state_2, state_3, coeff, planes, ahead, forces, upward,
    in_send, in_recv, halo_send, halo_recv, out_send, out_recv, coeff_send, coeff_recv, edge_send, edge_recv,
):
    me = lax.axis_index("dev")
    place, row = me % ROW, me // ROW
    base = me - place
    has_below, has_above = row > 0, row < devices // ROW - 1
    groups = turned.shape[0] // ROW
    state = [state_0, state_1, state_2, state_3]
    nodes = x.shape[1]
    mates = []
    for side in (0, 1):
        for step in (1, 3, 2) if side == 0 else (1, 3, 2, 0):
            chip, core = (place // 2 + step) % (ROW // 2), (place % 2 + side) % 2
            mates.append(2 * chip + core)
    barrier = pltpu.get_barrier_semaphore()
    for mate in mates:
        pl.semaphore_signal(barrier, inc=1, device_id=(base + mate,), device_id_type=MESH)
    for present, peer in ((has_below, me - ROW), (has_above, me + ROW)):

        @pl.when(present)
        def _():
            pl.semaphore_signal(barrier, inc=1, device_id=(peer,), device_id_type=MESH)

    @pl.loop(0, 3 * (nodes // TILE))
    def _(i):
        k, t = i // (nodes // TILE), i % (nodes // TILE)
        lanes = pl.ds(pl.multiple_of(t * TILE, TILE), TILE)
        for c in range(x.shape[2] // TILE):
            block = x[k, lanes, pl.ds(c * TILE, TILE)].T
            for g in range(TILE // GROUP):
                turned[c * (TILE // GROUP) + g, k, :, lanes] = block[g * GROUP : (g + 1) * GROUP]

    coeff[1 + place] = coeff_mine[...]

    def remote(src, dst, send_sem, recv_sem, peer):
        return pltpu.make_async_remote_copy(
            src_ref=src, dst_ref=dst, send_sem=send_sem, recv_sem=recv_sem, device_id=(peer,), device_id_type=MESH
        )

    def coeff_copy(mate):
        return remote(coeff_mine, coeff.at[1 + place], coeff_send.at[mate], coeff_recv.at[place], base + mate)

    def in_copy(q, mate):
        return remote(
            turned.at[groups * mate + q], state[0].at[q, 1 + place], in_send.at[q, mate], in_recv.at[q, place], base + mate
        )

    def out_copy(q, mate):
        return remote(state[3].at[q, 1 + mate], home.at[groups * place + q], out_send.at[q, mate], out_recv.at[q, place], base + mate)

    def halo_copy(s, q, way):
        source, target, peer = ((ROW, 0, me + ROW), (1, ROW + 1, me - ROW))[way]
        return remote(state[s].at[q, source], state[s].at[q, target], halo_send.at[s, q, way], halo_recv.at[s, q, way], peer)

    def edge_copy():
        return remote(coeff.at[ROW], coeff.at[0], edge_send, edge_recv, me + ROW)

    def arrived(dst, recv_sem):
        remote(dst, dst, edge_send, recv_sem, base + mates[0]).wait_recv()

    pl.semaphore_wait(barrier, len(mates) + has_below.astype(jnp.int32) + has_above.astype(jnp.int32))
    for mate in mates:
        coeff_copy(mate).start()

    @pl.loop(0, groups)
    def _(q):
        for mate in mates:
            in_copy(q, mate).start()

    @pl.loop(0, groups)
    def _(q):
        state[0][q, 1 + place] = turned[groups * place + q]

    upward[...] = jnp.zeros_like(upward)

    @pl.when(jnp.logical_not(has_below))
    def _():
        coeff[0] = jnp.zeros(coeff.shape[1:], jnp.float32)

    for present, layer in ((has_below, 0), (has_above, ROW + 1)):

        @pl.when(jnp.logical_not(present))
        def _():
            @pl.loop(0, groups)
            def _(q):
                for s in range(3):
                    state[s][q, layer] = jnp.zeros(state[s].shape[2:], jnp.float32)

    for mate in mates:
        arrived(coeff.at[1 + mate], coeff_recv.at[mate])

    @pl.when(has_above)
    def _():
        edge_copy().start()

    @pl.when(has_below)
    def _():
        arrived(coeff.at[0], edge_recv)

    def send_halo(s, q):
        for present, way in ((has_above, 0), (has_below, 1)):

            @pl.when(present)
            def _():
                halo_copy(s, q, way).start()

    for s, q in ORDER:
        if s == "in":
            for mate in mates:
                arrived(state[0].at[q, 1 + mate], in_recv.at[q, mate])
            send_halo(0, q)
            continue
        for present, way, layer in ((has_below, 0, 0), (has_above, 1, ROW + 1)):

            @pl.when(present)
            def _():
                arrived(state[s].at[q, layer], halo_recv.at[s, q, way])

        factor = (1.0 if s == 0 else 2.0) / half_width
        previous = state[s - 1].at[q] if s else None
        filter_round(factor, factor * center, width, state[s].at[q], previous, state[s + 1].at[q], coeff, planes, ahead, forces, upward)
        if s < 2:
            send_halo(s + 1, q)
        else:
            for mate in mates:
                out_copy(q, mate).start()
            home[groups * place + q] = state[3][q, 1 + place]

    @pl.loop(0, groups)
    def _(q):
        for mate in mates:
            arrived(home.at[groups * mate + q], out_recv.at[q, mate])
            in_copy(q, mate).wait_send()
            out_copy(q, mate).wait_send()
        for s in range(3):
            for present, way in ((has_above, 0), (has_below, 1)):

                @pl.when(present)
                def _():
                    halo_copy(s, q, way).wait_send()

    for mate in mates:
        coeff_copy(mate).wait_send()

    @pl.when(has_above)
    def _():
        edge_copy().wait_send()


def filtered(block, coeff, center, half_width, width):
    _, nodes, modes = block.shape
    groups, tiles = modes // GROUP // ROW, nodes // TILE
    vmem = lambda *shape: pltpu.VMEM(shape, jnp.float32)
    dma = pltpu.SemaphoreType.DMA
    return pl.pallas_call(
        functools.partial(filter_kernel, lax.axis_size("dev"), center, half_width, width),
        out_shape=jax.ShapeDtypeStruct((modes // GROUP, 3, GROUP, nodes), jnp.float32),
        in_specs=[pl.BlockSpec(memory_space=pltpu.VMEM)] * 2,
        out_specs=pl.BlockSpec(memory_space=pltpu.VMEM),
        scratch_shapes=[
            vmem(modes // GROUP, 3, GROUP, nodes), *[vmem(groups, SPARE + 1, 3, GROUP, nodes)] * 4, vmem(ROW + 1, tiles, TILE),
            *[vmem(tiles, 12, GROUP, TILE)] * 4,
            dma((groups, ROW)), dma((groups, ROW)), dma((3, groups, 2)), dma((3, groups, 2)), dma((groups, ROW)), dma((groups, ROW)),
            dma((ROW,)), dma((ROW,)), dma, dma,
        ],
        compiler_params=pltpu.CompilerParams(collective_id=1, has_side_effects=True),
        name="filter",
    )(block, coeff)


def split(x):
    high = x.astype(jnp.bfloat16)
    return high, (x - high.astype(jnp.float32)).astype(jnp.bfloat16)


def dot(a, b):
    return jnp.dot(a, b, precision=HIGHEST, preferred_element_type=jnp.float32)


def dot_ta(a, b):
    return lax.dot_general(a, b, (((0,), (0,)), ((), ())), precision=HIGHEST, preferred_element_type=jnp.float32)


SWEEPS = 10
TARGET = 1e-4


def factor_kernel(scale, gram, inverse, triangle, misfit):
    g = unpacked(gram[...])
    n = g.shape[0]
    row = lax.broadcasted_iota(jnp.int32, (n, n), 0)
    col = lax.broadcasted_iota(jnp.int32, (n, n), 1)
    diagonal = jnp.where(row == col, g, 0.0)
    d_col = lax.rsqrt(jnp.sum(diagonal, axis=1, keepdims=True))
    d_row = lax.rsqrt(jnp.sum(diagonal, axis=0, keepdims=True))
    unit = g * d_col * d_row
    one = jnp.where(row == col, 1.0, 0.0)
    weight = jnp.where(row < col, 1.0, jnp.where(row == col, 0.5, 0.0))

    def refined(state):
        s, _, count = state
        parts = split(s)
        excess = three(parts, split(three(unit_parts, parts, 0)), 0) - one
        s = s - three(parts, split(excess * weight), 1)
        return (s, jnp.sum(excess * excess), count + 1)

    unit_parts = split(unit)

    def three(p, q, dim):
        product = lambda a, b: lax.dot_general(a, b, (((dim,), (0,)), ((), ())), preferred_element_type=jnp.float32)
        return product(p[1], q[0]) + product(p[0], q[1]) + product(p[0], q[0])

    start = one - (unit - one) * weight
    s, size, _ = lax.while_loop(
        lambda state: jnp.logical_and(state[1] > TARGET, state[2] < SWEEPS), refined, (start, jnp.float32(1.0), 0)
    )
    inverse[...] = d_col * s
    r = three(split(s), unit_parts, 0)
    triangle[...] = jnp.where(row <= col, r * (scale / d_row), 0.0)
    norm = jnp.sum(s * s)
    misfit[0, 0] = jnp.where(norm <= n + 50.0, size, 1.0)


def factored(gram, scale):
    n = gram.shape[1] * 2
    return pl.pallas_call(
        functools.partial(factor_kernel, scale),
        out_shape=(
            jax.ShapeDtypeStruct((n, n), jnp.float32),
            jax.ShapeDtypeStruct((n, n), jnp.float32),
            jax.ShapeDtypeStruct((1, 1), jnp.float32),
        ),
        in_specs=[pl.BlockSpec(memory_space=pltpu.VMEM)],
        out_specs=(
            pl.BlockSpec(memory_space=pltpu.VMEM),
            pl.BlockSpec(memory_space=pltpu.VMEM),
            pl.BlockSpec(memory_space=pltpu.SMEM),
        ),
        name="factor",
    )(gram)


def elimination_kernel(gram, extra, inverse_t, triangle, a, w):
    n = gram.shape[0]
    row = lax.broadcasted_iota(jnp.int32, (n, n), 0)
    col = lax.broadcasted_iota(jnp.int32, (n, n), 1)
    g = gram[...]
    one = jnp.where(row == col, 1.0, 0.0)
    diagonal = jnp.where(row == col, g, 0.0)
    s_col = jnp.sum(diagonal, axis=1, keepdims=True)
    s_row = jnp.sum(diagonal, axis=0, keepdims=True)
    d_col = lax.rsqrt(jnp.where(s_col > 0, s_col, 1.0))
    d_row = lax.rsqrt(jnp.where(s_row > 0, s_row, 1.0))
    a[...] = g * d_col * d_row + extra[0, 0] * one
    w[...] = one

    @pl.loop(0, n)
    def _(k):
        pivot_row = a[pl.ds(k, 1), :]
        column = jnp.sum(jnp.where(col == k, a[...], 0.0), axis=1, keepdims=True)
        lane = lax.broadcasted_iota(jnp.int32, (1, n), 1)
        pivot = jnp.maximum(jnp.sum(jnp.where(lane == k, pivot_row, 0.0), axis=1, keepdims=True), 1e-12)
        below = lax.broadcasted_iota(jnp.int32, (n, 1), 0) > k
        ratio = jnp.where(below, column / pivot, 0.0)
        w_row = w[pl.ds(k, 1), :]
        a[...] = a[...] - ratio * pivot_row
        w[...] = w[...] - ratio * w_row

    u = a[...]
    pivots = jnp.maximum(jnp.sum(jnp.where(row == col, u, 0.0), axis=1, keepdims=True), 1e-12)
    root = lax.rsqrt(pivots)
    triangle[...] = jnp.where(row < col, u * root, jnp.where(row == col, pivots * root, 0.0)) / d_row
    inverse_t[...] = w[...] * root * d_row


def eliminated(gram, extra):
    n = gram.shape[0]
    return pl.pallas_call(
        elimination_kernel,
        out_shape=(jax.ShapeDtypeStruct((n, n), jnp.float32),) * 2,
        in_specs=[pl.BlockSpec(memory_space=pltpu.VMEM), pl.BlockSpec(memory_space=pltpu.SMEM)],
        out_specs=(pl.BlockSpec(memory_space=pltpu.VMEM),) * 2,
        scratch_shapes=[pltpu.VMEM((n, n), jnp.float32)] * 2,
        name="eliminate",
    )(gram, extra.reshape(1, 1))


def all_reduce_kernel(sizes, x, out, half, part, summed, full, core_in, x_in, y_in, z_in, send, core_sem, x_sem, y_sem, z_sem, back_sem, pair_sem):
    nz, ny, nx = sizes
    me = lax.axis_index("dev")
    core, at_x = me % 2, me // 2 % nx
    at_y, at_z = me // (2 * nx) % ny, me // (2 * nx * ny)
    partner = me + 1 - 2 * core
    along = lambda at, j, size, stride: ((at + j) % size, me + ((at + j) % size - at) * stride)
    x_peers = [along(at_x, j, nx, 2) for j in range(1, nx)]
    y_peers = [along(at_y, j, ny, 2 * nx) for j in range(1, ny)]
    z_peers = [along(at_z, j, nz, 2 * nx * ny) for j in range(1, nz)]

    barrier = pltpu.get_barrier_semaphore()
    others = [partner] + [peer for _, peer in x_peers + y_peers + z_peers]
    for peer in others:
        pl.semaphore_signal(barrier, inc=1, device_id=(peer,), device_id_type=MESH)
    pl.semaphore_wait(barrier, len(others))

    started = []

    def copy(src, dst, recv_sem, peer):
        transfer = pltpu.make_async_remote_copy(
            src_ref=src, dst_ref=dst, send_sem=send.at[len(started)], recv_sem=recv_sem, device_id=(peer,), device_id_type=MESH
        )
        transfer.start()
        started.append(transfer)

    def arrived(dst, recv_sem):
        pltpu.make_async_remote_copy(
            src_ref=dst, dst_ref=dst, send_sem=send.at[0], recv_sem=recv_sem, device_id=(partner,), device_id_type=MESH
        ).wait_recv()

    rows = x.shape[0] // 2
    piece = rows // nx
    copy(x.at[pl.ds((1 - core) * rows, rows)], core_in, core_sem, partner)
    arrived(core_in, core_sem)
    half[...] = x[pl.ds(core * rows, rows)] + core_in[...]

    for other, peer in x_peers:
        copy(half.at[pl.ds(other * piece, piece)], x_in.at[at_x], x_sem.at[at_x], peer)
    x_in[at_x] = half[pl.ds(at_x * piece, piece)]
    for other, peer in x_peers:
        arrived(x_in.at[other], x_sem.at[other])
    total = x_in[0]
    for i in range(1, nx):
        total = total + x_in[i]

    for stage, (peers, at, size, slots, sem) in enumerate(((y_peers, at_y, ny, y_in, y_sem), (z_peers, at_z, nz, z_in, z_sem))):
        part[stage] = total
        for other, peer in peers:
            copy(part.at[stage], slots.at[at], sem.at[at], peer)
        slots[at] = total
        for other, peer in peers:
            arrived(slots.at[other], sem.at[other])
        total = slots[0]
        for i in range(1, size):
            total = total + slots[i]

    summed[...] = total
    mine = core * rows + at_x * piece
    for other, peer in x_peers:
        copy(summed, full.at[pl.ds(mine, piece)], back_sem.at[at_x], peer)
    copy(summed, full.at[pl.ds(mine, piece)], pair_sem.at[at_x], partner)
    full[pl.ds(mine, piece)] = total
    for other, peer in x_peers:
        there = full.at[pl.ds(core * rows + other * piece, piece)]
        arrived(there, back_sem.at[other])
        copy(there, there, pair_sem.at[other], partner)
    for i in range(nx):
        arrived(full.at[pl.ds((1 - core) * rows + i * piece, piece)], pair_sem.at[i])
    out[...] = full[...]
    for transfer in started:
        transfer.wait_send()


def all_reduce(x, sizes=(4, 4, 4)):
    nz, ny, nx = sizes
    n, m = x.shape
    rows = n // 2
    piece = rows // nx
    copies = 1 + (nx - 1) + (ny - 1) + (nz - 1) + nx + (nx - 1)
    block = lambda *lead: pltpu.VMEM((*lead, m), jnp.float32)
    return pl.pallas_call(
        functools.partial(all_reduce_kernel, sizes),
        out_shape=jax.ShapeDtypeStruct(x.shape, jnp.float32),
        in_specs=[pl.BlockSpec(memory_space=pltpu.VMEM)],
        out_specs=pl.BlockSpec(memory_space=pltpu.VMEM),
        scratch_shapes=[
            block(rows), block(2, piece), block(piece), block(n), block(rows), block(nx, piece), block(ny, piece), block(nz, piece),
            pltpu.SemaphoreType.DMA((copies,)), pltpu.SemaphoreType.DMA, pltpu.SemaphoreType.DMA((nx,)), pltpu.SemaphoreType.DMA((ny,)),
            pltpu.SemaphoreType.DMA((nz,)), pltpu.SemaphoreType.DMA((nx,)), pltpu.SemaphoreType.DMA((nx,)),
        ],
        compiler_params=pltpu.CompilerParams(collective_id=0, has_side_effects=True),
        name="all_reduce",
    )(x)


def packed(gram):
    half = gram.shape[0] // 2
    return jnp.concatenate([gram[:half, :half], gram[:half, half:], gram[half:, half:]], axis=0)


def unpacked(blocks):
    half = blocks.shape[1]
    first, cross, last = (blocks[i * half : (i + 1) * half] for i in range(3))
    return jnp.concatenate([jnp.concatenate([first, cross], axis=1), jnp.concatenate([cross.T, last], axis=1)], axis=0)


def gram_kernel(x_ref, out):
    total, cross = 0.0, 0.0
    product = lambda p, q: lax.dot_general(p, q, (((1,), (1,)), ((), ())), preferred_element_type=jnp.float32)
    for k in range(x_ref.shape[1]):
        high, low = split(x_ref[:, k].reshape(-1, x_ref.shape[-1]))
        total = total + product(high, high)
        cross = cross + product(high, low)
    out[...] = packed(total + (cross + cross.T))


def gram_of(x):
    n = x.shape[0] * x.shape[2]
    return pl.pallas_call(
        gram_kernel,
        out_shape=jax.ShapeDtypeStruct((n // 2 * 3, n // 2), jnp.float32),
        in_specs=[pl.BlockSpec(memory_space=pltpu.VMEM)],
        out_specs=pl.BlockSpec(memory_space=pltpu.VMEM),
        name="gram",
    )(x)


PART = 512


def product_kernel(row_scale, x_ref, inverse, out, high_s, low_s):
    k, part = pl.program_id(0), pl.program_id(1)

    @pl.when(jnp.logical_and(k == 0, part == 0))
    def _():
        high_s[...], low_s[...] = split(inverse[...] * row_scale)

    nodes = pl.ds(pl.multiple_of(part * PART, PART), PART)
    high, low = split(x_ref[:, k, :, nodes].reshape(-1, PART))
    product = lambda p, q: lax.dot_general(p, q, (((0,), (0,)), ((), ())), preferred_element_type=jnp.float32)
    out[0] = product(low, high_s[...]) + product(high, low_s[...]) + product(high, high_s[...])


def product_of(x, inverse, row_scale):
    n, nodes = x.shape[0] * x.shape[2], x.shape[3]
    return pl.pallas_call(
        functools.partial(product_kernel, row_scale),
        out_shape=jax.ShapeDtypeStruct((3, nodes, n), jnp.float32),
        grid=(3, nodes // PART),
        in_specs=[pl.BlockSpec(memory_space=pltpu.VMEM)] * 2,
        out_specs=pl.BlockSpec((1, PART, n), lambda k, part: (k, part, 0)),
        scratch_shapes=[pltpu.VMEM((n, n), jnp.bfloat16)] * 2,
        name="product",
    )(x, inverse)


def local(start_block, modulus, occupancy):
    center, half_width = filter_bounds(element_matrix())
    coeff = (modulus * occupancy.astype(jnp.float32)).reshape(-1, TILE)
    modes = start_block.shape[4]
    flat = start_block.reshape(3, -1, modes)
    row_scale = math.sqrt(math.prod(flat.shape[:2]) * lax.axis_size("dev"))
    current = filtered(flat, coeff, center, half_width, start_block.shape[3])
    gram = all_reduce(gram_of(current))
    inverse, triangle, misfit = factored(gram, 1.0 / row_scale)

    def direct(x, inverse, triangle):
        return product_of(x, inverse, row_scale), triangle

    def general(x, inverse, triangle):
        def one_pass(i, state):
            x, total = state
            extra = jnp.where(i == 0, 3e-5, 0.0).astype(jnp.float32)
            inverse_t, r = eliminated(unpacked(all_reduce(packed(dot_ta(x, x)))), extra)
            return (dot(x, inverse_t.T), dot(r, total))

        x, total = lax.fori_loop(0, 4, one_pass, (x.transpose(1, 3, 0, 2).reshape(-1, modes), jnp.eye(modes, dtype=jnp.float32)))
        return (x * row_scale).reshape(flat.shape), total / row_scale

    basis, triangle = lax.cond(misfit[0, 0] <= TARGET, direct, general, current, inverse, triangle)
    return basis.reshape(start_block.shape), triangle


def solution(mesh):
    return jax.shard_map(
        local,
        mesh=mesh,
        in_specs=(P(None, "dev", None, None, None), P("dev", None, None), P("dev", None, None)),
        out_specs=(P(None, "dev", None, None, None), P()),
        check_vma=False,
    )
```

```python
import functools
import math

import jax
import jax.numpy as jnp
import numpy as np
from jax import lax
from jax.experimental import pallas as pl
from jax.experimental.pallas import tpu as pltpu
from jax.sharding import PartitionSpec as P

DEGREE = 3
HIGHEST = lax.Precision.HIGHEST
MESH = pl.DeviceIdType.MESH


def element_matrix():
    poisson = 0.3
    lame_first = poisson / ((1.0 + poisson) * (1.0 - 2.0 * poisson))
    shear_modulus = 0.5 / (1.0 + poisson)
    elastic = np.zeros((6, 6))
    elastic[:3, :3] = lame_first
    for axis_number in range(3):
        elastic[axis_number, axis_number] += 2.0 * shear_modulus
        elastic[axis_number + 3, axis_number + 3] = shear_modulus
    points = [0.5 - 0.5 / np.sqrt(3.0), 0.5 + 0.5 / np.sqrt(3.0)]
    stiffness = np.zeros((24, 24))
    for point_x in points:
        for point_y in points:
            for point_z in points:
                gradients = np.zeros((3, 8))
                for corner in range(8):
                    offset_x, offset_y, offset_z = (corner % 2, corner // 2 % 2, corner // 4)
                    along_x = point_x if offset_x else 1.0 - point_x
                    along_y = point_y if offset_y else 1.0 - point_y
                    along_z = point_z if offset_z else 1.0 - point_z
                    gradients[0, corner] = (2 * offset_x - 1) * along_y * along_z
                    gradients[1, corner] = (2 * offset_y - 1) * along_x * along_z
                    gradients[2, corner] = (2 * offset_z - 1) * along_x * along_y
                strain_map = np.zeros((6, 24))
                strain_map[0, 0:8] = gradients[0]
                strain_map[1, 8:16] = gradients[1]
                strain_map[2, 16:24] = gradients[2]
                strain_map[3, 0:8] = gradients[1]
                strain_map[3, 8:16] = gradients[0]
                strain_map[4, 8:16] = gradients[2]
                strain_map[4, 16:24] = gradients[1]
                strain_map[5, 0:8] = gradients[2]
                strain_map[5, 16:24] = gradients[0]
                stiffness += strain_map.T @ elastic @ strain_map / 8.0
    return stiffness


def filter_bounds(stiffness):
    upper_end = 8.0 * float(np.max(np.sum(np.abs(stiffness), axis=1)))
    lower_end = 0.15 * upper_end
    return (0.5 * (upper_end + lower_end), 0.5 * (upper_end - lower_end))


LAME = 0.3 / (1.3 * 0.4)
SHEAR = 0.5 / 1.3


def element_forces(h, coeff, factor):
    g = {}

    def coupled(keys, own, shared):
        total = h[keys[0]]
        for key in keys[1:]:
            total = total + h[key]
        total = total * shared
        for key in keys:
            g[key] = total if own is None else own * h[key] + total

    scaled = lambda value: coeff * (value * factor)
    mu16, mu48 = scaled(SHEAR / 16), scaled(SHEAR / 48)
    coupled([(0, "dss"), (1, "sds"), (2, "ssd")], scaled(2 * SHEAR / 16), scaled(LAME / 16))
    own, shared = scaled(3 * SHEAR / 48), scaled(LAME / 48)
    coupled([(0, "dsd"), (1, "sdd")], own, shared)
    coupled([(0, "dds"), (2, "sdd")], own, shared)
    coupled([(1, "dds"), (2, "dsd")], own, shared)
    coupled([(0, "sdd"), (1, "dsd"), (2, "dds")], mu48, mu48)
    coupled([(0, "sds"), (1, "dss")], None, mu16)
    coupled([(0, "ssd"), (2, "dss")], None, mu16)
    coupled([(1, "ssd"), (2, "sds")], None, mu16)
    last = scaled((LAME + 4 * SHEAR) / 144)
    for k in range(3):
        g[(k, "ddd")] = last * h[(k, "ddd")]
    return g


PLANES = {}
for _k in range(3):
    for _a in "sd":
        for _b in "sd":
            PLANES[(_k, _a, _b)] = len(PLANES)

TILE = 128
GROUP = 8
ROW = 8
SPARE = ROW + 2
PAIR = 4


def filter_round(factor, shift, width, here, previous, out, coeff, planes, ahead, forces, upward):
    tiles = here.shape[3] // TILE
    lane = lax.broadcasted_iota(jnp.int32, (GROUP, TILE), 1)
    first_x, last_x = lane % width == 0, lane % width == width - 1
    low_rows, high_rows = lane < TILE - width, lane >= width
    tile = lambda t: pl.ds(t * TILE, TILE)

    def along_x(layer, t):
        q = {}
        for k in range(3):
            a = here[layer, k, :, tile(t)]
            b = jnp.where(last_x, 0.0, pltpu.roll(a, TILE - 1, 1))
            for name, value in (("s", a + b), ("d", b - a)):
                q[(k, name)] = (value, pltpu.roll(value, TILE - width, 1))
        return q

    def along_xy(layer):
        later = along_x(layer, 0)
        for t in range(tiles):
            now = later
            later = along_x(layer, t + 1) if t + 1 < tiles else None
            q = {}
            for key, (value, rolled) in now.items():
                after = jnp.where(low_rows, rolled, later[key][1] if later else 0.0)
                q[(*key, "s")] = value + after
                q[(*key, "d")] = after - value
            yield t, q

    def fill(into, layer):
        for t, q in along_xy(layer):
            for key, value in q.items():
                into[t, PLANES[key]] = value

    fill(planes, 0)
    fill(ahead, 1)

    @pl.loop(0, ROW + 1)
    def _(e):
        target = jnp.where(e == 0, SPARE, e)

        @pl.loop(0, tiles, step=PAIR)
        def _(first):
            for t in [first + i for i in range(PAIR)]:
                h = {}
                for key, place in PLANES.items():
                    near, far = planes[t, place], ahead[t, place]
                    name = key[1] + key[2]
                    h[(key[0], name + "s")] = near + far
                    h[(key[0], name + "d")] = far - near
                    planes[t, place] = far
                g = element_forces(h, jnp.broadcast_to(coeff[e, pl.ds(t, 1), :], (GROUP, TILE)), factor)
                for key, place in PLANES.items():
                    name = key[1] + key[2]
                    even, odd = g.get((key[0], name + "s")), g[(key[0], name + "d")]
                    forces[t, place] = upward[t, place] + (-odd if even is None else even - odd)
                    upward[t, place] = odd if even is None else even + odd

        fill(ahead, jnp.minimum(e + 2, ROW + 1))
        behind = {}
        for t in range(tiles):
            for k in range(3):
                part = {}
                for a in "sd":
                    up, down = forces[t, PLANES[(k, a, "s")]], forces[t, PLANES[(k, a, "d")]]
                    rolled = pltpu.roll(up + down, width, 1)
                    part[a] = (up - down) + jnp.where(high_rows, rolled, behind.get((k, a), 0.0))
                    behind[(k, a)] = rolled
                moved = jnp.where(first_x, 0.0, pltpu.roll(part["s"] + part["d"], 1, 1))
                where = (k, slice(None), tile(t))
                value = (part["s"] - part["d"]) + moved - shift * here[(e, *where)]
                if previous is not None:
                    value = value - previous[(e, *where)]
                out[(target, *where)] = value


ORDER = (
    ("in", 0), (0, 0), ("in", 1), (1, 0), (0, 1), ("in", 2), (2, 0), (1, 1),
    (0, 2), ("in", 3), (2, 1), (1, 2), (0, 3), (2, 2), (1, 3), (2, 3),
)


def filter_kernel(
    devices, center, half_width, width, x, modulus, occupancy, home, turned, state_0, state_1, state_2, state_3, coeff, planes, ahead, forces, upward, coeff_mine,
    in_send, in_recv, halo_send, halo_recv, out_send, out_recv, coeff_send, coeff_recv, edge_send, edge_recv,
):
    me = lax.axis_index("dev")
    place, row = me % ROW, me // ROW
    base = me - place
    has_below, has_above = row > 0, row < devices // ROW - 1
    groups = turned.shape[0] // ROW
    state = [state_0, state_1, state_2, state_3]
    nodes = x.shape[1]
    mates = []
    for side in (0, 1):
        for step in (1, 3, 2) if side == 0 else (1, 3, 2, 0):
            chip, core = (place // 2 + step) % (ROW // 2), (place % 2 + side) % 2
            mates.append(2 * chip + core)
    barrier = pltpu.get_barrier_semaphore()
    for mate in mates:
        pl.semaphore_signal(barrier, inc=1, device_id=(base + mate,), device_id_type=MESH)
    for present, peer in ((has_below, me - ROW), (has_above, me + ROW)):

        @pl.when(present)
        def _():
            pl.semaphore_signal(barrier, inc=1, device_id=(peer,), device_id_type=MESH)

    @pl.loop(0, 3 * (nodes // TILE))
    def _(i):
        k, t = i // (nodes // TILE), i % (nodes // TILE)
        lanes = pl.ds(pl.multiple_of(t * TILE, TILE), TILE)
        for c in range(x.shape[2] // TILE):
            block = x[k, lanes, pl.ds(c * TILE, TILE)].T
            for g in range(TILE // GROUP):
                turned[c * (TILE // GROUP) + g, k, :, lanes] = block[g * GROUP : (g + 1) * GROUP]

    beside = coeff_mine.shape[1] // width
    pieces = []
    for i in range(beside):
        rows = pl.ds(i, coeff_mine.shape[0], stride=beside)
        pieces.append(modulus[rows, :] * occupancy[rows, :].astype(jnp.float32))
    coeff_mine[...] = jnp.concatenate(pieces, axis=1)
    coeff[1 + place] = coeff_mine[...]

    def remote(src, dst, send_sem, recv_sem, peer):
        return pltpu.make_async_remote_copy(
            src_ref=src, dst_ref=dst, send_sem=send_sem, recv_sem=recv_sem, device_id=(peer,), device_id_type=MESH
        )

    def coeff_copy(mate):
        return remote(coeff_mine, coeff.at[1 + place], coeff_send.at[mate], coeff_recv.at[place], base + mate)

    def in_copy(q, mate):
        return remote(
            turned.at[groups * mate + q], state[0].at[q, 1 + place], in_send.at[q, mate], in_recv.at[q, place], base + mate
        )

    def out_copy(q, mate):
        return remote(state[3].at[q, 1 + mate], home.at[groups * place + q], out_send.at[q, mate], out_recv.at[q, place], base + mate)

    def halo_copy(s, q, way):
        source, target, peer = ((ROW, 0, me + ROW), (1, ROW + 1, me - ROW))[way]
        return remote(state[s].at[q, source], state[s].at[q, target], halo_send.at[s, q, way], halo_recv.at[s, q, way], peer)

    def edge_copy():
        return remote(coeff.at[ROW], coeff.at[0], edge_send, edge_recv, me + ROW)

    def arrived(dst, recv_sem):
        remote(dst, dst, edge_send, recv_sem, base + mates[0]).wait_recv()

    pl.semaphore_wait(barrier, len(mates) + has_below.astype(jnp.int32) + has_above.astype(jnp.int32))
    for mate in mates:
        coeff_copy(mate).start()

    @pl.loop(0, groups)
    def _(q):
        for mate in mates:
            in_copy(q, mate).start()

    @pl.loop(0, groups)
    def _(q):
        state[0][q, 1 + place] = turned[groups * place + q]

    upward[...] = jnp.zeros_like(upward)

    @pl.when(jnp.logical_not(has_below))
    def _():
        coeff[0] = jnp.zeros(coeff.shape[1:], jnp.float32)

    for present, layer in ((has_below, 0), (has_above, ROW + 1)):

        @pl.when(jnp.logical_not(present))
        def _():
            @pl.loop(0, groups)
            def _(q):
                for s in range(3):
                    state[s][q, layer] = jnp.zeros(state[s].shape[2:], jnp.float32)

    for mate in mates:
        arrived(coeff.at[1 + mate], coeff_recv.at[mate])

    @pl.when(has_above)
    def _():
        edge_copy().start()

    @pl.when(has_below)
    def _():
        arrived(coeff.at[0], edge_recv)

    def send_halo(s, q):
        for present, way in ((has_above, 0), (has_below, 1)):

            @pl.when(present)
            def _():
                halo_copy(s, q, way).start()

    for s, q in ORDER:
        if s == "in":
            for mate in mates:
                arrived(state[0].at[q, 1 + mate], in_recv.at[q, mate])
            send_halo(0, q)
            continue
        for present, way, layer in ((has_below, 0, 0), (has_above, 1, ROW + 1)):

            @pl.when(present)
            def _():
                arrived(state[s].at[q, layer], halo_recv.at[s, q, way])

        factor = (1.0 if s == 0 else 2.0) / half_width
        previous = state[s - 1].at[q] if s else None
        filter_round(factor, factor * center, width, state[s].at[q], previous, state[s + 1].at[q], coeff, planes, ahead, forces, upward)
        if s < 2:
            send_halo(s + 1, q)
        else:
            for mate in mates:
                out_copy(q, mate).start()
            home[groups * place + q] = state[3][q, 1 + place]

    @pl.loop(0, groups)
    def _(q):
        for mate in mates:
            arrived(home.at[groups * mate + q], out_recv.at[q, mate])
            in_copy(q, mate).wait_send()
            out_copy(q, mate).wait_send()
        for s in range(3):
            for present, way in ((has_above, 0), (has_below, 1)):

                @pl.when(present)
                def _():
                    halo_copy(s, q, way).wait_send()

    for mate in mates:
        coeff_copy(mate).wait_send()

    @pl.when(has_above)
    def _():
        edge_copy().wait_send()


def filtered(block, modulus, occupancy, center, half_width):
    _, nodes, modes = block.shape
    groups, tiles = modes // GROUP // ROW, nodes // TILE
    vmem = lambda *shape: pltpu.VMEM(shape, jnp.float32)
    dma = pltpu.SemaphoreType.DMA
    return pl.pallas_call(
        functools.partial(filter_kernel, lax.axis_size("dev"), center, half_width, modulus.shape[1]),
        out_shape=jax.ShapeDtypeStruct((modes // GROUP, 3, GROUP, nodes), jnp.float32),
        in_specs=[pl.BlockSpec(memory_space=pltpu.VMEM)] * 3,
        out_specs=pl.BlockSpec(memory_space=pltpu.VMEM),
        scratch_shapes=[
            vmem(modes // GROUP, 3, GROUP, nodes), *[vmem(groups, SPARE + 1, 3, GROUP, nodes)] * 4, vmem(ROW + 1, tiles, TILE),
            *[vmem(tiles, 12, GROUP, TILE)] * 4, vmem(tiles, TILE),
            dma((groups, ROW)), dma((groups, ROW)), dma((3, groups, 2)), dma((3, groups, 2)), dma((groups, ROW)), dma((groups, ROW)),
            dma((ROW,)), dma((ROW,)), dma, dma,
        ],
        compiler_params=pltpu.CompilerParams(collective_id=1, has_side_effects=True),
        name="filter",
    )(block, modulus, occupancy)


def split(x):
    high = x.astype(jnp.bfloat16)
    return high, (x - high.astype(jnp.float32)).astype(jnp.bfloat16)


def dot(a, b):
    return jnp.dot(a, b, precision=HIGHEST, preferred_element_type=jnp.float32)


def dot_ta(a, b):
    return lax.dot_general(a, b, (((0,), (0,)), ((), ())), precision=HIGHEST, preferred_element_type=jnp.float32)


SWEEPS = 10
TARGET = 1e-4


def factor_kernel(scale, gram, inverse, triangle, misfit):
    g = unpacked(gram[...])
    n = g.shape[0]
    row = lax.broadcasted_iota(jnp.int32, (n, n), 0)
    col = lax.broadcasted_iota(jnp.int32, (n, n), 1)
    diagonal = jnp.where(row == col, g, 0.0)
    d_col = lax.rsqrt(jnp.sum(diagonal, axis=1, keepdims=True))
    d_row = lax.rsqrt(jnp.sum(diagonal, axis=0, keepdims=True))
    unit = g * d_col * d_row
    one = jnp.where(row == col, 1.0, 0.0)
    weight = jnp.where(row < col, 1.0, jnp.where(row == col, 0.5, 0.0))

    def refined(state):
        s, _, count = state
        parts = split(s)
        excess = three(parts, split(three(unit_parts, parts, 0)), 0) - one
        s = s - three(parts, split(excess * weight), 1)
        return (s, jnp.sum(excess * excess), count + 1)

    unit_parts = split(unit)

    def three(p, q, dim):
        product = lambda a, b: lax.dot_general(a, b, (((dim,), (0,)), ((), ())), preferred_element_type=jnp.float32)
        return product(p[1], q[0]) + product(p[0], q[1]) + product(p[0], q[0])

    start = one - (unit - one) * weight
    s, size, _ = lax.while_loop(
        lambda state: jnp.logical_and(state[1] > TARGET, state[2] < SWEEPS), refined, (start, jnp.float32(1.0), 0)
    )
    inverse[...] = d_col * s
    r = three(split(s), unit_parts, 0)
    triangle[...] = jnp.where(row <= col, r * (scale / d_row), 0.0)
    norm = jnp.sum(s * s)
    misfit[0, 0] = jnp.where(norm <= n + 50.0, size, 1.0)


def factored(gram, scale):
    n = gram.shape[1] * 2
    return pl.pallas_call(
        functools.partial(factor_kernel, scale),
        out_shape=(
            jax.ShapeDtypeStruct((n, n), jnp.float32),
            jax.ShapeDtypeStruct((n, n), jnp.float32),
            jax.ShapeDtypeStruct((1, 1), jnp.float32),
        ),
        in_specs=[pl.BlockSpec(memory_space=pltpu.VMEM)],
        out_specs=(
            pl.BlockSpec(memory_space=pltpu.VMEM),
            pl.BlockSpec(memory_space=pltpu.VMEM),
            pl.BlockSpec(memory_space=pltpu.SMEM),
        ),
        name="factor",
    )(gram)


def elimination_kernel(gram, extra, inverse_t, triangle, a, w):
    n = gram.shape[0]
    row = lax.broadcasted_iota(jnp.int32, (n, n), 0)
    col = lax.broadcasted_iota(jnp.int32, (n, n), 1)
    g = gram[...]
    one = jnp.where(row == col, 1.0, 0.0)
    diagonal = jnp.where(row == col, g, 0.0)
    s_col = jnp.sum(diagonal, axis=1, keepdims=True)
    s_row = jnp.sum(diagonal, axis=0, keepdims=True)
    d_col = lax.rsqrt(jnp.where(s_col > 0, s_col, 1.0))
    d_row = lax.rsqrt(jnp.where(s_row > 0, s_row, 1.0))
    a[...] = g * d_col * d_row + extra[0, 0] * one
    w[...] = one

    @pl.loop(0, n)
    def _(k):
        pivot_row = a[pl.ds(k, 1), :]
        column = jnp.sum(jnp.where(col == k, a[...], 0.0), axis=1, keepdims=True)
        lane = lax.broadcasted_iota(jnp.int32, (1, n), 1)
        pivot = jnp.maximum(jnp.sum(jnp.where(lane == k, pivot_row, 0.0), axis=1, keepdims=True), 1e-12)
        below = lax.broadcasted_iota(jnp.int32, (n, 1), 0) > k
        ratio = jnp.where(below, column / pivot, 0.0)
        w_row = w[pl.ds(k, 1), :]
        a[...] = a[...] - ratio * pivot_row
        w[...] = w[...] - ratio * w_row

    u = a[...]
    pivots = jnp.maximum(jnp.sum(jnp.where(row == col, u, 0.0), axis=1, keepdims=True), 1e-12)
    root = lax.rsqrt(pivots)
    triangle[...] = jnp.where(row < col, u * root, jnp.where(row == col, pivots * root, 0.0)) / d_row
    inverse_t[...] = w[...] * root * d_row


def eliminated(gram, extra):
    n = gram.shape[0]
    return pl.pallas_call(
        elimination_kernel,
        out_shape=(jax.ShapeDtypeStruct((n, n), jnp.float32),) * 2,
        in_specs=[pl.BlockSpec(memory_space=pltpu.VMEM), pl.BlockSpec(memory_space=pltpu.SMEM)],
        out_specs=(pl.BlockSpec(memory_space=pltpu.VMEM),) * 2,
        scratch_shapes=[pltpu.VMEM((n, n), jnp.float32)] * 2,
        name="eliminate",
    )(gram, extra.reshape(1, 1))


def all_reduce_kernel(prepare, sizes, x, out, half, part, summed, full, core_in, x_in, y_in, z_in, send, core_sem, x_sem, y_sem, z_sem, back_sem, pair_sem):
    nz, ny, nx = sizes
    me = lax.axis_index("dev")
    core, at_x = me % 2, me // 2 % nx
    at_y, at_z = me // (2 * nx) % ny, me // (2 * nx * ny)
    partner = me + 1 - 2 * core
    along = lambda at, j, size, stride: ((at + j) % size, me + ((at + j) % size - at) * stride)
    x_peers = [along(at_x, j, nx, 2) for j in range(1, nx)]
    y_peers = [along(at_y, j, ny, 2 * nx) for j in range(1, ny)]
    z_peers = [along(at_z, j, nz, 2 * nx * ny) for j in range(1, nz)]

    barrier = pltpu.get_barrier_semaphore()
    others = [partner] + [peer for _, peer in x_peers + y_peers + z_peers]
    for peer in others:
        pl.semaphore_signal(barrier, inc=1, device_id=(peer,), device_id_type=MESH)
    x = prepare(x)
    pl.semaphore_wait(barrier, len(others))

    started = []

    def copy(src, dst, recv_sem, peer):
        transfer = pltpu.make_async_remote_copy(
            src_ref=src, dst_ref=dst, send_sem=send.at[len(started)], recv_sem=recv_sem, device_id=(peer,), device_id_type=MESH
        )
        transfer.start()
        started.append(transfer)

    def arrived(dst, recv_sem):
        pltpu.make_async_remote_copy(
            src_ref=dst, dst_ref=dst, send_sem=send.at[0], recv_sem=recv_sem, device_id=(partner,), device_id_type=MESH
        ).wait_recv()

    rows = x.shape[0] // 2
    piece = rows // nx
    copy(x.at[pl.ds((1 - core) * rows, rows)], core_in, core_sem, partner)
    arrived(core_in, core_sem)
    half[...] = x[pl.ds(core * rows, rows)] + core_in[...]

    for other, peer in x_peers:
        copy(half.at[pl.ds(other * piece, piece)], x_in.at[at_x], x_sem.at[at_x], peer)
    x_in[at_x] = half[pl.ds(at_x * piece, piece)]
    for other, peer in x_peers:
        arrived(x_in.at[other], x_sem.at[other])
    total = x_in[0]
    for i in range(1, nx):
        total = total + x_in[i]

    for stage, (peers, at, size, slots, sem) in enumerate(((y_peers, at_y, ny, y_in, y_sem), (z_peers, at_z, nz, z_in, z_sem))):
        part[stage] = total
        for other, peer in peers:
            copy(part.at[stage], slots.at[at], sem.at[at], peer)
        slots[at] = total
        for other, peer in peers:
            arrived(slots.at[other], sem.at[other])
        total = slots[0]
        for i in range(1, size):
            total = total + slots[i]

    summed[...] = total
    mine = core * rows + at_x * piece
    for other, peer in x_peers:
        copy(summed, full.at[pl.ds(mine, piece)], back_sem.at[at_x], peer)
    copy(summed, full.at[pl.ds(mine, piece)], pair_sem.at[at_x], partner)
    full[pl.ds(mine, piece)] = total
    for other, peer in x_peers:
        there = full.at[pl.ds(core * rows + other * piece, piece)]
        arrived(there, back_sem.at[other])
        copy(there, there, pair_sem.at[other], partner)
    for i in range(nx):
        arrived(full.at[pl.ds((1 - core) * rows + i * piece, piece)], pair_sem.at[i])
    out[...] = full[...]
    for transfer in started:
        transfer.wait_send()


def all_reduce_call(kernel, x, shape, own, sizes, collective_id, name):
    nz, ny, nx = sizes
    n, m = shape
    rows = n // 2
    piece = rows // nx
    copies = 1 + (nx - 1) + (ny - 1) + (nz - 1) + nx + (nx - 1)
    block = lambda *lead: pltpu.VMEM((*lead, m), jnp.float32)
    return pl.pallas_call(
        kernel,
        out_shape=jax.ShapeDtypeStruct(shape, jnp.float32),
        in_specs=[pl.BlockSpec(memory_space=pltpu.VMEM)],
        out_specs=pl.BlockSpec(memory_space=pltpu.VMEM),
        scratch_shapes=[block(n)] * own + [
            block(rows), block(2, piece), block(piece), block(n), block(rows), block(nx, piece), block(ny, piece), block(nz, piece),
            pltpu.SemaphoreType.DMA((copies,)), pltpu.SemaphoreType.DMA, pltpu.SemaphoreType.DMA((nx,)), pltpu.SemaphoreType.DMA((ny,)),
            pltpu.SemaphoreType.DMA((nz,)), pltpu.SemaphoreType.DMA((nx,)), pltpu.SemaphoreType.DMA((nx,)),
        ],
        compiler_params=pltpu.CompilerParams(collective_id=collective_id, has_side_effects=True),
        name=name,
    )(x)


SIZES = (4, 4, 4)


def all_reduce(x, sizes=SIZES):
    kernel = functools.partial(all_reduce_kernel, lambda ref: ref, sizes)
    return all_reduce_call(kernel, x, x.shape, 0, sizes, 0, "all_reduce")


def summed_gram(x, sizes=SIZES):
    def kernel(x_ref, out, mine, *rest):
        def prepare(ref):
            gram_kernel(ref, mine)
            return mine

        all_reduce_kernel(prepare, sizes, x_ref, out, *rest)

    n = x.shape[0] * x.shape[2]
    return all_reduce_call(kernel, x, (n // 2 * 3, n // 2), 1, sizes, 2, "summed_gram")


def packed(gram):
    half = gram.shape[0] // 2
    return jnp.concatenate([gram[:half, :half], gram[:half, half:], gram[half:, half:]], axis=0)


def unpacked(blocks):
    half = blocks.shape[1]
    first, cross, last = (blocks[i * half : (i + 1) * half] for i in range(3))
    return jnp.concatenate([jnp.concatenate([first, cross], axis=1), jnp.concatenate([cross.T, last], axis=1)], axis=0)


def gram_kernel(x_ref, out):
    total, cross = 0.0, 0.0
    product = lambda p, q: lax.dot_general(p, q, (((1,), (1,)), ((), ())), preferred_element_type=jnp.float32)
    for k in range(x_ref.shape[1]):
        high, low = split(x_ref[:, k].reshape(-1, x_ref.shape[-1]))
        total = total + product(high, high)
        cross = cross + product(high, low)
    out[...] = packed(total + (cross + cross.T))


def component_spec(x):
    return pl.BlockSpec((x.shape[0], 1, *x.shape[2:]), lambda k: (0, k, 0, 0))


def product_kernel(row_scale, x_ref, inverse, out, high_s, low_s):
    @pl.when(pl.program_id(0) == 0)
    def _():
        high_s[...], low_s[...] = split(inverse[...] * row_scale)

    high, low = split(x_ref[...].reshape(-1, x_ref.shape[-1]))
    product = lambda p, q: lax.dot_general(p, q, (((0,), (0,)), ((), ())), preferred_element_type=jnp.float32)
    out[0] = product(low, high_s[...]) + product(high, low_s[...]) + product(high, high_s[...])


def product_of(x, inverse, row_scale):
    n, nodes = x.shape[0] * x.shape[2], x.shape[3]
    return pl.pallas_call(
        functools.partial(product_kernel, row_scale),
        out_shape=jax.ShapeDtypeStruct((3, nodes, n), jnp.float32),
        grid=(3,),
        in_specs=[component_spec(x), pl.BlockSpec((n, n), lambda k: (0, 0))],
        out_specs=pl.BlockSpec((1, nodes, n), lambda k: (k, 0, 0)),
        scratch_shapes=[pltpu.VMEM((n, n), jnp.bfloat16)] * 2,
        name="product",
    )(x, inverse)


def local(start_block, modulus, occupancy):
    center, half_width = filter_bounds(element_matrix())
    modes = start_block.shape[4]
    flat = start_block.reshape(3, -1, modes)
    row_scale = math.sqrt(math.prod(flat.shape[:2]) * lax.axis_size("dev"))
    current = filtered(flat, modulus[0], occupancy[0], center, half_width)
    gram = summed_gram(current)
    inverse, triangle, misfit = factored(gram, 1.0 / row_scale)

    def direct(x, inverse, triangle):
        return product_of(x, inverse, row_scale), triangle

    def general(x, inverse, triangle):
        def one_pass(i, state):
            x, total = state
            extra = jnp.where(i == 0, 3e-5, 0.0).astype(jnp.float32)
            inverse_t, r = eliminated(unpacked(all_reduce(packed(dot_ta(x, x)))), extra)
            return (dot(x, inverse_t.T), dot(r, total))

        x, total = lax.fori_loop(0, 4, one_pass, (x.transpose(1, 3, 0, 2).reshape(-1, modes), jnp.eye(modes, dtype=jnp.float32)))
        return (x * row_scale).reshape(flat.shape), total / row_scale

    basis, triangle = lax.cond(misfit[0, 0] <= TARGET, direct, general, current, inverse, triangle)
    return basis.reshape(start_block.shape), triangle


def solution(mesh):
    return jax.shard_map(
        local,
        mesh=mesh,
        in_specs=(P(None, "dev", None, None, None), P("dev", None, None), P("dev", None, None)),
        out_specs=(P(None, "dev", None, None, None), P()),
        check_vma=False,
    )
```

```python
import functools
import math

import jax
import jax.numpy as jnp
import numpy as np
from jax import lax
from jax.experimental import pallas as pl
from jax.experimental.pallas import tpu as pltpu
from jax.sharding import PartitionSpec as P

DEGREE = 3
HIGHEST = lax.Precision.HIGHEST
MESH = pl.DeviceIdType.MESH


def element_matrix():
    poisson = 0.3
    lame_first = poisson / ((1.0 + poisson) * (1.0 - 2.0 * poisson))
    shear_modulus = 0.5 / (1.0 + poisson)
    elastic = np.zeros((6, 6))
    elastic[:3, :3] = lame_first
    for axis_number in range(3):
        elastic[axis_number, axis_number] += 2.0 * shear_modulus
        elastic[axis_number + 3, axis_number + 3] = shear_modulus
    points = [0.5 - 0.5 / np.sqrt(3.0), 0.5 + 0.5 / np.sqrt(3.0)]
    stiffness = np.zeros((24, 24))
    for point_x in points:
        for point_y in points:
            for point_z in points:
                gradients = np.zeros((3, 8))
                for corner in range(8):
                    offset_x, offset_y, offset_z = (corner % 2, corner // 2 % 2, corner // 4)
                    along_x = point_x if offset_x else 1.0 - point_x
                    along_y = point_y if offset_y else 1.0 - point_y
                    along_z = point_z if offset_z else 1.0 - point_z
                    gradients[0, corner] = (2 * offset_x - 1) * along_y * along_z
                    gradients[1, corner] = (2 * offset_y - 1) * along_x * along_z
                    gradients[2, corner] = (2 * offset_z - 1) * along_x * along_y
                strain_map = np.zeros((6, 24))
                strain_map[0, 0:8] = gradients[0]
                strain_map[1, 8:16] = gradients[1]
                strain_map[2, 16:24] = gradients[2]
                strain_map[3, 0:8] = gradients[1]
                strain_map[3, 8:16] = gradients[0]
                strain_map[4, 8:16] = gradients[2]
                strain_map[4, 16:24] = gradients[1]
                strain_map[5, 0:8] = gradients[2]
                strain_map[5, 16:24] = gradients[0]
                stiffness += strain_map.T @ elastic @ strain_map / 8.0
    return stiffness


def filter_bounds(stiffness):
    upper_end = 8.0 * float(np.max(np.sum(np.abs(stiffness), axis=1)))
    lower_end = 0.15 * upper_end
    return (0.5 * (upper_end + lower_end), 0.5 * (upper_end - lower_end))


LAME = 0.3 / (1.3 * 0.4)
SHEAR = 0.5 / 1.3


def element_forces(h, coeff, factor):
    g = {}

    def coupled(keys, own, shared):
        total = h[keys[0]]
        for key in keys[1:]:
            total = total + h[key]
        total = total * shared
        for key in keys:
            g[key] = total if own is None else own * h[key] + total

    scaled = lambda value: coeff * (value * factor)
    mu16, mu48 = scaled(SHEAR / 16), scaled(SHEAR / 48)
    coupled([(0, "dss"), (1, "sds"), (2, "ssd")], scaled(2 * SHEAR / 16), scaled(LAME / 16))
    own, shared = scaled(3 * SHEAR / 48), scaled(LAME / 48)
    coupled([(0, "dsd"), (1, "sdd")], own, shared)
    coupled([(0, "dds"), (2, "sdd")], own, shared)
    coupled([(1, "dds"), (2, "dsd")], own, shared)
    coupled([(0, "sdd"), (1, "dsd"), (2, "dds")], mu48, mu48)
    coupled([(0, "sds"), (1, "dss")], None, mu16)
    coupled([(0, "ssd"), (2, "dss")], None, mu16)
    coupled([(1, "ssd"), (2, "sds")], None, mu16)
    last = scaled((LAME + 4 * SHEAR) / 144)
    for k in range(3):
        g[(k, "ddd")] = last * h[(k, "ddd")]
    return g


PLANES = {}
for _k in range(3):
    for _a in "sd":
        for _b in "sd":
            PLANES[(_k, _a, _b)] = len(PLANES)

TILE = 128
GROUP = 8
ROW = 8
SPARE = ROW + 2
PAIR = 4


def filter_round(factor, shift, width, here, previous, out, coeff, planes, ahead, forces, upward):
    tiles = here.shape[3] // TILE
    lane = lax.broadcasted_iota(jnp.int32, (GROUP, TILE), 1)
    first_x, last_x = lane % width == 0, lane % width == width - 1
    low_rows, high_rows = lane < TILE - width, lane >= width
    tile = lambda t: pl.ds(t * TILE, TILE)

    def along_x(layer, t):
        q = {}
        for k in range(3):
            a = here[layer, k, :, tile(t)]
            b = jnp.where(last_x, 0.0, pltpu.roll(a, TILE - 1, 1))
            for name, value in (("s", a + b), ("d", b - a)):
                q[(k, name)] = (value, pltpu.roll(value, TILE - width, 1))
        return q

    def along_xy(layer):
        later = along_x(layer, 0)
        for t in range(tiles):
            now = later
            later = along_x(layer, t + 1) if t + 1 < tiles else None
            q = {}
            for key, (value, rolled) in now.items():
                after = jnp.where(low_rows, rolled, later[key][1] if later else 0.0)
                q[(*key, "s")] = value + after
                q[(*key, "d")] = after - value
            yield t, q

    def fill(into, layer):
        for t, q in along_xy(layer):
            for key, value in q.items():
                into[t, PLANES[key]] = value

    fill(planes, 0)
    fill(ahead, 1)

    @pl.loop(0, ROW + 1)
    def _(e):
        target = jnp.where(e == 0, SPARE, e)

        @pl.loop(0, tiles, step=PAIR)
        def _(first):
            for t in [first + i for i in range(PAIR)]:
                h = {}
                for key, place in PLANES.items():
                    near, far = planes[t, place], ahead[t, place]
                    name = key[1] + key[2]
                    h[(key[0], name + "s")] = near + far
                    h[(key[0], name + "d")] = far - near
                    planes[t, place] = far
                g = element_forces(h, jnp.broadcast_to(coeff[e, pl.ds(t, 1), :], (GROUP, TILE)), factor)
                for key, place in PLANES.items():
                    name = key[1] + key[2]
                    even, odd = g.get((key[0], name + "s")), g[(key[0], name + "d")]
                    forces[t, place] = upward[t, place] + (-odd if even is None else even - odd)
                    upward[t, place] = odd if even is None else even + odd

        fill(ahead, jnp.minimum(e + 2, ROW + 1))
        behind = {}
        for t in range(tiles):
            for k in range(3):
                part = {}
                for a in "sd":
                    up, down = forces[t, PLANES[(k, a, "s")]], forces[t, PLANES[(k, a, "d")]]
                    rolled = pltpu.roll(up + down, width, 1)
                    part[a] = (up - down) + jnp.where(high_rows, rolled, behind.get((k, a), 0.0))
                    behind[(k, a)] = rolled
                moved = jnp.where(first_x, 0.0, pltpu.roll(part["s"] + part["d"], 1, 1))
                where = (k, slice(None), tile(t))
                value = (part["s"] - part["d"]) + moved - shift * here[(e, *where)]
                if previous is not None:
                    value = value - previous[(e, *where)]
                out[(target, *where)] = value


ORDER = (
    ("in", 0), (0, 0), ("in", 1), (1, 0), (0, 1), ("in", 2), (2, 0), (1, 1),
    (0, 2), ("in", 3), (2, 1), (0, 3), (1, 2), (1, 3), (2, 2), (2, 3),
)


def filter_kernel(
    devices, center, half_width, width, x, modulus, occupancy, home, turned, state_0, state_1, state_2, state_3, coeff, planes, ahead, forces, upward, coeff_mine,
    in_send, in_recv, halo_send, halo_recv, out_send, out_recv, coeff_send, coeff_recv, edge_send, edge_recv,
):
    me = lax.axis_index("dev")
    place, row = me % ROW, me // ROW
    base = me - place
    has_below, has_above = row > 0, row < devices // ROW - 1
    groups = turned.shape[0] // ROW
    state = [state_0, state_1, state_2, state_3]
    nodes = x.shape[1]
    mates = []
    for side in (0, 1):
        for step in (1, 3, 2) if side == 0 else (1, 3, 2, 0):
            chip, core = (place // 2 + step) % (ROW // 2), (place % 2 + side) % 2
            mates.append(2 * chip + core)
    barrier = pltpu.get_barrier_semaphore()
    for mate in mates:
        pl.semaphore_signal(barrier, inc=1, device_id=(base + mate,), device_id_type=MESH)
    for present, peer in ((has_below, me - ROW), (has_above, me + ROW)):

        @pl.when(present)
        def _():
            pl.semaphore_signal(barrier, inc=1, device_id=(peer,), device_id_type=MESH)

    @pl.loop(0, 3 * (nodes // TILE))
    def _(i):
        k, t = i // (nodes // TILE), i % (nodes // TILE)
        lanes = pl.ds(pl.multiple_of(t * TILE, TILE), TILE)
        for c in range(x.shape[2] // TILE):
            block = x[k, lanes, pl.ds(c * TILE, TILE)].T
            for g in range(TILE // GROUP):
                turned[c * (TILE // GROUP) + g, k, :, lanes] = block[g * GROUP : (g + 1) * GROUP]

    beside = coeff_mine.shape[1] // width
    pieces = []
    for i in range(beside):
        rows = pl.ds(i, coeff_mine.shape[0], stride=beside)
        pieces.append(modulus[rows, :] * occupancy[rows, :].astype(jnp.float32))
    coeff_mine[...] = jnp.concatenate(pieces, axis=1)
    coeff[1 + place] = coeff_mine[...]

    def remote(src, dst, send_sem, recv_sem, peer):
        return pltpu.make_async_remote_copy(
            src_ref=src, dst_ref=dst, send_sem=send_sem, recv_sem=recv_sem, device_id=(peer,), device_id_type=MESH
        )

    def coeff_copy(mate):
        return remote(coeff_mine, coeff.at[1 + place], coeff_send.at[mate], coeff_recv.at[place], base + mate)

    def in_copy(q, mate):
        return remote(
            turned.at[groups * mate + q], state[0].at[q, 1 + place], in_send.at[q, mate], in_recv.at[q, place], base + mate
        )

    def out_copy(q, mate):
        return remote(state[3].at[q, 1 + mate], home.at[groups * place + q], out_send.at[q, mate], out_recv.at[q, place], base + mate)

    def halo_copy(s, q, way):
        source, target, peer = ((ROW, 0, me + ROW), (1, ROW + 1, me - ROW))[way]
        return remote(state[s].at[q, source], state[s].at[q, target], halo_send.at[s, q, way], halo_recv.at[s, q, way], peer)

    def edge_copy():
        return remote(coeff.at[ROW], coeff.at[0], edge_send, edge_recv, me + ROW)

    def arrived(dst, recv_sem):
        remote(dst, dst, edge_send, recv_sem, base + mates[0]).wait_recv()

    pl.semaphore_wait(barrier, len(mates) + has_below.astype(jnp.int32) + has_above.astype(jnp.int32))
    for mate in mates:
        coeff_copy(mate).start()

    @pl.loop(0, groups)
    def _(q):
        for mate in mates:
            in_copy(q, mate).start()

    @pl.loop(0, groups)
    def _(q):
        state[0][q, 1 + place] = turned[groups * place + q]

    upward[...] = jnp.zeros_like(upward)

    @pl.when(jnp.logical_not(has_below))
    def _():
        coeff[0] = jnp.zeros(coeff.shape[1:], jnp.float32)

    for present, layer in ((has_below, 0), (has_above, ROW + 1)):

        @pl.when(jnp.logical_not(present))
        def _():
            @pl.loop(0, groups)
            def _(q):
                for s in range(3):
                    state[s][q, layer] = jnp.zeros(state[s].shape[2:], jnp.float32)

    for mate in mates:
        arrived(coeff.at[1 + mate], coeff_recv.at[mate])

    @pl.when(has_above)
    def _():
        edge_copy().start()

    @pl.when(has_below)
    def _():
        arrived(coeff.at[0], edge_recv)

    def send_halo(s, q):
        for present, way in ((has_above, 0), (has_below, 1)):

            @pl.when(present)
            def _():
                halo_copy(s, q, way).start()

    for s, q in ORDER:
        if s == "in":
            for mate in mates:
                arrived(state[0].at[q, 1 + mate], in_recv.at[q, mate])
            send_halo(0, q)
            continue
        for present, way, layer in ((has_below, 0, 0), (has_above, 1, ROW + 1)):

            @pl.when(present)
            def _():
                arrived(state[s].at[q, layer], halo_recv.at[s, q, way])

        factor = (1.0 if s == 0 else 2.0) / half_width
        previous = state[s - 1].at[q] if s else None
        filter_round(factor, factor * center, width, state[s].at[q], previous, state[s + 1].at[q], coeff, planes, ahead, forces, upward)
        if s < 2:
            send_halo(s + 1, q)
        else:
            for mate in mates:
                out_copy(q, mate).start()
            home[groups * place + q] = state[3][q, 1 + place]

    @pl.loop(0, groups)
    def _(q):
        for mate in mates:
            arrived(home.at[groups * mate + q], out_recv.at[q, mate])
            in_copy(q, mate).wait_send()
            out_copy(q, mate).wait_send()
        for s in range(3):
            for present, way in ((has_above, 0), (has_below, 1)):

                @pl.when(present)
                def _():
                    halo_copy(s, q, way).wait_send()

    for mate in mates:
        coeff_copy(mate).wait_send()

    @pl.when(has_above)
    def _():
        edge_copy().wait_send()


def filtered(block, modulus, occupancy, center, half_width):
    _, nodes, modes = block.shape
    groups, tiles = modes // GROUP // ROW, nodes // TILE
    vmem = lambda *shape: pltpu.VMEM(shape, jnp.float32)
    dma = pltpu.SemaphoreType.DMA
    return pl.pallas_call(
        functools.partial(filter_kernel, lax.axis_size("dev"), center, half_width, modulus.shape[1]),
        out_shape=jax.ShapeDtypeStruct((modes // GROUP, 3, GROUP, nodes), jnp.float32),
        in_specs=[pl.BlockSpec(memory_space=pltpu.VMEM)] * 3,
        out_specs=pl.BlockSpec(memory_space=pltpu.VMEM),
        scratch_shapes=[
            vmem(modes // GROUP, 3, GROUP, nodes), *[vmem(groups, SPARE + 1, 3, GROUP, nodes)] * 4, vmem(ROW + 1, tiles, TILE),
            *[vmem(tiles, 12, GROUP, TILE)] * 4, vmem(tiles, TILE),
            dma((groups, ROW)), dma((groups, ROW)), dma((3, groups, 2)), dma((3, groups, 2)), dma((groups, ROW)), dma((groups, ROW)),
            dma((ROW,)), dma((ROW,)), dma, dma,
        ],
        compiler_params=pltpu.CompilerParams(collective_id=1, has_side_effects=True),
        name="filter",
    )(block, modulus, occupancy)


def split(x):
    high = x.astype(jnp.bfloat16)
    return high, (x - high.astype(jnp.float32)).astype(jnp.bfloat16)


def dot(a, b):
    return jnp.dot(a, b, precision=HIGHEST, preferred_element_type=jnp.float32)


def dot_ta(a, b):
    return lax.dot_general(a, b, (((0,), (0,)), ((), ())), precision=HIGHEST, preferred_element_type=jnp.float32)


SWEEPS = 10
TARGET = 1e-4


def factor_kernel(scale, gram, inverse, triangle, misfit):
    g = unpacked(gram[...])
    n = g.shape[0]
    row = lax.broadcasted_iota(jnp.int32, (n, n), 0)
    col = lax.broadcasted_iota(jnp.int32, (n, n), 1)
    diagonal = jnp.where(row == col, g, 0.0)
    d_col = lax.rsqrt(jnp.sum(diagonal, axis=1, keepdims=True))
    d_row = lax.rsqrt(jnp.sum(diagonal, axis=0, keepdims=True))
    unit = g * d_col * d_row
    one = jnp.where(row == col, 1.0, 0.0)
    weight = jnp.where(row < col, 1.0, jnp.where(row == col, 0.5, 0.0))

    def refined(state):
        s, _, count = state
        parts = split(s)
        excess = three(parts, split(three(unit_parts, parts, 0)), 0) - one
        s = s - three(parts, split(excess * weight), 1)
        return (s, jnp.sum(excess * excess), count + 1)

    unit_parts = split(unit)

    def three(p, q, dim):
        product = lambda a, b: lax.dot_general(a, b, (((dim,), (0,)), ((), ())), preferred_element_type=jnp.float32)
        return product(p[1], q[0]) + product(p[0], q[1]) + product(p[0], q[0])

    start = one - (unit - one) * weight
    s, size, _ = lax.while_loop(
        lambda state: jnp.logical_and(state[1] > TARGET, state[2] < SWEEPS), refined, (start, jnp.float32(1.0), 0)
    )
    inverse[...] = d_col * s
    r = three(split(s), unit_parts, 0)
    triangle[...] = jnp.where(row <= col, r * (scale / d_row), 0.0)
    norm = jnp.sum(s * s)
    misfit[0, 0] = jnp.where(norm <= n + 50.0, size, 1.0)


def factored(gram, scale):
    n = gram.shape[1] * 2
    return pl.pallas_call(
        functools.partial(factor_kernel, scale),
        out_shape=(
            jax.ShapeDtypeStruct((n, n), jnp.float32),
            jax.ShapeDtypeStruct((n, n), jnp.float32),
            jax.ShapeDtypeStruct((1, 1), jnp.float32),
        ),
        in_specs=[pl.BlockSpec(memory_space=pltpu.VMEM)],
        out_specs=(
            pl.BlockSpec(memory_space=pltpu.VMEM),
            pl.BlockSpec(memory_space=pltpu.VMEM),
            pl.BlockSpec(memory_space=pltpu.SMEM),
        ),
        name="factor",
    )(gram)


def elimination_kernel(gram, extra, inverse_t, triangle, a, w):
    n = gram.shape[0]
    row = lax.broadcasted_iota(jnp.int32, (n, n), 0)
    col = lax.broadcasted_iota(jnp.int32, (n, n), 1)
    g = gram[...]
    one = jnp.where(row == col, 1.0, 0.0)
    diagonal = jnp.where(row == col, g, 0.0)
    s_col = jnp.sum(diagonal, axis=1, keepdims=True)
    s_row = jnp.sum(diagonal, axis=0, keepdims=True)
    d_col = lax.rsqrt(jnp.where(s_col > 0, s_col, 1.0))
    d_row = lax.rsqrt(jnp.where(s_row > 0, s_row, 1.0))
    a[...] = g * d_col * d_row + extra[0, 0] * one
    w[...] = one

    @pl.loop(0, n)
    def _(k):
        pivot_row = a[pl.ds(k, 1), :]
        column = jnp.sum(jnp.where(col == k, a[...], 0.0), axis=1, keepdims=True)
        lane = lax.broadcasted_iota(jnp.int32, (1, n), 1)
        pivot = jnp.maximum(jnp.sum(jnp.where(lane == k, pivot_row, 0.0), axis=1, keepdims=True), 1e-12)
        below = lax.broadcasted_iota(jnp.int32, (n, 1), 0) > k
        ratio = jnp.where(below, column / pivot, 0.0)
        w_row = w[pl.ds(k, 1), :]
        a[...] = a[...] - ratio * pivot_row
        w[...] = w[...] - ratio * w_row

    u = a[...]
    pivots = jnp.maximum(jnp.sum(jnp.where(row == col, u, 0.0), axis=1, keepdims=True), 1e-12)
    root = lax.rsqrt(pivots)
    triangle[...] = jnp.where(row < col, u * root, jnp.where(row == col, pivots * root, 0.0)) / d_row
    inverse_t[...] = w[...] * root * d_row


def eliminated(gram, extra):
    n = gram.shape[0]
    return pl.pallas_call(
        elimination_kernel,
        out_shape=(jax.ShapeDtypeStruct((n, n), jnp.float32),) * 2,
        in_specs=[pl.BlockSpec(memory_space=pltpu.VMEM), pl.BlockSpec(memory_space=pltpu.SMEM)],
        out_specs=(pl.BlockSpec(memory_space=pltpu.VMEM),) * 2,
        scratch_shapes=[pltpu.VMEM((n, n), jnp.float32)] * 2,
        name="eliminate",
    )(gram, extra.reshape(1, 1))


def all_reduce_kernel(prepare, sizes, x, out, half, part, summed, full, core_in, x_in, y_in, z_in, send, core_sem, x_sem, y_sem, z_sem, back_sem, pair_sem):
    nz, ny, nx = sizes
    me = lax.axis_index("dev")
    core, at_x = me % 2, me // 2 % nx
    at_y, at_z = me // (2 * nx) % ny, me // (2 * nx * ny)
    partner = me + 1 - 2 * core
    along = lambda at, j, size, stride: ((at + j) % size, me + ((at + j) % size - at) * stride)
    x_peers = [along(at_x, j, nx, 2) for j in range(1, nx)]
    y_peers = [along(at_y, j, ny, 2 * nx) for j in range(1, ny)]
    z_peers = [along(at_z, j, nz, 2 * nx * ny) for j in range(1, nz)]

    barrier = pltpu.get_barrier_semaphore()
    others = [partner] + [peer for _, peer in x_peers + y_peers + z_peers]
    for peer in others:
        pl.semaphore_signal(barrier, inc=1, device_id=(peer,), device_id_type=MESH)
    x = prepare(x)
    pl.semaphore_wait(barrier, len(others))

    started = []

    def copy(src, dst, recv_sem, peer):
        transfer = pltpu.make_async_remote_copy(
            src_ref=src, dst_ref=dst, send_sem=send.at[len(started)], recv_sem=recv_sem, device_id=(peer,), device_id_type=MESH
        )
        transfer.start()
        started.append(transfer)

    def arrived(dst, recv_sem):
        pltpu.make_async_remote_copy(
            src_ref=dst, dst_ref=dst, send_sem=send.at[0], recv_sem=recv_sem, device_id=(partner,), device_id_type=MESH
        ).wait_recv()

    rows = x.shape[0] // 2
    piece = rows // nx
    copy(x.at[pl.ds((1 - core) * rows, rows)], core_in, core_sem, partner)
    arrived(core_in, core_sem)
    half[...] = x[pl.ds(core * rows, rows)] + core_in[...]

    for other, peer in x_peers:
        copy(half.at[pl.ds(other * piece, piece)], x_in.at[at_x], x_sem.at[at_x], peer)
    x_in[at_x] = half[pl.ds(at_x * piece, piece)]
    for other, peer in x_peers:
        arrived(x_in.at[other], x_sem.at[other])
    total = x_in[0]
    for i in range(1, nx):
        total = total + x_in[i]

    for stage, (peers, at, size, slots, sem) in enumerate(((y_peers, at_y, ny, y_in, y_sem), (z_peers, at_z, nz, z_in, z_sem))):
        part[stage] = total
        for other, peer in peers:
            copy(part.at[stage], slots.at[at], sem.at[at], peer)
        slots[at] = total
        for other, peer in peers:
            arrived(slots.at[other], sem.at[other])
        total = slots[0]
        for i in range(1, size):
            total = total + slots[i]

    summed[...] = total
    mine = core * rows + at_x * piece
    for other, peer in x_peers:
        copy(summed, full.at[pl.ds(mine, piece)], back_sem.at[at_x], peer)
    copy(summed, full.at[pl.ds(mine, piece)], pair_sem.at[at_x], partner)
    full[pl.ds(mine, piece)] = total
    for other, peer in x_peers:
        there = full.at[pl.ds(core * rows + other * piece, piece)]
        arrived(there, back_sem.at[other])
        copy(there, there, pair_sem.at[other], partner)
    for i in range(nx):
        arrived(full.at[pl.ds((1 - core) * rows + i * piece, piece)], pair_sem.at[i])
    out[...] = full[...]
    for transfer in started:
        transfer.wait_send()


def all_reduce_call(kernel, x, shape, own, sizes, collective_id, name):
    nz, ny, nx = sizes
    n, m = shape
    rows = n // 2
    piece = rows // nx
    copies = 1 + (nx - 1) + (ny - 1) + (nz - 1) + nx + (nx - 1)
    block = lambda *lead: pltpu.VMEM((*lead, m), jnp.float32)
    return pl.pallas_call(
        kernel,
        out_shape=jax.ShapeDtypeStruct(shape, jnp.float32),
        in_specs=[pl.BlockSpec(memory_space=pltpu.VMEM)],
        out_specs=pl.BlockSpec(memory_space=pltpu.VMEM),
        scratch_shapes=[block(n)] * own + [
            block(rows), block(2, piece), block(piece), block(n), block(rows), block(nx, piece), block(ny, piece), block(nz, piece),
            pltpu.SemaphoreType.DMA((copies,)), pltpu.SemaphoreType.DMA, pltpu.SemaphoreType.DMA((nx,)), pltpu.SemaphoreType.DMA((ny,)),
            pltpu.SemaphoreType.DMA((nz,)), pltpu.SemaphoreType.DMA((nx,)), pltpu.SemaphoreType.DMA((nx,)),
        ],
        compiler_params=pltpu.CompilerParams(collective_id=collective_id, has_side_effects=True),
        name=name,
    )(x)


SIZES = (4, 4, 4)


def all_reduce(x, sizes=SIZES):
    kernel = functools.partial(all_reduce_kernel, lambda ref: ref, sizes)
    return all_reduce_call(kernel, x, x.shape, 0, sizes, 0, "all_reduce")


def summed_gram(x, sizes=SIZES):
    def kernel(x_ref, out, mine, *rest):
        def prepare(ref):
            gram_kernel(ref, mine)
            return mine

        all_reduce_kernel(prepare, sizes, x_ref, out, *rest)

    n = x.shape[0] * x.shape[2]
    return all_reduce_call(kernel, x, (n // 2 * 3, n // 2), 1, sizes, 2, "summed_gram")


def packed(gram):
    half = gram.shape[0] // 2
    return jnp.concatenate([gram[:half, :half], gram[:half, half:], gram[half:, half:]], axis=0)


def unpacked(blocks):
    half = blocks.shape[1]
    first, cross, last = (blocks[i * half : (i + 1) * half] for i in range(3))
    return jnp.concatenate([jnp.concatenate([first, cross], axis=1), jnp.concatenate([cross.T, last], axis=1)], axis=0)


def gram_kernel(x_ref, out):
    total, cross = 0.0, 0.0
    product = lambda p, q: lax.dot_general(p, q, (((1,), (1,)), ((), ())), preferred_element_type=jnp.float32)
    for k in range(x_ref.shape[1]):
        high, low = split(x_ref[:, k].reshape(-1, x_ref.shape[-1]))
        total = total + product(high, high)
        cross = cross + product(high, low)
    out[...] = packed(total + (cross + cross.T))


def component_spec(x):
    return pl.BlockSpec((x.shape[0], 1, *x.shape[2:]), lambda k: (0, k, 0, 0))


def product_kernel(row_scale, x_ref, inverse, out, high_s, low_s):
    @pl.when(pl.program_id(0) == 0)
    def _():
        high_s[...], low_s[...] = split(inverse[...] * row_scale)

    high, low = split(x_ref[...].reshape(-1, x_ref.shape[-1]))
    product = lambda p, q: lax.dot_general(p, q, (((0,), (0,)), ((), ())), preferred_element_type=jnp.float32)
    out[0] = product(low, high_s[...]) + product(high, low_s[...]) + product(high, high_s[...])


def product_of(x, inverse, row_scale):
    n, nodes = x.shape[0] * x.shape[2], x.shape[3]
    return pl.pallas_call(
        functools.partial(product_kernel, row_scale),
        out_shape=jax.ShapeDtypeStruct((3, nodes, n), jnp.float32),
        grid=(3,),
        in_specs=[component_spec(x), pl.BlockSpec((n, n), lambda k: (0, 0))],
        out_specs=pl.BlockSpec((1, nodes, n), lambda k: (k, 0, 0)),
        scratch_shapes=[pltpu.VMEM((n, n), jnp.bfloat16)] * 2,
        name="product",
    )(x, inverse)


def local(start_block, modulus, occupancy):
    center, half_width = filter_bounds(element_matrix())
    modes = start_block.shape[4]
    flat = start_block.reshape(3, -1, modes)
    row_scale = math.sqrt(math.prod(flat.shape[:2]) * lax.axis_size("dev"))
    current = filtered(flat, modulus[0], occupancy[0], center, half_width)
    gram = summed_gram(current)
    inverse, triangle, misfit = factored(gram, 1.0 / row_scale)

    def direct(x, inverse, triangle):
        return product_of(x, inverse, row_scale), triangle

    def general(x, inverse, triangle):
        def one_pass(i, state):
            x, total = state
            extra = jnp.where(i == 0, 3e-5, 0.0).astype(jnp.float32)
            inverse_t, r = eliminated(unpacked(all_reduce(packed(dot_ta(x, x)))), extra)
            return (dot(x, inverse_t.T), dot(r, total))

        x, total = lax.fori_loop(0, 4, one_pass, (x.transpose(1, 3, 0, 2).reshape(-1, modes), jnp.eye(modes, dtype=jnp.float32)))
        return (x * row_scale).reshape(flat.shape), total / row_scale

    basis, triangle = lax.cond(misfit[0, 0] <= TARGET, direct, general, current, inverse, triangle)
    return basis.reshape(start_block.shape), triangle


def solution(mesh):
    return jax.shard_map(
        local,
        mesh=mesh,
        in_specs=(P(None, "dev", None, None, None), P("dev", None, None), P("dev", None, None)),
        out_specs=(P(None, "dev", None, None, None), P()),
        check_vma=False,
    )
```
